32 devices in a mesh: rows: 4 (over y, x), mp: 8 (over z, core).
Axes of the slice: x: 2, y: 2, z: 4, core: 2. Of those that a mesh axis runs over, the one named last changes fastest.
Arguments:
- inputs: bfloat16 [8192, 2048], P(('rows', 'mp')), may hold values from -6 to 6
- cotangent: bfloat16 [8192, 2048], P(('rows', 'mp')), may hold values from -6 to 6
- corpus_ids: int32 [4], P('rows'), may hold values from 0 to 3
- corpus_weight: float32 [4], replicated, may hold values from 0.5 to 2
- attn_gain: bfloat16 [2048], P(('rows', 'mp')), may hold values from 0.099609375 to 1.8984375
- qkv_weight: bfloat16 [2048, 1920], P(('rows', 'mp')), may hold values from -0.125 to 0.125
- out_weight: bfloat16 [1280, 2048], P(('rows', 'mp')), may hold values from -2.5 to 2.5
- ffn_gain: bfloat16 [2048], P(('rows', 'mp')), may hold values from 0.099609375 to 1.8984375
- gate_weight: bfloat16 [2048, 6144], P(None, 'mp'), may hold values from -0.125 to 0.125
- up_weight: bfloat16 [2048, 6144], P(None, 'mp'), may hold values from -0.125 to 0.125
- down_weight: bfloat16 [6144, 2048], P('mp'), may hold values from -0.078125 to 0.078125
Outputs:
- outputs: bfloat16 [8192, 2048], P(('rows', 'mp'))
- input_grad: float32 [8192, 2048], P(('rows', 'mp'))
- qkv_grad: float32 [2048, 1920], P(('rows', 'mp'))
- proj_grad: float32 [1280, 2048], P(('rows', 'mp'))
- gate_grad: float32 [2048, 6144], P(None, 'mp')
- up_grad: float32 [2048, 6144], P(None, 'mp')
- down_grad: float32 [6144, 2048], P('mp')
- attn_gain_grad: float32 [2048], P(('rows', 'mp'))
- ffn_gain_grad: float32 [2048], P(('rows', 'mp'))
The draws below stay inside these ranges and needn't reach their ends.
All inputs are finite; a program needn't handle non-finite values.
Results may differ from the reference program's by a relative error of at most 0.015.
Values may be sent and summed in bfloat16 or wider, within the bound.
A program may use at most 256 MiB of HBM per device.

```python
import math
import jax
import jax.numpy as jnp
from jax import lax

D = 2048
HEADS = 20
KV_HEADS = 5
HEAD_DIM = 64
FF = 6144
LEN = 2048
CORPORA = 4
SEQUENCES = 4
TOKENS = 8192
QKV = 1920


def plant(values, rng, smallest, top_value):
    longest = values.shape.index(max(values.shape))
    spots = []
    for shift in (0, 1):
        where = [jax.random.randint(jax.random.fold_in(rng, axis), (), 0, length) for axis, length in enumerate(values.shape)]
        where[longest] = (where[longest] + shift) % values.shape[longest]
        spots.append(tuple(where))
    return values.at[spots[0]].set(smallest).at[spots[1]].set(top_value)


def levels(stream_key, extent, shards, low, largest):
    loudness = 1.0
    for position, blocks in shards:
        draws = jax.random.uniform(jax.random.fold_in(jax.random.fold_in(stream_key, 6), position), (blocks,), jnp.float32, low / len(shards), largest / len(shards))
        loudness = loudness * jnp.repeat(jnp.exp(draws), extent[position] // blocks).reshape((-1,) + (1,) * (len(extent) - 1 - position))
    return loudness


def centred(own_key, shape, scale, most, cuts=(), kind=jnp.bfloat16):
    entries = scale * jax.random.normal(own_key, shape, jnp.float32)
    if cuts:
        entries = entries * levels(own_key, shape, cuts, -0.22, 0.18)
    return jnp.clip(entries, -most, most).astype(kind)


def setup_inputs(seed: int = 0) -> dict:
    keys = jax.random.split(jax.random.key(seed), 12)
    inputs = centred(keys[0], (TOKENS, D), 1.0, 6.0, ((0, 32),))
    cotangent = centred(keys[1], (TOKENS, D), 1.0, 6.0, ((0, 32),))
    corpus_ids = plant(jax.random.randint(keys[2], (SEQUENCES,), 0, CORPORA), jax.random.fold_in(keys[2], 1), 0, CORPORA - 1).astype(jnp.int32)
    corpus_weight = jnp.clip(jnp.exp(jax.random.uniform(keys[3], (CORPORA,), jnp.float32, math.log(0.5), math.log(2.0))), 0.5, 2.0)
    attn_gain = jnp.clip(1.0 + 0.18 * jax.random.normal(keys[4], (D,), jnp.float32), 0.099609375, 1.8984375).astype(jnp.bfloat16)
    qkv_weight = centred(keys[5], (D, QKV), D ** -0.5, 0.125, ((0, 32),))
    out_weight = centred(keys[6], (HEADS * HEAD_DIM, D), (HEADS * HEAD_DIM // 256) ** -0.5, 2.5, ((0, 32),))
    ffn_gain = jnp.clip(1.0 + 0.18 * jax.random.normal(keys[7], (D,), jnp.float32), 0.099609375, 1.8984375).astype(jnp.bfloat16)
    gate_weight = centred(keys[8], (D, FF), D ** -0.5, 0.125, ((1, 8),))
    up_weight = centred(keys[9], (D, FF), D ** -0.5, 0.125, ((1, 8),))
    down_weight = centred(keys[10], (FF, D), FF ** -0.5, 0.078125, ((0, 8),))
    return dict(inputs=inputs, cotangent=cotangent, corpus_ids=corpus_ids, corpus_weight=corpus_weight, attn_gain=attn_gain, qkv_weight=qkv_weight, out_weight=out_weight, ffn_gain=ffn_gain, gate_weight=gate_weight, up_weight=up_weight, down_weight=down_weight)


EPS = 1e-05
THETA = 10000.0

@jax.custom_vjp
def low(v):
    return lax.optimization_barrier(v.astype(jnp.bfloat16)).astype(jnp.float32)

@jax.custom_vjp
def low_back(v):
    return v

def low_keep(v):
    return (low(v), None)

def low_pass(kept, grad):
    return (grad,)

def back_keep(v):
    return (v, None)

def back_low(kept, grad):
    return (low(grad),)
low.defvjp(low_keep, low_pass)
low_back.defvjp(back_keep, back_low)

def rotation(positions):
    half_dim = HEAD_DIM // 2
    freqs = jnp.exp(-jnp.log(THETA) * (2.0 * jnp.arange(half_dim, dtype=jnp.float32)) / HEAD_DIM)
    angles = positions.astype(jnp.float32)[:, None] * freqs[None, :]
    return (jnp.cos(angles), jnp.sin(angles))

def rotate(values_in, cosine, sine_part):
    half_dim = HEAD_DIM // 2
    first = values_in[..., :half_dim]
    second = values_in[..., half_dim:]
    return jnp.concatenate([first * cosine - second * sine_part, second * cosine + first * sine_part], axis=-1)

def head_attend(operands):
    queries, keys_part, values_part = operands
    scores = low_back(jnp.dot(queries, keys_part.T, precision=lax.Precision.HIGHEST) * HEAD_DIM ** (-0.5))
    allowed = jnp.arange(LEN)[None, :] <= jnp.arange(LEN)[:, None]
    scores = jnp.where(allowed, scores, -1e+30)
    probabilities = low(jax.nn.softmax(scores, axis=-1))
    return jnp.dot(probabilities, values_part, precision=lax.Precision.HIGHEST)

def layer(residual, gain_one, weight_qkv, weight_out, gain_two, weight_gate, weight_up, weight_down):
    highest = lax.Precision.HIGHEST
    q_width = HEADS * HEAD_DIM
    kv_width = KV_HEADS * HEAD_DIM
    inverse_one = lax.rsqrt(lax.optimization_barrier(jnp.mean(residual * residual, axis=-1, keepdims=True)) + EPS)
    normed_one = low(residual * inverse_one * gain_one)
    projected = jnp.dot(normed_one, weight_qkv, precision=highest)
    cosine, sine_part = rotation(jnp.arange(LEN))
    cos_heads = cosine[:, None, :]
    sin_heads = sine_part[:, None, :]
    queries = low(rotate(low_back(projected[:, :q_width]).reshape(LEN, HEADS, HEAD_DIM), cos_heads, sin_heads))
    keys_all = low(rotate(low_back(projected[:, q_width:q_width + kv_width]).reshape(LEN, KV_HEADS, HEAD_DIM), cos_heads, sin_heads))
    values_all = low(low_back(projected[:, q_width + kv_width:])).reshape(LEN, KV_HEADS, HEAD_DIM)
    repeat = HEADS // KV_HEADS
    head_queries = jnp.transpose(queries, (1, 0, 2))
    head_keys = jnp.repeat(jnp.transpose(keys_all, (1, 0, 2)), repeat, axis=0)
    head_values = jnp.repeat(jnp.transpose(values_all, (1, 0, 2)), repeat, axis=0)
    attended = lax.map(jax.checkpoint(head_attend), (head_queries, head_keys, head_values))
    attended = low(low_back(attended))
    joined = jnp.transpose(attended, (1, 0, 2)).reshape(LEN, q_width)
    middle = residual + low_back(jnp.dot(joined, weight_out, precision=highest))
    inverse_two = lax.rsqrt(lax.optimization_barrier(jnp.mean(middle * middle, axis=-1, keepdims=True)) + EPS)
    normed_two = low(middle * inverse_two * gain_two)
    gate_val = low_back(jnp.dot(normed_two, weight_gate, precision=highest))
    up_val = low_back(jnp.dot(normed_two, weight_up, precision=highest))
    hidden = low(jax.nn.silu(gate_val) * up_val)
    return middle + low_back(jnp.dot(hidden, weight_down, precision=highest))

def reference(inputs, cotangent, corpus_ids, corpus_weight, attn_gain, qkv_weight, out_weight, ffn_gain, gate_weight, up_weight, down_weight):
    params = tuple((w.astype(jnp.float32) for w in (attn_gain, qkv_weight, out_weight, ffn_gain, gate_weight, up_weight, down_weight)))
    chosen = (corpus_ids[:, None] == jnp.arange(CORPORA)[None, :]).astype(jnp.float32)
    counts = lax.optimization_barrier(jnp.sum(chosen, axis=0))
    count_seq = lax.optimization_barrier(jnp.sum(chosen * counts[None, :], axis=1))
    weight_seq = lax.optimization_barrier(jnp.sum(chosen * corpus_weight[None, :], axis=1))
    seq_scale = weight_seq * SEQUENCES / (CORPORA * count_seq)
    seq_inputs = inputs.astype(jnp.float32).reshape(SEQUENCES, LEN, D)
    seq_cots = cotangent.astype(jnp.float32).reshape(SEQUENCES, LEN, D) * seq_scale[:, None, None]

    def one_seq(totals, operands):
        seq_input, seq_cot = operands
        result, pullback = jax.vjp(layer, seq_input, *params)
        gradients = pullback(seq_cot)
        totals = tuple((a + b for a, b in zip(totals, gradients[1:])))
        return (totals, (result.astype(jnp.bfloat16), gradients[0]))
    zero_grads = tuple((jnp.zeros_like(p) for p in params))
    totals, (out_rows, in_grads) = lax.scan(one_seq, zero_grads, (seq_inputs, seq_cots))
    return (out_rows.reshape(TOKENS, D), in_grads.reshape(TOKENS, D), totals[1], totals[2], totals[4], totals[5], totals[6], totals[0], totals[3])
```

```python
import functools

import jax
import jax.numpy as jnp
from jax import lax
from jax.experimental import pallas as pl
from jax.experimental.pallas import tpu as pltpu
from jax.sharding import PartitionSpec as P

HEADS = 20
KV_HEADS = 5
HEAD_DIM = 64
GROUP = HEADS // KV_HEADS
Q_WIDTH = HEADS * HEAD_DIM
KV_WIDTH = KV_HEADS * HEAD_DIM
LEN = 2048
BLOCK = 128
KTILE = 256
EPS = 1e-05
THETA = 10000.0
LANES = GROUP * BLOCK
SLAB = 2 * HEAD_DIM

MESH = pl.DeviceIdType.MESH
F32 = jnp.float32
BF16 = jnp.bfloat16
VMEM_LIMIT = 62 * 1024 * 1024


def rope_tables(positions):
    half_dim = HEAD_DIM // 2
    freqs = jnp.exp(-jnp.log(THETA) * (2.0 * jnp.arange(half_dim, dtype=F32)) / HEAD_DIM)
    angles = positions.astype(F32)[:, None] * freqs[None, :]
    cosine, sine = jnp.cos(angles), jnp.sin(angles)
    ones, zeros = jnp.ones_like(cosine), jnp.zeros_like(cosine)
    head_cos = jnp.concatenate([cosine, cosine], axis=1)
    head_sin = jnp.concatenate([-sine, sine], axis=1)
    cos_q = jnp.concatenate([head_cos, head_cos], axis=1)
    sin_q = jnp.concatenate([head_sin, head_sin], axis=1)
    cos_kv = jnp.concatenate([head_cos, ones, ones], axis=1)
    sin_kv = jnp.concatenate([head_sin, zeros, zeros], axis=1)
    return (cos_q, sin_q, cos_kv, sin_kv)


def swap_halves(slab):
    lane = lax.broadcasted_iota(jnp.int32, slab.shape, 1)
    half_dim = HEAD_DIM // 2
    up = pltpu.roll(slab, SLAB - half_dim, 1)
    down = pltpu.roll(slab, half_dim, 1)
    return jnp.where(lane % HEAD_DIM < half_dim, up, down)


def qkv_kernel(x_ref, gain_ref, w_ref, cos_q, sin_q, cos_kv, sin_kv, normed_ref, inv_ref, q_ref, kv_ref):
    x = x_ref[...].astype(F32)
    inverse = lax.rsqrt(jnp.mean(x * x, axis=-1, keepdims=True) + EPS)
    normed = (x * inverse * gain_ref[...]).astype(BF16)
    normed_ref[...] = normed
    inv_ref[...] = inverse
    for s in range(Q_WIDTH // 256):
        part = jnp.dot(normed, w_ref[:, s * 256 : (s + 1) * 256], preferred_element_type=F32)
        for t in range(2):
            slab = part[:, t * SLAB : (t + 1) * SLAB]
            col = s * 256 + t * SLAB
            turned = slab * cos_q[...] + swap_halves(slab) * sin_q[...]
            q_ref[:, col : col + SLAB] = (turned.astype(BF16).astype(F32) * HEAD_DIM ** (-0.5)).astype(BF16)
    part = jnp.dot(normed, w_ref[:, Q_WIDTH : Q_WIDTH + 2 * KV_WIDTH], preferred_element_type=F32)
    for g in range(KV_HEADS):
        slab = part[:, g * SLAB : (g + 1) * SLAB]
        turned = slab * cos_kv[...] + swap_halves(slab) * sin_kv[...]
        kv_ref[:, g * SLAB : (g + 1) * SLAB] = turned.astype(BF16)


def qkv_project(x, gain, weight, tables):
    rows, width = x.shape
    return pl.pallas_call(
        qkv_kernel,
        out_shape=(
            jax.ShapeDtypeStruct((rows, width), BF16),
            jax.ShapeDtypeStruct((rows, 1), F32),
            jax.ShapeDtypeStruct((rows, Q_WIDTH), BF16),
            jax.ShapeDtypeStruct((rows, 2 * KV_WIDTH), BF16),
        ),
        compiler_params=pltpu.CompilerParams(vmem_limit_bytes=VMEM_LIMIT),
        name="qkv_project",
    )(x, gain, weight, *tables)


def heads_to_lanes(rows_part):
    turned = rows_part.T
    return jnp.concatenate(
        [turned[h * HEAD_DIM : (h + 1) * HEAD_DIM, :] for h in range(GROUP)], axis=1
    )


def lanes_to_heads(lanes_part):
    stacked = jnp.concatenate(
        [lanes_part[:, h * BLOCK : (h + 1) * BLOCK] for h in range(GROUP)], axis=0
    )
    return stacked.T


def causal(tile, block):
    key_pos = tile * KTILE + lax.broadcasted_iota(jnp.int32, (KTILE, LANES), 0)
    query_pos = block * BLOCK + lax.broadcasted_iota(jnp.int32, (KTILE, LANES), 1) % BLOCK
    return key_pos <= query_pos


def over_rows(left, right):
    return lax.dot_general(left, right, (((0,), (0,)), ((), ())), preferred_element_type=F32)


def attend_kernel(block_ref, q_ref, kv_ref, o_ref, total_ref):
    subs = q_ref.shape[0] // BLOCK
    for sub in range(subs):
        block = block_ref[sub]
        queries = heads_to_lanes(q_ref[sub * BLOCK : (sub + 1) * BLOCK, :].astype(F32))
        queries = jnp.concatenate([queries, jnp.zeros_like(queries)], axis=0).astype(BF16)

        def step(tile, carry, masked):
            top, total, acc = carry
            kv = kv_ref[pl.ds(pl.multiple_of(tile * KTILE, KTILE), KTILE), :]
            scores = jnp.dot(kv, queries, preferred_element_type=F32)
            if masked:
                scores = jnp.where(causal(tile, block), scores, -1e30)
            new_top = jnp.maximum(top, jnp.max(scores, axis=0, keepdims=True))
            decay = jnp.exp(top - new_top)
            probs = jnp.exp(scores - new_top)
            total = decay * total + jnp.sum(probs, axis=0, keepdims=True)
            acc = decay * acc + over_rows(kv, probs.astype(BF16))
            return (new_top, total, acc)

        start = (
            jnp.full((1, LANES), -1e30, F32),
            jnp.zeros((1, LANES), F32),
            jnp.zeros((SLAB, LANES), F32),
        )
        full = block * BLOCK // KTILE
        carry = lax.fori_loop(0, full, lambda t, c: step(t, c, False), start)
        top, total, acc = step(full, carry, True)
        out = acc[HEAD_DIM:, :] / total
        o_ref[sub * BLOCK : (sub + 1) * BLOCK, :] = lanes_to_heads(out).astype(BF16)
        total_ref[sub : sub + 1, :] = top + jnp.log(total)


def attend(blocks, q, kv_all):
    rows = q.shape[0]
    subs = rows // BLOCK
    return pl.pallas_call(
        attend_kernel,
        grid_spec=pltpu.PrefetchScalarGridSpec(
            num_scalar_prefetch=1,
            grid=(KV_HEADS,),
            in_specs=[
                pl.BlockSpec((rows, GROUP * HEAD_DIM), lambda g, b: (0, g)),
                pl.BlockSpec((LEN, SLAB), lambda g, b: (0, g)),
            ],
            out_specs=[
                pl.BlockSpec((rows, GROUP * HEAD_DIM), lambda g, b: (0, g)),
                pl.BlockSpec((None, subs, LANES), lambda g, b: (g, 0, 0)),
            ],
        ),
        out_shape=(
            jax.ShapeDtypeStruct((rows, Q_WIDTH), BF16),
            jax.ShapeDtypeStruct((KV_HEADS, subs, LANES), F32),
        ),
        compiler_params=pltpu.CompilerParams(vmem_limit_bytes=VMEM_LIMIT),
        cost_estimate=pl.CostEstimate(
            flops=60_000_000_000, bytes_accessed=8_000_000, transcendentals=6_000_000
        ),
        name="attend",
    )(blocks, q, kv_all)


def block_of(device, sub, subs):
    if subs == 2:
        return 2 * device if sub == 0 else 2 * lax.axis_size("mp") - 1 - 2 * device
    return subs * device + sub


def attend_back_kernel(
    q_ref,
    kv_ref,
    o_ref,
    do_ref,
    total_ref,
    cos_q,
    sin_q,
    cos_kv,
    sin_kv,
    grad_ref,
    dkv_acc,
    own_part,
    twin_out,
    twin_in,
    sum_out,
    sum_in,
    mine,
    twin_send,
    twin_recv,
    sum_send,
    sum_recv,
):
    subs = q_ref.shape[0] // BLOCK
    chips = lax.axis_size("mp") // 2
    me = lax.axis_index("mp")
    row = lax.axis_index("rows")
    chip = me // 2
    core = me % 2
    twin = (row, me + 1 - 2 * core)
    width = GROUP * HEAD_DIM

    barrier = pltpu.get_barrier_semaphore()
    pl.semaphore_signal(barrier, inc=1, device_id=twin, device_id_type=MESH)
    for step in range(1, chips):
        pl.semaphore_signal(
            barrier,
            inc=1,
            device_id=(row, 2 * ((chip + step) % chips) + core),
            device_id_type=MESH,
        )
    pl.semaphore_wait(barrier, chips)

    def twin_copy(g):
        return pltpu.make_async_remote_copy(
            src_ref=twin_out.at[g % 2],
            dst_ref=twin_in.at[g],
            send_sem=twin_send.at[g % 2],
            recv_sem=twin_recv.at[g],
            device_id=twin,
            device_id_type=MESH,
        )

    def sum_copy(g, step):
        return pltpu.make_async_remote_copy(
            src_ref=sum_out.at[g, step - 1],
            dst_ref=sum_in.at[g, step - 1],
            send_sem=sum_send.at[g, step - 1],
            recv_sem=sum_recv.at[g, step - 1],
            device_id=(row, 2 * ((chip + step) % chips) + core),
            device_id_type=MESH,
        )

    def combine(g):
        twin_copy(g).wait_recv()
        for step in range(1, chips):
            goal = (chip + step) % chips
            sum_out[g, step - 1] = (
                own_part[g % 2, goal] + twin_in[g, goal].astype(F32)
            ).astype(BF16)
            sum_copy(g, step).start()
        mine[g] = own_part[g % 2, chip] + twin_in[g, chip].astype(F32)

    def head_step(g, _):
        cols = pl.ds(pl.multiple_of(g * width, width), width)
        pair = pl.ds(pl.multiple_of(g * SLAB, SLAB), SLAB)
        dkv_acc[...] = jnp.zeros_like(dkv_acc)
        for sub in range(subs):
            rows = slice(sub * BLOCK, (sub + 1) * BLOCK)
            block = block_of(me, sub, subs)
            queries = heads_to_lanes(q_ref[rows, cols].astype(F32))
            grads = heads_to_lanes(do_ref[rows, cols].astype(F32))
            outs = heads_to_lanes(o_ref[rows, cols].astype(F32))
            delta = jnp.sum(grads * outs, axis=0, keepdims=True)
            empty = jnp.zeros_like(queries)
            queries = jnp.concatenate([queries, empty], axis=0)
            grads = jnp.concatenate([empty, grads], axis=0)
            query_rows = queries.T.astype(BF16)
            grad_rows = grads.T.astype(BF16)
            queries = queries.astype(BF16)
            grads = grads.astype(BF16)
            log_total = total_ref[g, sub : sub + 1, :]

            def step(tile, dq, masked):
                keys = pl.ds(pl.multiple_of(tile * KTILE, KTILE), KTILE)
                kv = kv_ref[keys, pair]
                scores = jnp.dot(kv, queries, preferred_element_type=F32)
                probs = jnp.exp(scores - log_total)
                if masked:
                    probs = jnp.where(causal(tile, block), probs, 0.0)
                grad_probs = jnp.dot(kv, grads, preferred_element_type=F32)
                grad_scores = (probs * (grad_probs - delta)).astype(BF16)
                dkv_acc[keys, :] += jnp.dot(
                    grad_scores, query_rows, preferred_element_type=F32
                ) + jnp.dot(probs.astype(BF16), grad_rows, preferred_element_type=F32)
                return dq + over_rows(kv, grad_scores)

            full = block * BLOCK // KTILE
            dq = lax.fori_loop(
                0, full, lambda t, c: step(t, c, False), jnp.zeros((SLAB, LANES), F32)
            )
            dq = step(full, dq, True)
            dq = lanes_to_heads(dq[:HEAD_DIM, :]) * HEAD_DIM ** (-0.5)
            for t in range(width // SLAB):
                slab = dq[:, t * SLAB : (t + 1) * SLAB]
                turned = slab * cos_q[rows, :] - swap_halves(slab) * sin_q[rows, :]
                first = pl.multiple_of(g * width + t * SLAB, SLAB)
                grad_ref[rows, pl.ds(first, SLAB)] = turned.astype(BF16)

        @pl.when(g >= 2)
        def _():
            twin_copy(g - 2).wait_send()

        for goal in range(chips):
            for sub in range(subs):
                first = block_of(2 * goal + core, sub, subs) * BLOCK
                own_part[g % 2, goal, sub] = dkv_acc[pl.ds(pl.multiple_of(first, BLOCK), BLOCK), :]
                first = block_of(2 * goal + 1 - core, sub, subs) * BLOCK
                twin_out[g % 2, goal, sub] = dkv_acc[
                    pl.ds(pl.multiple_of(first, BLOCK), BLOCK), :
                ].astype(BF16)
        twin_copy(g).start()

        @pl.when(g >= 1)
        def _():
            combine(g - 1)

        return 0

    lax.fori_loop(0, KV_HEADS, head_step, 0)
    combine(KV_HEADS - 1)

    for g in range(KV_HEADS):
        total = mine[g]
        for step in range(1, chips):
            sum_copy(g, step).wait_recv()
            total = total + sum_in[g, step - 1].astype(F32)
        slab = total.reshape(subs * BLOCK, SLAB)
        turned = slab * cos_kv[...] - swap_halves(slab) * sin_kv[...]
        first = Q_WIDTH + g * SLAB
        grad_ref[:, first : first + SLAB] = turned.astype(BF16)
    for g in range(KV_HEADS):
        for step in range(1, chips):
            sum_copy(g, step).wait_send()
    for g in range(KV_HEADS - 2, KV_HEADS):
        twin_copy(g).wait_send()


def attend_back(q, kv_all, o, grad_o, totals, tables):
    rows = q.shape[0]
    subs = rows // BLOCK
    chips = lax.axis_size("mp") // 2
    vmem = pl.BlockSpec(memory_space=pltpu.VMEM)
    dma = pltpu.SemaphoreType.DMA
    part = (chips, subs, BLOCK, SLAB)
    return pl.pallas_call(
        attend_back_kernel,
        in_specs=[vmem] * 9,
        out_specs=vmem,
        out_shape=jax.ShapeDtypeStruct((rows, Q_WIDTH + 2 * KV_WIDTH), BF16),
        scratch_shapes=[
            pltpu.VMEM((LEN, SLAB), F32),
            pltpu.VMEM((2,) + part, F32),
            pltpu.VMEM((2,) + part, BF16),
            pltpu.VMEM((KV_HEADS,) + part, BF16),
            pltpu.VMEM((KV_HEADS, chips - 1) + part[1:], BF16),
            pltpu.VMEM((KV_HEADS, chips - 1) + part[1:], BF16),
            pltpu.VMEM((KV_HEADS,) + part[1:], F32),
            dma((2,)),
            dma((KV_HEADS,)),
            dma((KV_HEADS, chips - 1)),
            dma((KV_HEADS, chips - 1)),
        ],
        compiler_params=pltpu.CompilerParams(
            collective_id=3, has_side_effects=True, vmem_limit_bytes=VMEM_LIMIT
        ),
        cost_estimate=pl.CostEstimate(
            flops=120_000_000_000, bytes_accessed=12_000_000, transcendentals=6_000_000
        ),
        name="attend_back",
    )(q, kv_all, o, grad_o, totals, *tables)


def pack_kv(columns):
    lead = columns.shape[:-1]
    kv = columns[..., Q_WIDTH:].reshape(*lead, 2, KV_HEADS, HEAD_DIM)
    kv = jnp.swapaxes(kv, -3, -2).reshape(*lead, 2 * KV_WIDTH)
    return jnp.concatenate([columns[..., :Q_WIDTH], kv], axis=-1)


def unpack_kv(columns):
    lead = columns.shape[:-1]
    kv = columns[..., Q_WIDTH:].reshape(*lead, KV_HEADS, 2, HEAD_DIM)
    kv = jnp.swapaxes(kv, -3, -2).reshape(*lead, 2 * KV_WIDTH)
    return jnp.concatenate([columns[..., :Q_WIDTH], kv], axis=-1)


def dot(left, right):
    return jnp.dot(left, right, preferred_element_type=F32)


def dot_nt(left, right):
    return lax.dot_general(left, right, (((1,), (1,)), ((), ())), preferred_element_type=F32)


def dot_tn(left, right):
    return lax.dot_general(left, right, (((0,), (0,)), ((), ())), preferred_element_type=F32)


def half_of(ref, chip, core, sub, rows):
    tokens = ref.shape[0] // (lax.axis_size("mp") // 2)
    start = chip * tokens + core * (tokens // 2) + sub * rows
    return ref.at[pl.ds(pl.multiple_of(start, rows), rows)]


def ffn_kernel(
    subs,
    scale_ref,
    x_ref,
    cot_ref,
    gate_ref,
    up_ref,
    down_ref,
    part_ref,
    sum_ref,
    gate_out,
    up_out,
    down_out,
    x_all,
    hid,
    dgate,
    dup,
    cot_buf,
    part_buf,
    own_buf,
    twin_buf,
    twin_in,
    send_buf,
    sums_in,
    cot_cols,
    wide_buf,
    tall_buf,
    x_send,
    x_recv,
    twin_x_send,
    twin_x_recv,
    twin_send,
    twin_recv,
    sum_send,
    sum_recv,
    cot_sem,
    part_sem,
    cols_sem,
    out_sem,
):
    chips = lax.axis_size("mp") // 2
    me = lax.axis_index("mp")
    row = lax.axis_index("rows")
    chip = me // 2
    core = me % 2
    rows = x_ref.shape[0] // subs
    units = chips * subs
    twin = (row, me + 1 - 2 * core)

    def on_chip(other):
        return (row, 2 * other + core)

    barrier = pltpu.get_barrier_semaphore()
    pl.semaphore_signal(barrier, inc=1, device_id=twin, device_id_type=MESH)
    for step in range(1, chips):
        pl.semaphore_signal(
            barrier, inc=1, device_id=on_chip((chip + step) % chips), device_id_type=MESH
        )
    pl.semaphore_wait(barrier, chips)

    def order(i):
        near = jnp.minimum(chip, chips - 1 - chip)
        long_side = jnp.where(chip < chips - 1 - chip, 1, -1)
        j = i - subs
        paired = j < 2 * subs * near
        rest = j - 2 * subs * near
        dist = jnp.where(paired, j // (2 * subs) + 1, near + 1 + rest // subs)
        sub = jnp.where(paired, (j % (2 * subs)) // 2, rest % subs)
        side = jnp.where(paired, 1 - 2 * (j % 2), long_side)
        own = i < subs
        return (jnp.where(own, chip, chip + side * dist), jnp.where(own, i, sub))

    def x_copy(other, sub, side, source=None):
        spot = half_of(x_all, other, core, sub, rows)
        return pltpu.make_async_remote_copy(
            src_ref=spot if source is None else source,
            dst_ref=spot,
            send_sem=x_send.at[(side + 1) // 2, other * subs + sub],
            recv_sem=x_recv.at[other * subs + sub],
            device_id=on_chip(chip + side),
            device_id_type=MESH,
        )

    def twin_x_copy(other, sub, source=None):
        spot = half_of(x_all, other, core, sub, rows)
        return pltpu.make_async_remote_copy(
            src_ref=spot if source is None else source,
            dst_ref=spot,
            send_sem=twin_x_send.at[other * subs + sub],
            recv_sem=twin_x_recv.at[other * subs + sub],
            device_id=twin,
            device_id_type=MESH,
        )

    def twin_sum_copy(other, sub, slot):
        return pltpu.make_async_remote_copy(
            src_ref=twin_buf.at[slot],
            dst_ref=twin_in.at[other * subs + sub],
            send_sem=twin_send.at[slot],
            recv_sem=twin_recv.at[other * subs + sub],
            device_id=twin,
            device_id_type=MESH,
        )

    def sum_copy(other, sub):
        return pltpu.make_async_remote_copy(
            src_ref=send_buf.at[other * subs + sub],
            dst_ref=sums_in.at[(chip - other + chips) % chips - 1, sub],
            send_sem=sum_send.at[other * subs + sub],
            recv_sem=sum_recv.at[(chip - other + chips) % chips - 1, sub],
            device_id=on_chip(other),
            device_id_type=MESH,
        )

    def cot_copies(other, sub, slot):
        return [
            pltpu.make_async_copy(
                half_of(cot_ref, other, c, sub, rows),
                cot_buf.at[slot, pl.ds(c * rows, rows)],
                cot_sem.at[slot, c],
            )
            for c in range(2)
        ]

    def part_copies(other, sub, slot):
        return [
            pltpu.make_async_copy(
                part_buf.at[slot, pl.ds(c * rows, rows)],
                half_of(part_ref, other, c, sub, rows),
                part_sem.at[slot, c],
            )
            for c in range(2)
        ]

    for sub in range(subs):
        source = x_ref.at[pl.ds(sub * rows, rows)]

        @pl.when(chip < chips - 1)
        def _():
            x_copy(chip, sub, 1, source).start()

        @pl.when(chip > 0)
        def _():
            x_copy(chip, sub, -1, source).start()

        twin_x_copy(chip, sub, source).start()
    for copy in cot_copies(chip, 0, 0):
        copy.start()
    for sub in range(subs):
        half_of(x_all, chip, core, sub, rows)[...] = x_ref[sub * rows : (sub + 1) * rows, :]

    def reduce_unit(i):
        other, sub = order(i)
        unit = other * subs + sub
        twin_sum_copy(other, sub, i % 2).wait_recv()
        total = own_buf[i % 2] + twin_in[unit].astype(F32)

        @pl.when(other == chip)
        def _():
            sum_ref[pl.ds(pl.multiple_of(sub * rows, rows), rows), :] = total

        @pl.when(other != chip)
        def _():
            send_buf[unit] = total.astype(BF16)
            sum_copy(other, sub).start()

    def unit_step(i, _):
        other, sub = order(i)
        slot = i % 2

        @pl.when(i + 1 < units)
        def _():
            for copy in cot_copies(*order(i + 1), 1 - slot):
                copy.start()

        @pl.when(other != chip)
        def _():
            x_copy(other, sub, 1).wait_recv()
            twin_x_copy(other, sub).start()

            @pl.when((other > chip) & (chip > 0))
            def _():
                x_copy(other, sub, -1).start()

            @pl.when((other < chip) & (chip < chips - 1))
            def _():
                x_copy(other, sub, 1).start()

        twin_x_copy(other, sub).wait_recv()
        for copy in cot_copies(other, sub, slot):
            copy.wait()
        halves = [half_of(x_all, other, c, sub, rows)[...] for c in range(2)]
        x = jnp.concatenate(halves, axis=0)
        gate = dot(x, gate_ref[...])
        up = dot(x, up_ref[...])
        grad = dot_nt(cot_buf[slot], down_ref[...]) * scale_ref[0]
        sig = 1.0 / (1.0 + jnp.exp(-gate))
        act = gate * sig
        h = (act * up).astype(BF16)
        dg = (grad * up * (sig * (1.0 + gate * (1.0 - sig)))).astype(BF16)
        du = (grad * act).astype(BF16)
        for c in range(2):
            piece = slice(c * rows, (c + 1) * rows)
            half_of(hid, other, c, sub, rows)[...] = h[piece]
            half_of(dgate, other, c, sub, rows)[...] = dg[piece]
            half_of(dup, other, c, sub, rows)[...] = du[piece]

        @pl.when(i >= 2)
        def _():
            for copy in part_copies(*order(i - 2), slot):
                copy.wait()

        part_buf[slot] = dot(h, down_ref[...]).astype(BF16)
        for copy in part_copies(other, sub, slot):
            copy.start()

        @pl.when(i >= 2)
        def _():
            twin_sum_copy(*order(i - 2), slot).wait_send()

        dx = dot_nt(dg, gate_ref[...]) + dot_nt(du, up_ref[...])

        @pl.when(core == 0)
        def _():
            own_buf[slot] = dx[:rows]
            twin_buf[slot] = dx[rows:].astype(BF16)

        @pl.when(core == 1)
        def _():
            own_buf[slot] = dx[rows:]
            twin_buf[slot] = dx[:rows].astype(BF16)

        twin_sum_copy(other, sub, slot).start()

        @pl.when(i >= 1)
        def _():
            reduce_unit(i - 1)

        return 0

    lax.fori_loop(0, units, unit_step, 0)
    reduce_unit(units - 1)

    width = x_ref.shape[1]
    ff = gate_ref.shape[1]
    tall = tall_buf.shape[1]
    narrow = tall_buf.shape[2]
    down_cols = cot_cols.shape[2]
    col_steps = width // down_cols

    def cols_copy(j):
        return pltpu.make_async_copy(
            cot_ref.at[:, pl.ds(pl.multiple_of(j * down_cols, down_cols), down_cols)],
            cot_cols.at[j % 2],
            cols_sem.at[j % 2],
        )

    def wide_out(j):
        return pltpu.make_async_copy(
            wide_buf.at[j % 2],
            down_out.at[:, pl.ds(pl.multiple_of(j * down_cols, down_cols), down_cols)],
            out_sem.at[j % 2],
        )

    cols_copy(0).start()

    def down_step(j, _):
        @pl.when(j + 1 < col_steps)
        def _():
            cols_copy(j + 1).start()

        cols_copy(j).wait()

        @pl.when(j >= 2)
        def _():
            wide_out(j - 2).wait()

        wide_buf[j % 2] = (dot_tn(hid[...], cot_cols[j % 2]) * scale_ref[0]).astype(BF16)
        wide_out(j).start()
        return 0

    lax.fori_loop(0, col_steps, down_step, 0)
    for j in range(max(0, col_steps - 2), col_steps):
        wide_out(j).wait()

    pieces = width // tall
    steps = pieces * (ff // narrow)

    for source, target in ((dgate, gate_out), (dup, up_out)):

        def tall_out(j):
            first = pl.multiple_of(j % pieces * tall, tall)
            col = pl.multiple_of(j // pieces * narrow, narrow)
            return pltpu.make_async_copy(
                tall_buf.at[j % 2],
                target.at[pl.ds(first, tall), pl.ds(col, narrow)],
                out_sem.at[j % 2],
            )

        def tall_step(j, _):
            @pl.when(j >= 2)
            def _():
                tall_out(j - 2).wait()

            first = pl.multiple_of(j % pieces * tall, tall)
            col = pl.multiple_of(j // pieces * narrow, narrow)
            tall_buf[j % 2] = dot_tn(
                x_all[:, pl.ds(first, tall)], source[:, pl.ds(col, narrow)]
            ).astype(BF16)
            tall_out(j).start()
            return 0

        lax.fori_loop(0, steps, tall_step, 0)
        for j in range(steps - 2, steps):
            tall_out(j).wait()

    for sub in range(subs):
        total = sum_ref[sub * rows : (sub + 1) * rows, :]
        for step in range(1, chips):
            pltpu.make_async_remote_copy(
                src_ref=send_buf.at[0],
                dst_ref=sums_in.at[step - 1, sub],
                send_sem=sum_send.at[0],
                recv_sem=sum_recv.at[step - 1, sub],
                device_id=twin,
                device_id_type=MESH,
            ).wait_recv()
            total = total + sums_in[step - 1, sub].astype(F32)
        sum_ref[sub * rows : (sub + 1) * rows, :] = total

    def finish(i, _):
        other, sub = order(i)
        twin_x_copy(other, sub).wait_send()

        @pl.when(((other >= chip) & (chip > 0)))
        def _():
            x_copy(other, sub, -1).wait_send()

        @pl.when(((other <= chip) & (chip < chips - 1)))
        def _():
            x_copy(other, sub, 1).wait_send()

        @pl.when(other != chip)
        def _():
            sum_copy(other, sub).wait_send()

        @pl.when(i >= units - 2)
        def _():
            twin_sum_copy(other, sub, i % 2).wait_send()
            for copy in part_copies(other, sub, i % 2):
                copy.wait()

        return 0

    lax.fori_loop(0, units, finish, 0)


def ffn(scale, x, cot_all, gate_weight, up_weight, down_weight):
    tokens, width = cot_all.shape
    rows_dev = x.shape[0]
    chips = lax.axis_size("mp") // 2
    ff = gate_weight.shape[1]
    subs = max(1, rows_dev // BLOCK)
    rows = rows_dev // subs
    units = chips * subs
    narrow = ff // 3
    tall = 512
    down_cols = 512
    vmem = pl.BlockSpec(memory_space=pltpu.VMEM)
    hbm = pl.BlockSpec(memory_space=pl.ANY)
    dma = pltpu.SemaphoreType.DMA
    return pl.pallas_call(
        functools.partial(ffn_kernel, subs),
        out_shape=(
            jax.ShapeDtypeStruct((tokens, width), BF16),
            jax.ShapeDtypeStruct((rows_dev, width), F32),
            jax.ShapeDtypeStruct((width, ff), BF16),
            jax.ShapeDtypeStruct((width, ff), BF16),
            jax.ShapeDtypeStruct((ff, width), BF16),
        ),
        in_specs=[pl.BlockSpec(memory_space=pltpu.SMEM), vmem, hbm, vmem, vmem, vmem],
        out_specs=(hbm, vmem, hbm, hbm, hbm),
        scratch_shapes=[
            pltpu.VMEM((tokens, width), BF16),
            pltpu.VMEM((tokens, ff), BF16),
            pltpu.VMEM((tokens, ff), BF16),
            pltpu.VMEM((tokens, ff), BF16),
            pltpu.VMEM((2, 2 * rows, width), BF16),
            pltpu.VMEM((2, 2 * rows, width), BF16),
            pltpu.VMEM((2, rows, width), F32),
            pltpu.VMEM((2, rows, width), BF16),
            pltpu.VMEM((units, rows, width), BF16),
            pltpu.VMEM((units, rows, width), BF16),
            pltpu.VMEM((chips - 1, subs, rows, width), BF16),
            pltpu.VMEM((2, tokens, down_cols), BF16),
            pltpu.VMEM((2, ff, down_cols), BF16),
            pltpu.VMEM((2, tall, narrow), BF16),
            dma((2, units)),
            dma((units,)),
            dma((units,)),
            dma((units,)),
            dma((2,)),
            dma((units,)),
            dma((units,)),
            dma((chips - 1, subs)),
            dma((2, 2)),
            dma((2, 2)),
            dma((2,)),
            dma((2,)),
        ],
        compiler_params=pltpu.CompilerParams(
            collective_id=1, has_side_effects=True, vmem_limit_bytes=VMEM_LIMIT
        ),
        cost_estimate=pl.CostEstimate(
            flops=60_000_000_000, bytes_accessed=60_000_000, transcendentals=2_000_000
        ),
        name="ffn",
    )(scale.reshape(1), x, cot_all, gate_weight, up_weight, down_weight)


def reduce_kernel(heights, *refs):
    count = len(heights)
    lefts = refs[:count]
    rights = refs[count : 2 * count]
    gains = refs[2 * count]
    outs = refs[2 * count + 1 : 3 * count + 1]
    scratch = refs[3 * count + 1 :]
    per = 17
    chips = lax.axis_size("mp") // 2
    me = lax.axis_index("mp")
    row = lax.axis_index("rows")
    chip = me // 2
    core = me % 2
    down, across = row // 2, row % 2
    twin = (row, me + 1 - 2 * core)
    beside = (row + 1 - 2 * across, me)
    above = ((1 - down) * 2 + across, me)

    barrier = pltpu.get_barrier_semaphore()
    for device in (twin, beside, above):
        pl.semaphore_signal(barrier, inc=1, device_id=device, device_id_type=MESH)
    for step in range(1, chips):
        pl.semaphore_signal(
            barrier,
            inc=1,
            device_id=(row, 2 * ((chip + step) % chips) + core),
            device_id_type=MESH,
        )
    pl.semaphore_wait(barrier, chips + 2)

    streams = []
    for s in range(count):
        streams.append((heights[s], rights[s].shape[1], scratch[s * per : (s + 1) * per]))
    for s in range(count):
        turned = streams[s][2][0]
        turned[...] = lefts[s][...].T

    def target(i):
        return (chip + 1 + i) % chips

    def remote(source, dest, send, recv, device):
        return pltpu.make_async_remote_copy(
            src_ref=source,
            dst_ref=dest,
            send_sem=send,
            recv_sem=recv,
            device_id=device,
            device_id_type=MESH,
        )

    def copies(s, i):
        height, cols, bufs = streams[s]
        (_, own, twin_out, twin_in, out1, in1, out2, in2, out3, in3, s0, r0, s1, r1, s2, r2, s3) = bufs
        goal = target(i)
        return dict(
            twin=lambda: remote(twin_out.at[i], twin_in.at[i], s0.at[i], r0.at[i], twin),
            first=lambda d: remote(
                out1.at[i, d], in1.at[i, d], s1.at[i, d], r1.at[i, d], (beside, above)[d]
            ),
            second=lambda d: remote(
                out2.at[i, d], in2.at[i, d], s2.at[i, d], r2.at[i, d], (above, beside)[d]
            ),
            last=lambda: remote(
                out3.at[i], in3.at[i], s3.at[0, i], s3.at[1, i], (row, 2 * goal + core)
            ),
        )

    def make(s, i):
        height, cols, bufs = streams[s]
        turned, own, twin_out = bufs[:3]
        goal = target(i)
        for r in range(4):
            first = (r * chips + goal) * 2 * height
            lines = pl.ds(pl.multiple_of(first, 16), 2 * height)
            block = dot(turned[lines, :], rights[s][...])
            spare = cols_of(s) - block.shape[1]
            if spare:
                piece = gains[:, pl.ds(pl.multiple_of(first, 128), 2 * height)]
                piece = jnp.concatenate(
                    [piece, jnp.zeros((spare - piece.shape[0], 2 * height), F32)], axis=0
                ).T
                block = jnp.concatenate([block, piece], axis=1)

            @pl.when(core == 0)
            def _():
                own[i, r] = block[:height]
                twin_out[i, r] = block[height:].astype(BF16)

            @pl.when(core == 1)
            def _():
                own[i, r] = block[height:]
                twin_out[i, r] = block[:height].astype(BF16)

        copies(s, i)["twin"]().start()

    def cols_of(s):
        return streams[s][2][1].shape[-1]

    def first_stage(s, i):
        height, cols, bufs = streams[s]
        (_, own, twin_out, twin_in, out1, in1, out2, in2, out3, in3, s0, r0, s1, r1, s2, r2, s3) = bufs
        half = cols_of(s) // 2
        c = copies(s, i)
        c["twin"]().wait_recv()
        for r in range(4):
            own[i, r] = own[i, r] + twin_in[i, r].astype(F32)
        for k in range(2):
            out1[i, 0, k] = own[i, k * 2 + 1 - across, :, :half].astype(BF16)
            out1[i, 1, k] = own[i, (1 - down) * 2 + k, :, half:].astype(BF16)
        for d in range(2):
            c["first"](d).start()

    def second_stage(s, i):
        height, cols, bufs = streams[s]
        (_, own, twin_out, twin_in, out1, in1, out2, in2, out3, in3, s0, r0, s1, r1, s2, r2, s3) = bufs
        half = cols_of(s) // 2
        c = copies(s, i)
        for d in range(2):
            c["first"](d).wait_recv()
        other_down = (1 - down) * 2 + across
        other_across = down * 2 + 1 - across
        out2[i, 0] = (own[i, other_down, :, :half] + in1[i, 0, 1 - down].astype(F32)).astype(BF16)
        out2[i, 1] = (own[i, other_across, :, half:] + in1[i, 1, 1 - across].astype(F32)).astype(BF16)
        for d in range(2):
            c["second"](d).start()

    def third_stage(s, i):
        height, cols, bufs = streams[s]
        (_, own, twin_out, twin_in, out1, in1, out2, in2, out3, in3, s0, r0, s1, r1, s2, r2, s3) = bufs
        half = cols_of(s) // 2
        c = copies(s, i)
        for d in range(2):
            c["second"](d).wait_recv()
        left = own[i, row, :, :half] + in1[i, 0, down].astype(F32) + in2[i, 0].astype(F32)
        right = own[i, row, :, half:] + in1[i, 1, across].astype(F32) + in2[i, 1].astype(F32)

        @pl.when(i < chips - 1)
        def _():
            out3[i, :, :half] = left.astype(BF16)
            out3[i, :, half:] = right.astype(BF16)
            c["last"]().start()

        @pl.when(i == chips - 1)
        def _():
            outs[s][:, :half] = left
            outs[s][:, half:] = right

    def round_step(n, _):
        for stage, work in enumerate((make, first_stage, second_stage, third_stage)):

            @pl.when((n >= stage) & (n < chips + stage))
            def _():
                for s in range(count):
                    work(s, n - stage)

        return 0

    lax.fori_loop(0, chips + 3, round_step, 0)
    for s in range(count):
        in3 = streams[s][2][9]
        for i in range(chips - 1):
            copies(s, i)["last"]().wait_recv()
            outs[s][...] = outs[s][...] + in3[i].astype(F32)

    def finish(i, _):
        for s in range(count):
            c = copies(s, i)
            c["twin"]().wait_send()
            for d in range(2):
                c["first"](d).wait_send()
                c["second"](d).wait_send()

            @pl.when(i < chips - 1)
            def _():
                c["last"]().wait_send()

        return 0

    lax.fori_loop(0, chips, finish, 0)


def reduce_products(pairs, gains):
    chips = lax.axis_size("mp") // 2
    shards = lax.axis_size("rows") * lax.axis_size("mp")
    heights = tuple(left.shape[1] // shards for left, _ in pairs)
    dma = pltpu.SemaphoreType.DMA
    out_shape, scratch = [], []
    for s, (left, right) in enumerate(pairs):
        height = heights[s]
        cols = -(-right.shape[1] // 256) * 256
        half = cols // 2
        out_shape.append(jax.ShapeDtypeStruct((height, cols), F32))
        scratch += [
            pltpu.VMEM((left.shape[1], left.shape[0]), BF16),
            pltpu.VMEM((chips, 4, height, cols), F32),
            pltpu.VMEM((chips, 4, height, cols), BF16),
            pltpu.VMEM((chips, 4, height, cols), BF16),
            pltpu.VMEM((chips, 2, 2, height, half), BF16),
            pltpu.VMEM((chips, 2, 2, height, half), BF16),
            pltpu.VMEM((chips, 2, height, half), BF16),
            pltpu.VMEM((chips, 2, height, half), BF16),
            pltpu.VMEM((chips - 1, height, cols), BF16),
            pltpu.VMEM((chips - 1, height, cols), BF16),
            dma((chips,)),
            dma((chips,)),
            dma((chips, 2)),
            dma((chips, 2)),
            dma((chips, 2)),
            dma((chips, 2)),
            dma((2, chips)),
        ]
    vmem = pl.BlockSpec(memory_space=pltpu.VMEM)
    return pl.pallas_call(
        functools.partial(reduce_kernel, heights),
        out_shape=tuple(out_shape),
        in_specs=[vmem] * (2 * len(pairs) + 1),
        out_specs=(vmem,) * len(pairs),
        scratch_shapes=scratch,
        compiler_params=pltpu.CompilerParams(
            collective_id=2, has_side_effects=True, vmem_limit_bytes=VMEM_LIMIT
        ),
        cost_estimate=pl.CostEstimate(
            flops=50_000_000_000, bytes_accessed=10_000_000, transcendentals=0
        ),
        name="reduce_products",
    )(*[left for left, _ in pairs], *[right for _, right in pairs], gains)


def on_device(
    inputs,
    cotangent,
    corpus_ids,
    corpus_weight,
    attn_gain,
    qkv_weight,
    out_weight,
    ffn_gain,
    gate_weight,
    up_weight,
    down_weight,
):
    both = ("rows", "mp")
    rows_dev, width = inputs.shape
    mp = lax.axis_size("mp")
    me = lax.axis_index("mp")
    row_groups = lax.axis_size("rows")
    corpora = corpus_weight.shape[0]
    subs = rows_dev // BLOCK
    folded = subs == 2
    mirror = [(i, mp - 1 - i) for i in range(mp)]

    def fold(rows):
        if not folded:
            return rows
        return jnp.concatenate(
            [rows[:BLOCK], lax.ppermute(rows[BLOCK:], "mp", mirror)], axis=0
        )

    def to_order(gathered):
        if not folded:
            return gathered
        parts = gathered.reshape(mp, 2, BLOCK, gathered.shape[-1])
        return jnp.stack([parts[:, 0], parts[::-1, 1]], axis=1).reshape(gathered.shape)

    if folded:
        blocks = jnp.stack([2 * me, 2 * mp - 1 - 2 * me]).astype(jnp.int32)
    else:
        blocks = (subs * me + jnp.arange(subs)).astype(jnp.int32)
    positions = (blocks[:, None] * BLOCK + jnp.arange(BLOCK)[None, :]).reshape(-1)

    shard_rows = qkv_weight.shape[0]
    ident = jnp.broadcast_to(corpus_ids.astype(BF16)[:1, None], (shard_rows, 1))
    spare = (-(Q_WIDTH + 2 * KV_WIDTH + 3)) % 128
    shard = jnp.concatenate(
        [
            pack_kv(qkv_weight),
            attn_gain[:, None],
            ffn_gain[:, None],
            ident,
            jnp.zeros((shard_rows, spare), BF16),
        ],
        axis=1,
    )
    qkv_cols = Q_WIDTH + 2 * KV_WIDTH
    qkv_ext = lax.all_gather(shard, both, axis=0, tiled=True)
    qkv_full = qkv_ext[:, :qkv_cols]
    extras = qkv_ext[:, qkv_cols : qkv_cols + 3].astype(F32).T
    gain_one, gain_two = extras[0:1], extras[1:2]
    all_ids = extras[2].reshape(row_groups, -1)[:, 0]
    my_id = corpus_ids[0].astype(F32)
    count = jnp.sum((all_ids == my_id).astype(F32))
    weight_seq = jnp.sum(
        jnp.where(jnp.arange(corpora) == corpus_ids[0], corpus_weight, 0.0)
    )
    seq_scale = weight_seq * row_groups / (corpora * count)

    x = fold(inputs)
    cot = fold(cotangent)
    cot_all = lax.all_gather(cot, "mp", axis=0, tiled=True)
    out_full = lax.all_gather(out_weight, both, axis=0, tiled=True)
    tables = rope_tables(positions)
    normed_one, inverse_one, q, kv = qkv_project(x, gain_one, qkv_full, tables)
    kv_all = to_order(lax.all_gather(kv, "mp", axis=0, tiled=True))
    o, totals = attend(blocks, q, kv_all)

    residual = x.astype(F32)
    middle = residual + dot(o, out_full)
    inverse_two = lax.rsqrt(jnp.mean(middle * middle, axis=-1, keepdims=True) + EPS)
    normed_two = (middle * inverse_two * gain_two).astype(BF16)
    ffn_part, grad_normed_two, gate_grad, up_grad, down_grad = ffn(
        seq_scale, normed_two, cot_all, gate_weight, up_weight, down_weight
    )
    ffn_sum = lax.psum_scatter(ffn_part, "mp", scatter_dimension=0, tiled=True)

    grad_out = cot.astype(F32) * seq_scale
    scaled_two = grad_normed_two * gain_two
    ffn_gain_part = jnp.sum(grad_normed_two * middle * inverse_two, axis=0)
    grad_middle = (
        grad_out
        + inverse_two * scaled_two
        - middle * inverse_two**3 * jnp.mean(scaled_two * middle, axis=-1, keepdims=True)
    )
    grad_middle_low = grad_middle.astype(BF16)
    grad_o = dot_nt(grad_middle_low, out_full).astype(BF16)
    grad_qkv = attend_back(q, kv_all, o, grad_o, totals, tables)
    grad_normed_one = dot_nt(grad_qkv, qkv_full)
    scaled_one = grad_normed_one * gain_one
    attn_gain_part = jnp.sum(grad_normed_one * residual * inverse_one, axis=0)
    input_grad = (
        grad_middle
        + inverse_one * scaled_one
        - residual * inverse_one**3 * jnp.mean(scaled_one * residual, axis=-1, keepdims=True)
    )
    if folded:
        input_grad = jnp.concatenate(
            [
                input_grad[:BLOCK],
                lax.ppermute(input_grad[BLOCK:].astype(BF16), "mp", mirror).astype(F32),
            ],
            axis=0,
        )
    gain_parts = jnp.concatenate(
        [attn_gain_part[None], ffn_gain_part[None], jnp.zeros((6, width), F32)], axis=0
    )
    if row_groups == 4:
        part, proj_grad = reduce_products(
            ((normed_one, grad_qkv), (o, grad_middle_low)), gain_parts
        )
    else:
        part = jnp.concatenate(
            [dot_tn(normed_one, grad_qkv), gain_parts.T, jnp.zeros((width, 120), F32)], axis=1
        )
        part, proj_grad = (
            lax.psum_scatter(p.astype(BF16), both, scatter_dimension=0, tiled=True).astype(F32)
            for p in (part, dot_tn(o, grad_middle_low))
        )
    qkv_grad = unpack_kv(part[:, :qkv_cols])
    attn_gain_grad = part[:, qkv_cols]
    ffn_gain_grad = part[:, qkv_cols + 1]
    outputs = fold((middle + ffn_sum.astype(F32)).astype(BF16))
    gate_grad, up_grad, down_grad = (
        lax.psum(gate_grad, "rows"),
        lax.psum(up_grad, "rows"),
        lax.psum(down_grad, "rows"),
    )
    gate_grad, up_grad, down_grad, part, ffn_sum = lax.optimization_barrier(
        (gate_grad, up_grad, down_grad, part, ffn_sum)
    )
    gate_grad, up_grad, down_grad = (g.astype(F32) for g in (gate_grad, up_grad, down_grad))
    qkv_grad = unpack_kv(part[:, :qkv_cols])
    attn_gain_grad = part[:, qkv_cols]
    ffn_gain_grad = part[:, qkv_cols + 1]
    outputs = fold((middle + ffn_sum.astype(F32)).astype(BF16))
    return (
        outputs,
        input_grad,
        qkv_grad,
        proj_grad,
        gate_grad,
        up_grad,
        down_grad,
        attn_gain_grad,
        ffn_gain_grad,
    )


def solution(mesh):
    split = P(("rows", "mp"), None)
    line = P(("rows", "mp"))
    in_specs = (
        split,
        split,
        P("rows"),
        P(),
        line,
        split,
        split,
        line,
        P(None, "mp"),
        P(None, "mp"),
        P("mp", None),
    )
    out_specs = (
        split,
        split,
        split,
        split,
        P(None, "mp"),
        P(None, "mp"),
        P("mp", None),
        line,
        line,
    )
    return jax.shard_map(
        on_device, mesh=mesh, in_specs=in_specs, out_specs=out_specs, check_vma=False
    )
```

```python
import functools

import jax
import jax.numpy as jnp
from jax import lax
from jax.experimental import pallas as pl
from jax.experimental.pallas import tpu as pltpu
from jax.sharding import PartitionSpec as P

HEADS = 20
KV_HEADS = 5
HEAD_DIM = 64
GROUP = HEADS // KV_HEADS
Q_WIDTH = HEADS * HEAD_DIM
KV_WIDTH = KV_HEADS * HEAD_DIM
LEN = 2048
BLOCK = 128
KTILE = 256
EPS = 1e-05
THETA = 10000.0
LANES = GROUP * BLOCK
SLAB = 2 * HEAD_DIM

MESH = pl.DeviceIdType.MESH
F32 = jnp.float32
BF16 = jnp.bfloat16
VMEM_LIMIT = 62 * 1024 * 1024


def rope_tables(positions):
    half_dim = HEAD_DIM // 2
    freqs = jnp.exp(-jnp.log(THETA) * (2.0 * jnp.arange(half_dim, dtype=F32)) / HEAD_DIM)
    angles = positions.astype(F32)[:, None] * freqs[None, :]
    cosine, sine = jnp.cos(angles), jnp.sin(angles)
    ones, zeros = jnp.ones_like(cosine), jnp.zeros_like(cosine)
    head_cos = jnp.concatenate([cosine, cosine], axis=1)
    head_sin = jnp.concatenate([-sine, sine], axis=1)
    cos_q = jnp.concatenate([head_cos, head_cos], axis=1)
    sin_q = jnp.concatenate([head_sin, head_sin], axis=1)
    cos_kv = jnp.concatenate([head_cos, ones, ones], axis=1)
    sin_kv = jnp.concatenate([head_sin, zeros, zeros], axis=1)
    return (cos_q, sin_q, cos_kv, sin_kv)


def swap_halves(slab):
    lane = lax.broadcasted_iota(jnp.int32, slab.shape, 1)
    half_dim = HEAD_DIM // 2
    up = pltpu.roll(slab, SLAB - half_dim, 1)
    down = pltpu.roll(slab, half_dim, 1)
    return jnp.where(lane % HEAD_DIM < half_dim, up, down)


def qkv_kernel(x_ref, gain_ref, w_ref, cos_q, sin_q, cos_kv, sin_kv, normed_ref, inv_ref, q_ref, kv_ref):
    x = x_ref[...].astype(F32)
    inverse = lax.rsqrt(jnp.mean(x * x, axis=-1, keepdims=True) + EPS)
    normed = (x * inverse * gain_ref[...]).astype(BF16)
    normed_ref[...] = normed
    inv_ref[...] = inverse
    for s in range(Q_WIDTH // 256):
        part = jnp.dot(normed, w_ref[:, s * 256 : (s + 1) * 256], preferred_element_type=F32)
        for t in range(2):
            slab = part[:, t * SLAB : (t + 1) * SLAB]
            col = s * 256 + t * SLAB
            turned = slab * cos_q[...] + swap_halves(slab) * sin_q[...]
            q_ref[:, col : col + SLAB] = (turned.astype(BF16).astype(F32) * HEAD_DIM ** (-0.5)).astype(BF16)
    part = jnp.dot(normed, w_ref[:, Q_WIDTH : Q_WIDTH + 2 * KV_WIDTH], preferred_element_type=F32)
    for g in range(KV_HEADS):
        slab = part[:, g * SLAB : (g + 1) * SLAB]
        turned = slab * cos_kv[...] + swap_halves(slab) * sin_kv[...]
        kv_ref[:, g * SLAB : (g + 1) * SLAB] = turned.astype(BF16)


def qkv_project(x, gain, weight, tables):
    rows, width = x.shape
    return pl.pallas_call(
        qkv_kernel,
        out_shape=(
            jax.ShapeDtypeStruct((rows, width), BF16),
            jax.ShapeDtypeStruct((rows, 1), F32),
            jax.ShapeDtypeStruct((rows, Q_WIDTH), BF16),
            jax.ShapeDtypeStruct((rows, 2 * KV_WIDTH), BF16),
        ),
        compiler_params=pltpu.CompilerParams(vmem_limit_bytes=VMEM_LIMIT),
        name="qkv_project",
    )(x, gain, weight, *tables)


def heads_to_lanes(rows_part):
    turned = rows_part.T
    return jnp.concatenate(
        [turned[h * HEAD_DIM : (h + 1) * HEAD_DIM, :] for h in range(GROUP)], axis=1
    )


def lanes_to_heads(lanes_part):
    stacked = jnp.concatenate(
        [lanes_part[:, h * BLOCK : (h + 1) * BLOCK] for h in range(GROUP)], axis=0
    )
    return stacked.T


def causal(tile, block):
    key_pos = tile * KTILE + lax.broadcasted_iota(jnp.int32, (KTILE, LANES), 0)
    query_pos = block * BLOCK + lax.broadcasted_iota(jnp.int32, (KTILE, LANES), 1) % BLOCK
    return key_pos <= query_pos


def over_rows(left, right):
    return lax.dot_general(left, right, (((0,), (0,)), ((), ())), preferred_element_type=F32)


def attend_kernel(block_ref, q_ref, kv_ref, o_ref, total_ref):
    subs = q_ref.shape[0] // BLOCK
    for sub in range(subs):
        block = block_ref[sub]
        queries = heads_to_lanes(q_ref[sub * BLOCK : (sub + 1) * BLOCK, :].astype(F32))
        queries = jnp.concatenate([queries, jnp.zeros_like(queries)], axis=0).astype(BF16)

        def step(tile, carry, masked):
            top, total, acc = carry
            kv = kv_ref[pl.ds(pl.multiple_of(tile * KTILE, KTILE), KTILE), :]
            scores = jnp.dot(kv, queries, preferred_element_type=F32)
            if masked:
                scores = jnp.where(causal(tile, block), scores, -1e30)
            new_top = jnp.maximum(top, jnp.max(scores, axis=0, keepdims=True))
            decay = jnp.exp(top - new_top)
            probs = jnp.exp(scores - new_top)
            total = decay * total + jnp.sum(probs, axis=0, keepdims=True)
            acc = decay * acc + over_rows(kv, probs.astype(BF16))
            return (new_top, total, acc)

        start = (
            jnp.full((1, LANES), -1e30, F32),
            jnp.zeros((1, LANES), F32),
            jnp.zeros((SLAB, LANES), F32),
        )
        full = block * BLOCK // KTILE
        carry = lax.fori_loop(0, full, lambda t, c: step(t, c, False), start)
        top, total, acc = step(full, carry, True)
        out = acc[HEAD_DIM:, :] / total
        o_ref[sub * BLOCK : (sub + 1) * BLOCK, :] = lanes_to_heads(out).astype(BF16)
        total_ref[sub : sub + 1, :] = top + jnp.log(total)


def attend(blocks, q, kv_all):
    rows = q.shape[0]
    subs = rows // BLOCK
    return pl.pallas_call(
        attend_kernel,
        grid_spec=pltpu.PrefetchScalarGridSpec(
            num_scalar_prefetch=1,
            grid=(KV_HEADS,),
            in_specs=[
                pl.BlockSpec((rows, GROUP * HEAD_DIM), lambda g, b: (0, g)),
                pl.BlockSpec((LEN, SLAB), lambda g, b: (0, g)),
            ],
            out_specs=[
                pl.BlockSpec((rows, GROUP * HEAD_DIM), lambda g, b: (0, g)),
                pl.BlockSpec((None, subs, LANES), lambda g, b: (g, 0, 0)),
            ],
        ),
        out_shape=(
            jax.ShapeDtypeStruct((rows, Q_WIDTH), BF16),
            jax.ShapeDtypeStruct((KV_HEADS, subs, LANES), F32),
        ),
        compiler_params=pltpu.CompilerParams(vmem_limit_bytes=VMEM_LIMIT),
        cost_estimate=pl.CostEstimate(
            flops=60_000_000_000, bytes_accessed=8_000_000, transcendentals=6_000_000
        ),
        name="attend",
    )(blocks, q, kv_all)


def attend_back_kernel(
    q_ref,
    kv_ref,
    o_ref,
    do_ref,
    total_ref,
    cos_q,
    sin_q,
    cos_kv,
    sin_kv,
    grad_ref,
    dkv_acc,
    own_part,
    twin_out,
    twin_in,
    sum_out,
    sum_in,
    mine,
    twin_send,
    twin_recv,
    sum_send,
    sum_recv,
):
    subs = q_ref.shape[0] // BLOCK
    chips = lax.axis_size("mp") // 2
    me = lax.axis_index("mp")
    row = lax.axis_index("rows")
    chip = me // 2
    core = me % 2
    twin = (row, me + 1 - 2 * core)
    width = GROUP * HEAD_DIM

    barrier = pltpu.get_barrier_semaphore()
    pl.semaphore_signal(barrier, inc=1, device_id=twin, device_id_type=MESH)
    for step in range(1, chips):
        pl.semaphore_signal(
            barrier,
            inc=1,
            device_id=(row, 2 * ((chip + step) % chips) + core),
            device_id_type=MESH,
        )
    pl.semaphore_wait(barrier, chips)

    def twin_copy(g):
        return pltpu.make_async_remote_copy(
            src_ref=twin_out.at[g % 2],
            dst_ref=twin_in.at[g],
            send_sem=twin_send.at[g % 2],
            recv_sem=twin_recv.at[g],
            device_id=twin,
            device_id_type=MESH,
        )

    def sum_copy(g, step):
        return pltpu.make_async_remote_copy(
            src_ref=sum_out.at[g, step - 1],
            dst_ref=sum_in.at[g, step - 1],
            send_sem=sum_send.at[g, step - 1],
            recv_sem=sum_recv.at[g, step - 1],
            device_id=(row, 2 * ((chip + step) % chips) + core),
            device_id_type=MESH,
        )

    def combine(g):
        twin_copy(g).wait_recv()
        for step in range(1, chips):
            goal = (chip + step) % chips
            sum_out[g, step - 1] = (
                own_part[g % 2, goal] + twin_in[g, goal].astype(F32)
            ).astype(BF16)
            sum_copy(g, step).start()
        mine[g] = own_part[g % 2, chip] + twin_in[g, chip].astype(F32)

    def head_step(g, _):
        cols = pl.ds(pl.multiple_of(g * width, width), width)
        pair = pl.ds(pl.multiple_of(g * SLAB, SLAB), SLAB)
        dkv_acc[...] = jnp.zeros_like(dkv_acc)
        for sub in range(subs):
            rows = slice(sub * BLOCK, (sub + 1) * BLOCK)
            block = natural(me, sub, subs)
            queries = heads_to_lanes(q_ref[rows, cols].astype(F32))
            grads = heads_to_lanes(do_ref[rows, cols].astype(F32))
            outs = heads_to_lanes(o_ref[rows, cols].astype(F32))
            delta = jnp.sum(grads * outs, axis=0, keepdims=True)
            empty = jnp.zeros_like(queries)
            queries = jnp.concatenate([queries, empty], axis=0)
            grads = jnp.concatenate([empty, grads], axis=0)
            query_rows = queries.T.astype(BF16)
            grad_rows = grads.T.astype(BF16)
            queries = queries.astype(BF16)
            grads = grads.astype(BF16)
            log_total = total_ref[g, sub : sub + 1, :]

            def step(tile, dq, masked):
                keys = pl.ds(pl.multiple_of(tile * KTILE, KTILE), KTILE)
                kv = kv_ref[keys, pair]
                scores = jnp.dot(kv, queries, preferred_element_type=F32)
                probs = jnp.exp(scores - log_total)
                if masked:
                    probs = jnp.where(causal(tile, block), probs, 0.0)
                grad_probs = jnp.dot(kv, grads, preferred_element_type=F32)
                grad_scores = (probs * (grad_probs - delta)).astype(BF16)
                dkv_acc[keys, :] += jnp.dot(
                    grad_scores, query_rows, preferred_element_type=F32
                ) + jnp.dot(probs.astype(BF16), grad_rows, preferred_element_type=F32)
                return dq + over_rows(kv, grad_scores)

            full = block * BLOCK // KTILE
            dq = lax.fori_loop(
                0, full, lambda t, c: step(t, c, False), jnp.zeros((SLAB, LANES), F32)
            )
            dq = step(full, dq, True)
            dq = lanes_to_heads(dq[:HEAD_DIM, :]) * HEAD_DIM ** (-0.5)
            for t in range(width // SLAB):
                slab = dq[:, t * SLAB : (t + 1) * SLAB]
                turned = slab * cos_q[rows, :] - swap_halves(slab) * sin_q[rows, :]
                first = pl.multiple_of(g * width + t * SLAB, SLAB)
                grad_ref[rows, pl.ds(first, SLAB)] = turned.astype(BF16)

        @pl.when(g >= 2)
        def _():
            twin_copy(g - 2).wait_send()

        for goal in range(chips):
            for sub in range(subs):
                first = natural(2 * goal + core, sub, subs) * BLOCK
                own_part[g % 2, goal, sub] = dkv_acc[pl.ds(pl.multiple_of(first, BLOCK), BLOCK), :]
                first = natural(2 * goal + 1 - core, sub, subs) * BLOCK
                twin_out[g % 2, goal, sub] = dkv_acc[
                    pl.ds(pl.multiple_of(first, BLOCK), BLOCK), :
                ].astype(BF16)
        twin_copy(g).start()

        @pl.when(g >= 1)
        def _():
            combine(g - 1)

        return 0

    lax.fori_loop(0, KV_HEADS, head_step, 0)
    combine(KV_HEADS - 1)

    for g in range(KV_HEADS):
        total = mine[g]
        for step in range(1, chips):
            sum_copy(g, step).wait_recv()
            total = total + sum_in[g, step - 1].astype(F32)
        slab = total.reshape(subs * BLOCK, SLAB)
        turned = slab * cos_kv[...] - swap_halves(slab) * sin_kv[...]
        first = Q_WIDTH + g * SLAB
        grad_ref[:, first : first + SLAB] = turned.astype(BF16)
    for g in range(KV_HEADS):
        for step in range(1, chips):
            sum_copy(g, step).wait_send()
    for g in range(KV_HEADS - 2, KV_HEADS):
        twin_copy(g).wait_send()


def attend_back(q, kv_all, o, grad_o, totals, tables):
    rows = q.shape[0]
    subs = rows // BLOCK
    chips = lax.axis_size("mp") // 2
    vmem = pl.BlockSpec(memory_space=pltpu.VMEM)
    dma = pltpu.SemaphoreType.DMA
    part = (chips, subs, BLOCK, SLAB)
    return pl.pallas_call(
        attend_back_kernel,
        in_specs=[vmem] * 9,
        out_specs=vmem,
        out_shape=jax.ShapeDtypeStruct((rows, Q_WIDTH + 2 * KV_WIDTH), BF16),
        scratch_shapes=[
            pltpu.VMEM((LEN, SLAB), F32),
            pltpu.VMEM((2,) + part, F32),
            pltpu.VMEM((2,) + part, BF16),
            pltpu.VMEM((KV_HEADS,) + part, BF16),
            pltpu.VMEM((KV_HEADS, chips - 1) + part[1:], BF16),
            pltpu.VMEM((KV_HEADS, chips - 1) + part[1:], BF16),
            pltpu.VMEM((KV_HEADS,) + part[1:], F32),
            dma((2,)),
            dma((KV_HEADS,)),
            dma((KV_HEADS, chips - 1)),
            dma((KV_HEADS, chips - 1)),
        ],
        compiler_params=pltpu.CompilerParams(
            collective_id=3, has_side_effects=True, vmem_limit_bytes=VMEM_LIMIT
        ),
        cost_estimate=pl.CostEstimate(
            flops=120_000_000_000, bytes_accessed=12_000_000, transcendentals=6_000_000
        ),
        name="attend_back",
    )(q, kv_all, o, grad_o, totals, *tables)


def pack_kv(columns):
    lead = columns.shape[:-1]
    kv = columns[..., Q_WIDTH:].reshape(*lead, 2, KV_HEADS, HEAD_DIM)
    kv = jnp.swapaxes(kv, -3, -2).reshape(*lead, 2 * KV_WIDTH)
    return jnp.concatenate([columns[..., :Q_WIDTH], kv], axis=-1)


def unpack_kv(columns):
    lead = columns.shape[:-1]
    kv = columns[..., Q_WIDTH:].reshape(*lead, KV_HEADS, 2, HEAD_DIM)
    kv = jnp.swapaxes(kv, -3, -2).reshape(*lead, 2 * KV_WIDTH)
    return jnp.concatenate([columns[..., :Q_WIDTH], kv], axis=-1)


def dot(left, right):
    return jnp.dot(left, right, preferred_element_type=F32)


def dot_nt(left, right):
    return lax.dot_general(left, right, (((1,), (1,)), ((), ())), preferred_element_type=F32)


def dot_tn(left, right):
    return lax.dot_general(left, right, (((0,), (0,)), ((), ())), preferred_element_type=F32)


def half_of(ref, chip, core, sub, rows):
    subs = ref.shape[0] // (rows * lax.axis_size("mp"))
    start = natural(2 * chip + core, sub, subs) * rows
    return ref.at[pl.ds(pl.multiple_of(start, rows), rows)]


def part_of(ref, chip, core, sub, rows):
    subs = ref.shape[0] // (rows * lax.axis_size("mp"))
    start = (subs * (2 * chip + core) + sub) * rows
    return ref.at[pl.ds(pl.multiple_of(start, rows), rows)]


def ffn_kernel(
    subs,
    quad,
    scale_ref,
    x_ref,
    cot_ref,
    gate_ref,
    up_ref,
    down_ref,
    part_ref,
    part_in,
    relay_in,
    part_sum,
    sum_ref,
    gate_out,
    up_out,
    down_out,
    *rest,
):
    slots = rest[:9] if quad else ()
    scratch = rest[9:] if quad else rest
    ffn_body(
        subs,
        quad,
        slots,
        scale_ref,
        x_ref,
        cot_ref,
        gate_ref,
        up_ref,
        down_ref,
        part_ref,
        part_in,
        relay_in,
        part_sum,
        sum_ref,
        gate_out,
        up_out,
        down_out,
        *scratch,
    )


def ffn_body(
    subs,
    quad,
    slots,
    scale_ref,
    x_ref,
    cot_ref,
    gate_ref,
    up_ref,
    down_ref,
    part_ref,
    part_in,
    relay_in,
    part_sum,
    sum_ref,
    gate_out,
    up_out,
    down_out,
    x_all,
    hid,
    dgate,
    dup,
    cot_buf,
    part_own,
    twin_buf,
    twin_in,
    send_buf,
    sums_in,
    cot_cols,
    wide_buf,
    tall_buf,
    x_send,
    x_recv,
    twin_x_send,
    twin_x_recv,
    twin_send,
    twin_recv,
    sum_send,
    sum_recv,
    p_send,
    p_recv,
    relay_recv,
    relay_sem,
    cot_sem,
    part_sem,
    cols_sem,
    out_sem,
    *row_scratch,
):
    chips = lax.axis_size("mp") // 2
    me = lax.axis_index("mp")
    row = lax.axis_index("rows")
    chip = me // 2
    core = me % 2
    rows = x_ref.shape[0] // subs
    units = chips * subs
    twin = (row, me + 1 - 2 * core)

    def on_chip(other):
        return (row, 2 * other + core)

    barrier = pltpu.get_barrier_semaphore()
    pl.semaphore_signal(barrier, inc=1, device_id=twin, device_id_type=MESH)
    for step in range(1, chips):
        pl.semaphore_signal(
            barrier, inc=1, device_id=on_chip((chip + step) % chips), device_id_type=MESH
        )
    down, across = row // 2, row % 2
    beside_row = row + 1 - 2 * across
    above_row = (1 - down) * 2 + across
    neighbours = ((beside_row, me), (above_row, me))
    if quad:
        for device in neighbours:
            pl.semaphore_signal(barrier, inc=1, device_id=device, device_id_type=MESH)
    pl.semaphore_wait(barrier, chips + 2 if quad else chips)

    def order(i):
        near = jnp.minimum(chip, chips - 1 - chip)
        long_side = jnp.where(chip < chips - 1 - chip, 1, -1)
        j = i - subs
        paired = j < 2 * subs * near
        rest = j - 2 * subs * near
        dist = jnp.where(paired, j // (2 * subs) + 1, near + 1 + rest // subs)
        sub = jnp.where(paired, (j % (2 * subs)) // 2, rest % subs)
        side = jnp.where(paired, 1 - 2 * (j % 2), long_side)
        own = i < subs
        return (jnp.where(own, chip, chip + side * dist), jnp.where(own, i, sub))

    def x_copy(other, sub, side, source=None):
        spot = half_of(x_all, other, core, sub, rows)
        return pltpu.make_async_remote_copy(
            src_ref=spot if source is None else source,
            dst_ref=spot,
            send_sem=x_send.at[(side + 1) // 2, other * subs + sub],
            recv_sem=x_recv.at[other * subs + sub],
            device_id=on_chip(chip + side),
            device_id_type=MESH,
        )

    def twin_x_copy(other, sub, source=None):
        spot = half_of(x_all, other, core, sub, rows)
        return pltpu.make_async_remote_copy(
            src_ref=spot if source is None else source,
            dst_ref=spot,
            send_sem=twin_x_send.at[other * subs + sub],
            recv_sem=twin_x_recv.at[other * subs + sub],
            device_id=twin,
            device_id_type=MESH,
        )

    def twin_sum_copy(slot):
        return pltpu.make_async_remote_copy(
            src_ref=twin_buf.at[slot],
            dst_ref=twin_in.at[slot],
            send_sem=twin_send.at[slot],
            recv_sem=twin_recv.at[slot],
            device_id=twin,
            device_id_type=MESH,
        )

    def sum_copy(other, sub):
        side = jnp.where(other > chip, 1, -1)
        slot = jnp.where((side == 1) & (other == chip + 1), chips, other)
        return pltpu.make_async_remote_copy(
            src_ref=send_buf.at[other * subs + sub],
            dst_ref=sums_in.at[slot, sub],
            send_sem=sum_send.at[other * subs + sub],
            recv_sem=sum_recv.at[slot, sub],
            device_id=on_chip(chip + side),
            device_id_type=MESH,
        )

    def sum_arrival(slot, sub):
        return pltpu.make_async_remote_copy(
            src_ref=send_buf.at[0],
            dst_ref=sums_in.at[slot, sub],
            send_sem=sum_send.at[0],
            recv_sem=sum_recv.at[slot, sub],
            device_id=twin,
            device_id_type=MESH,
        )

    def cot_copies(other, sub, slot):
        return [
            pltpu.make_async_copy(
                half_of(cot_ref, other, c, sub, rows),
                cot_buf.at[slot, pl.ds(c * rows, rows)],
                cot_sem.at[slot, c],
            )
            for c in range(2)
        ]

    def part_copy(i):
        other, sub = order(i)
        return pltpu.make_async_copy(
            part_own.at[i % 2], part_ref.at[other * subs + sub], part_sem.at[i % 2]
        )

    for sub in range(subs):
        source = x_ref.at[pl.ds(sub * rows, rows)]

        @pl.when(chip < chips - 1)
        def _():
            x_copy(chip, sub, 1, source).start()

        @pl.when(chip > 0)
        def _():
            x_copy(chip, sub, -1, source).start()

        twin_x_copy(chip, sub, source).start()
    for copy in cot_copies(chip, 0, 0):
        copy.start()
    for sub in range(subs):
        half_of(x_all, chip, core, sub, rows)[...] = x_ref[sub * rows : (sub + 1) * rows, :]

    def reduce_unit(i):
        other, sub = order(i)
        unit = other * subs + sub
        slot = i % 2
        twin_sum_copy(slot).wait_recv()
        part_own[slot] = (
            part_own[slot].astype(F32) + twin_in[slot, 1].astype(F32)
        ).astype(BF16)
        part_copy(i).start()
        arrived = twin_in[slot, 0].astype(F32)
        lines = pl.ds(pl.multiple_of(sub * rows, rows), rows)

        @pl.when(other == chip)
        def _():
            sum_ref[lines, :] = sum_ref[lines, :] + arrived

        @pl.when(other != chip)
        def _():
            send_buf[unit] = (send_buf[unit].astype(F32) + arrived).astype(BF16)

        @pl.when(((other > chip) & (chip == 0)) | ((other < chip) & (chip == chips - 1)))
        def _():
            sum_copy(other, sub).start()

    def pass_on(e):
        right, left = chips - 1 - chip, chip
        right_first = chip < chips // 2
        ahead = jnp.where(right_first, right, left)
        step = jnp.where(e < ahead, e + 1, e - ahead + 1)
        toward = jnp.where((e < ahead) == right_first, 1, -1)
        other = chip + toward * step

        @pl.when((chip > 0) & (chip < chips - 1))
        def _():
            for sub in range(subs):
                unit = other * subs + sub
                sum_arrival(other, sub).wait_recv()
                send_buf[unit] = (
                    send_buf[unit].astype(F32) + sums_in[other, sub].astype(F32)
                ).astype(BF16)
                sum_copy(other, sub).start()

    def unit_step(i, _):
        other, sub = order(i)
        slot = i % 2

        @pl.when(i + 1 < units)
        def _():
            for copy in cot_copies(*order(i + 1), 1 - slot):
                copy.start()

        @pl.when(other != chip)
        def _():
            x_copy(other, sub, 1).wait_recv()
            twin_x_copy(other, sub).start()

            @pl.when((other > chip) & (chip > 0))
            def _():
                x_copy(other, sub, -1).start()

            @pl.when((other < chip) & (chip < chips - 1))
            def _():
                x_copy(other, sub, 1).start()

        twin_x_copy(other, sub).wait_recv()
        for copy in cot_copies(other, sub, slot):
            copy.wait()
        halves = [half_of(x_all, other, c, sub, rows)[...] for c in range(2)]
        x = jnp.concatenate(halves, axis=0)
        gate = dot(x, gate_ref[...])
        up = dot(x, up_ref[...])
        grad = dot_nt(cot_buf[slot], down_ref[...]) * scale_ref[0]
        sig = 1.0 / (1.0 + jnp.exp(-gate))
        act = gate * sig
        h = (act * up).astype(BF16)
        dg = (grad * up * (sig * (1.0 + gate * (1.0 - sig)))).astype(BF16)
        du = (grad * act).astype(BF16)
        for c in range(2):
            piece = slice(c * rows, (c + 1) * rows)
            half_of(hid, other, c, sub, rows)[...] = h[piece]
            half_of(dgate, other, c, sub, rows)[...] = dg[piece]
            half_of(dup, other, c, sub, rows)[...] = du[piece]

        @pl.when(i >= 2)
        def _():
            part_copy(i - 2).wait()
            twin_sum_copy(slot).wait_send()

        part = dot(h, down_ref[...])

        def keep_part(own, away):
            part_own[slot] = own.astype(BF16)
            twin_buf[slot, 1] = away.astype(BF16)

        @pl.when(core == 0)
        def _():
            keep_part(part[:rows], part[rows:])

        @pl.when(core == 1)
        def _():
            keep_part(part[rows:], part[:rows])

        dx = dot_nt(dg, gate_ref[...]) + dot_nt(du, up_ref[...])

        def keep(own, away):
            twin_buf[slot, 0] = away.astype(BF16)

            @pl.when(other == chip)
            def _():
                sum_ref[pl.ds(pl.multiple_of(sub * rows, rows), rows), :] = own

            @pl.when(other != chip)
            def _():
                send_buf[other * subs + sub] = own.astype(BF16)

        @pl.when(core == 0)
        def _():
            keep(dx[:rows], dx[rows:])

        @pl.when(core == 1)
        def _():
            keep(dx[rows:], dx[:rows])

        twin_sum_copy(slot).start()

        @pl.when(i >= 1)
        def _():
            reduce_unit(i - 1)

        return 0

    lax.fori_loop(0, units, unit_step, 0)
    reduce_unit(units - 1)
    for i in (units - 2, units - 1):
        part_copy(i).wait()
        twin_sum_copy(i % 2).wait_send()

    width = x_ref.shape[1]
    ff = gate_ref.shape[1]
    tall = tall_buf.shape[1]
    narrow = tall_buf.shape[2]
    down_cols = cot_cols.shape[2]
    col_steps = width // down_cols
    pieces = width // tall
    steps = pieces * (ff // narrow)
    wholes = (gate_out, up_out, down_out)

    if quad:
        firsts, seconds, finals = slots[0:3], slots[3:6], slots[6:9]
        tall_in, wide_in, moved, one_send, one_recv, two_send, two_recv, load_sem, fin_sem = (
            row_scratch[:2] + (row_scratch[2:5],) + row_scratch[5:]
        )

    def remote(source, dest, send, recv, device):
        return pltpu.make_async_remote_copy(
            src_ref=source,
            dst_ref=dest,
            send_sem=send,
            recv_sem=recv,
            device_id=device,
            device_id_type=MESH,
        )

    def block_at(a, block, d):
        high, wide = firsts[a].shape[2:]
        lines = pl.ds(pl.multiple_of(block * high, high), high)
        return wholes[a].at[lines, pl.ds(d * wide, wide)]

    def one_copy(a, d, k):
        block = k * 2 + 1 - across if d == 0 else (1 - down) * 2 + k
        return remote(
            block_at(a, block, d),
            firsts[a].at[d, k],
            one_send.at[a, d, k],
            one_recv.at[a, d, k],
            neighbours[d],
        )

    def two_copy(a, d):
        return remote(
            moved[a].at[d],
            seconds[a].at[d],
            two_send.at[a, d],
            two_recv.at[a, d],
            neighbours[1 - d],
        )

    def fin_copy(a, d):
        wide = firsts[a].shape[3]
        return pltpu.make_async_copy(
            (wide_in if a == 2 else tall_in).at[0],
            finals[a].at[:, pl.ds(d * wide, wide)],
            fin_sem.at[d],
        )

    def load(sources, buf):
        copies = [
            pltpu.make_async_copy(source, buf.at[i], load_sem.at[i])
            for i, source in enumerate(sources)
        ]
        for copy in copies:
            copy.start()
        for copy in copies:
            copy.wait()

    def stage_one(a):
        if quad:
            for d in range(2):
                for k in range(2):
                    one_copy(a, d, k).start()

    def stage_two(a):
        if quad:
            buf = wide_in if a == 2 else tall_in
            for d in range(2):
                for k in range(2):
                    one_copy(a, d, k).wait_recv()
                block = above_row if d == 0 else beside_row
                other = 1 - down if d == 0 else 1 - across
                load([block_at(a, block, d), firsts[a].at[d, other]], buf)
                moved[a][d] = (buf[0].astype(F32) + buf[1].astype(F32)).astype(BF16)
                two_copy(a, d).start()

    def stage_three(a):
        if quad:
            buf = wide_in if a == 2 else tall_in
            for d in range(2):
                two_copy(a, d).wait_recv()
                other = down if d == 0 else across
                load([block_at(a, row, d), firsts[a].at[d, other], seconds[a].at[d]], buf)
                buf[0] = (
                    buf[0].astype(F32) + buf[1].astype(F32) + buf[2].astype(F32)
                ).astype(BF16)
                fin_copy(a, d).start()
                fin_copy(a, d).wait()

    def end_far(source, other):
        return ((source == 0) & (other >= 2)) | ((source == chips - 1) & (other <= chips - 3))

    def relayed(source, other):
        return ((source == 1) & (other >= 2)) | ((source == chips - 2) & (other <= chips - 3))

    def p_copy(other, sub, source=None):
        return remote(
            part_ref.at[other * subs + sub] if source is None else source,
            part_in.at[chip, sub],
            p_send.at[other * subs + sub],
            p_recv.at[chip, sub],
            on_chip(other),
        )

    def relay_copy(other, sub):
        return remote(
            part_ref.at[other * subs + sub],
            relay_in.at[other, sub],
            p_send.at[other * subs + sub],
            relay_recv.at[other, sub],
            on_chip(jnp.where(chip == 0, 1, chips - 2)),
        )

    def send_parts():
        for far in (True, False):
            for step in range(1, chips):
                other = (chip + step) % chips
                beyond = end_far(chip, other)
                for sub in range(subs):
                    if far:

                        @pl.when(beyond)
                        def _():
                            relay_copy(other, sub).start()

                    else:

                        @pl.when(jnp.logical_not(beyond | relayed(chip, other)))
                        def _():
                            p_copy(other, sub).start()

    def piece(index):
        return cot_buf.at[index // 2, pl.ds(index % 2 * rows, rows)]

    def fetch(source, index):
        copy = pltpu.make_async_copy(source, piece(index), relay_sem.at[index])
        copy.start()
        return copy

    def relay_parts():
        for step in range(1, chips):
            other = (chip + step) % chips

            @pl.when(relayed(chip, other))
            def _():
                for sub in range(subs):
                    mine = fetch(part_ref.at[other * subs + sub], 2 * sub)
                    remote(
                        part_ref.at[0],
                        relay_in.at[other, sub],
                        p_send.at[0],
                        relay_recv.at[other, sub],
                        twin,
                    ).wait_recv()
                    theirs = fetch(relay_in.at[other, sub], 2 * sub + 1)
                    mine.wait()
                    theirs.wait()
                    part_ref_sum = piece(2 * sub)[...].astype(F32) + piece(2 * sub + 1)[
                        ...
                    ].astype(F32)
                    piece(2 * sub)[...] = part_ref_sum.astype(BF16)
                    back = pltpu.make_async_copy(
                        piece(2 * sub), part_ref.at[other * subs + sub], relay_sem.at[2 * sub]
                    )
                    back.start()
                    back.wait()
                    p_copy(other, sub).start()

    def total_parts():
        for sub in range(subs):
            lines = slice(sub * rows, (sub + 1) * rows)
            fetch(part_ref.at[chip * subs + sub], 0).wait()
            part_sum[lines, :] = piece(0)[...].astype(F32)
            for step in range(1, chips):
                other = (chip + step) % chips

                @pl.when(jnp.logical_not(end_far(other, chip)))
                def _():
                    remote(
                        part_ref.at[0],
                        part_in.at[other, sub],
                        p_send.at[0],
                        p_recv.at[other, sub],
                        twin,
                    ).wait_recv()
                    fetch(part_in.at[other, sub], 0).wait()
                    part_sum[lines, :] = part_sum[lines, :] + piece(0)[...].astype(F32)

    for a, source in enumerate((dgate, dup)):

        def tall_out(j):
            first = pl.multiple_of(j % pieces * tall, tall)
            col = pl.multiple_of(j // pieces * narrow, narrow)
            return pltpu.make_async_copy(
                tall_buf.at[j % 2],
                wholes[a].at[pl.ds(first, tall), pl.ds(col, narrow)],
                out_sem.at[j % 2],
            )

        def tall_step(j, _):
            @pl.when(j >= 2)
            def _():
                tall_out(j - 2).wait()

            first = pl.multiple_of(j % pieces * tall, tall)
            col = pl.multiple_of(j // pieces * narrow, narrow)
            tall_buf[j % 2] = dot_tn(
                x_all[:, pl.ds(first, tall)], source[:, pl.ds(col, narrow)]
            ).astype(BF16)
            tall_out(j).start()
            return 0

        lax.fori_loop(0, steps, tall_step, 0)
        for j in range(steps - 2, steps):
            tall_out(j).wait()
        stage_one(a)
        for e in range(a * (chips - 1) // 3, (a + 1) * (chips - 1) // 3):
            pass_on(e)
    send_parts()

    def cols_copy(j):
        return pltpu.make_async_copy(
            cot_ref.at[:, pl.ds(pl.multiple_of(j * down_cols, down_cols), down_cols)],
            cot_cols.at[j % 2],
            cols_sem.at[j % 2],
        )

    def wide_out(j):
        return pltpu.make_async_copy(
            wide_buf.at[j % 2],
            down_out.at[:, pl.ds(pl.multiple_of(j * down_cols, down_cols), down_cols)],
            out_sem.at[j % 2],
        )

    cols_copy(0).start()

    def down_step(j, _):
        @pl.when(j + 1 < col_steps)
        def _():
            cols_copy(j + 1).start()

        cols_copy(j).wait()

        @pl.when(j >= 2)
        def _():
            wide_out(j - 2).wait()

        wide_buf[j % 2] = (dot_tn(hid[...], cot_cols[j % 2]) * scale_ref[0]).astype(BF16)
        wide_out(j).start()
        return 0

    lax.fori_loop(0, col_steps, down_step, 0)
    for j in range(max(0, col_steps - 2), col_steps):
        wide_out(j).wait()
    stage_one(2)
    for e in range(2 * (chips - 1) // 3, chips - 1):
        pass_on(e)
    stage_two(0)
    stage_two(1)
    stage_three(0)
    relay_parts()
    stage_two(2)
    stage_three(1)
    stage_three(2)
    total_parts()
    if quad:
        for a in range(3):
            for d in range(2):
                two_copy(a, d).wait_send()
                for k in range(2):
                    one_copy(a, d, k).wait_send()

    for sub in range(subs):
        lines = slice(sub * rows, (sub + 1) * rows)

        @pl.when(chip < chips - 1)
        def _():
            sum_arrival(chip, sub).wait_recv()
            sum_ref[lines, :] = sum_ref[lines, :] + sums_in[chip, sub].astype(F32)

        @pl.when(chip > 0)
        def _():
            sum_arrival(chips, sub).wait_recv()
            sum_ref[lines, :] = sum_ref[lines, :] + sums_in[chips, sub].astype(F32)

    def finish(i, _):
        other, sub = order(i)
        twin_x_copy(other, sub).wait_send()

        @pl.when(((other >= chip) & (chip > 0)))
        def _():
            x_copy(other, sub, -1).wait_send()

        @pl.when(((other <= chip) & (chip < chips - 1)))
        def _():
            x_copy(other, sub, 1).wait_send()

        @pl.when(other != chip)
        def _():
            sum_copy(other, sub).wait_send()
            p_copy(other, sub).wait_send()

        return 0

    lax.fori_loop(0, units, finish, 0)


def ffn(scale, x, cot_all, gate_weight, up_weight, down_weight):
    tokens, width = cot_all.shape
    rows_dev = x.shape[0]
    chips = lax.axis_size("mp") // 2
    ff = gate_weight.shape[1]
    subs = max(1, rows_dev // BLOCK)
    rows = rows_dev // subs
    units = chips * subs
    narrow = ff // 3
    tall = 512
    down_cols = 256
    quad = lax.axis_size("rows") == 4
    extra_out, row_scratch = (), []
    vmem = pl.BlockSpec(memory_space=pltpu.VMEM)
    hbm = pl.BlockSpec(memory_space=pl.ANY)
    dma = pltpu.SemaphoreType.DMA
    if quad:
        sizes = ((width // 4, ff // 2), (width // 4, ff // 2), (ff // 4, width // 2))
        extra_out = (
            tuple(jax.ShapeDtypeStruct((2, 2, *size), BF16) for size in sizes)
            + tuple(jax.ShapeDtypeStruct((2, *size), BF16) for size in sizes)
            + tuple(jax.ShapeDtypeStruct((size[0], 2 * size[1]), BF16) for size in sizes)
        )
        row_scratch = (
            [pltpu.VMEM((3, *sizes[0]), BF16), pltpu.VMEM((3, *sizes[2]), BF16)]
            + [pltpu.VMEM((2, *size), BF16) for size in sizes]
            + [dma((3, 2, 2)), dma((3, 2, 2)), dma((3, 2)), dma((3, 2)), dma((3,)), dma((2,))]
        )
    out = pl.pallas_call(
        functools.partial(ffn_kernel, subs, quad),
        out_shape=(
            jax.ShapeDtypeStruct((units, rows, width), BF16),
            jax.ShapeDtypeStruct((chips, subs, rows, width), BF16),
            jax.ShapeDtypeStruct((chips, subs, rows, width), BF16),
            jax.ShapeDtypeStruct((rows_dev, width), F32),
            jax.ShapeDtypeStruct((rows_dev, width), F32),
            jax.ShapeDtypeStruct((width, ff), BF16),
            jax.ShapeDtypeStruct((width, ff), BF16),
            jax.ShapeDtypeStruct((ff, width), BF16),
        )
        + extra_out,
        in_specs=[pl.BlockSpec(memory_space=pltpu.SMEM), vmem, hbm, vmem, vmem, vmem],
        out_specs=(hbm, hbm, hbm, vmem, vmem, hbm, hbm, hbm) + (hbm,) * len(extra_out),
        scratch_shapes=[
            pltpu.VMEM((tokens, width), BF16),
            pltpu.VMEM((tokens, ff), BF16),
            pltpu.VMEM((tokens, ff), BF16),
            pltpu.VMEM((tokens, ff), BF16),
            pltpu.VMEM((2, 2 * rows, width), BF16),
            pltpu.VMEM((2, rows, width), BF16),
            pltpu.VMEM((2, 2, rows, width), BF16),
            pltpu.VMEM((2, 2, rows, width), BF16),
            pltpu.VMEM((units, rows, width), BF16),
            pltpu.VMEM((chips + 1, subs, rows, width), BF16),
            pltpu.VMEM((2, tokens, down_cols), BF16),
            pltpu.VMEM((2, ff, down_cols), BF16),
            pltpu.VMEM((2, tall, narrow), BF16),
            dma((2, units)),
            dma((units,)),
            dma((units,)),
            dma((units,)),
            dma((2,)),
            dma((2,)),
            dma((units,)),
            dma((chips + 1, subs)),
            dma((units,)),
            dma((chips, subs)),
            dma((chips, subs)),
            dma((4,)),
            dma((2, 2)),
            dma((2,)),
            dma((2,)),
            dma((2,)),
        ]
        + row_scratch,
        compiler_params=pltpu.CompilerParams(
            collective_id=1, has_side_effects=True, vmem_limit_bytes=VMEM_LIMIT
        ),
        cost_estimate=pl.CostEstimate(
            flops=60_000_000_000, bytes_accessed=60_000_000, transcendentals=2_000_000
        ),
        name="ffn",
    )(scale.reshape(1), x, cot_all, gate_weight, up_weight, down_weight)
    if quad:
        shards = out[14:17]
    else:
        shards = [lax.psum(part, "rows") for part in out[5:8]]
    return (*out[3:5], *shards)


def reduce_kernel(heights, *refs):
    count = len(heights)
    lefts = refs[:count]
    rights = refs[count : 2 * count]
    gains = refs[2 * count]
    outs = refs[2 * count + 1 : 3 * count + 1]
    scratch = refs[3 * count + 1 :]
    per = 17
    chips = lax.axis_size("mp") // 2
    me = lax.axis_index("mp")
    row = lax.axis_index("rows")
    chip = me // 2
    core = me % 2
    down, across = row // 2, row % 2
    twin = (row, me + 1 - 2 * core)
    beside = (row + 1 - 2 * across, me)
    above = ((1 - down) * 2 + across, me)

    barrier = pltpu.get_barrier_semaphore()
    for device in (twin, beside, above):
        pl.semaphore_signal(barrier, inc=1, device_id=device, device_id_type=MESH)
    for step in range(1, chips):
        pl.semaphore_signal(
            barrier,
            inc=1,
            device_id=(row, 2 * ((chip + step) % chips) + core),
            device_id_type=MESH,
        )
    pl.semaphore_wait(barrier, chips + 2)

    streams = []
    for s in range(count):
        streams.append((heights[s], rights[s].shape[1], scratch[s * per : (s + 1) * per]))
    for s in range(count):
        turned = streams[s][2][0]
        turned[...] = lefts[s][...].T

    def target(i):
        return (chip + 1 + i) % chips

    def remote(source, dest, send, recv, device):
        return pltpu.make_async_remote_copy(
            src_ref=source,
            dst_ref=dest,
            send_sem=send,
            recv_sem=recv,
            device_id=device,
            device_id_type=MESH,
        )

    def copies(s, i):
        height, cols, bufs = streams[s]
        (_, own, twin_out, twin_in, out1, in1, out2, in2, out3, in3, s0, r0, s1, r1, s2, r2, s3) = bufs
        goal = target(i)
        return dict(
            twin=lambda: remote(twin_out.at[i], twin_in.at[i], s0.at[i], r0.at[i], twin),
            first=lambda d: remote(
                out1.at[i, d], in1.at[i, d], s1.at[i, d], r1.at[i, d], (beside, above)[d]
            ),
            second=lambda d: remote(
                out2.at[i, d], in2.at[i, d], s2.at[i, d], r2.at[i, d], (above, beside)[d]
            ),
            last=lambda: remote(
                out3.at[i], in3.at[i], s3.at[0, i], s3.at[1, i], (row, 2 * goal + core)
            ),
        )

    def make(s, i):
        height, cols, bufs = streams[s]
        turned, own, twin_out = bufs[:3]
        goal = target(i)
        for r in range(4):
            first = (r * chips + goal) * 2 * height
            lines = pl.ds(pl.multiple_of(first, 16), 2 * height)
            block = dot(turned[lines, :], rights[s][...])
            spare = cols_of(s) - block.shape[1]
            if spare:
                piece = gains[:, pl.ds(pl.multiple_of(first, 128), 2 * height)]
                piece = jnp.concatenate(
                    [piece, jnp.zeros((spare - piece.shape[0], 2 * height), F32)], axis=0
                ).T
                block = jnp.concatenate([block, piece], axis=1)

            @pl.when(core == 0)
            def _():
                own[i, r] = block[:height]
                twin_out[i, r] = block[height:].astype(BF16)

            @pl.when(core == 1)
            def _():
                own[i, r] = block[height:]
                twin_out[i, r] = block[:height].astype(BF16)

        copies(s, i)["twin"]().start()

    def cols_of(s):
        return streams[s][2][1].shape[-1]

    def first_stage(s, i):
        height, cols, bufs = streams[s]
        (_, own, twin_out, twin_in, out1, in1, out2, in2, out3, in3, s0, r0, s1, r1, s2, r2, s3) = bufs
        half = cols_of(s) // 2
        c = copies(s, i)
        c["twin"]().wait_recv()
        for r in range(4):
            own[i, r] = own[i, r] + twin_in[i, r].astype(F32)
        for k in range(2):
            out1[i, 0, k] = own[i, k * 2 + 1 - across, :, :half].astype(BF16)
            out1[i, 1, k] = own[i, (1 - down) * 2 + k, :, half:].astype(BF16)
        for d in range(2):
            c["first"](d).start()

    def second_stage(s, i):
        height, cols, bufs = streams[s]
        (_, own, twin_out, twin_in, out1, in1, out2, in2, out3, in3, s0, r0, s1, r1, s2, r2, s3) = bufs
        half = cols_of(s) // 2
        c = copies(s, i)
        for d in range(2):
            c["first"](d).wait_recv()
        other_down = (1 - down) * 2 + across
        other_across = down * 2 + 1 - across
        out2[i, 0] = (own[i, other_down, :, :half] + in1[i, 0, 1 - down].astype(F32)).astype(BF16)
        out2[i, 1] = (own[i, other_across, :, half:] + in1[i, 1, 1 - across].astype(F32)).astype(BF16)
        for d in range(2):
            c["second"](d).start()

    def third_stage(s, i):
        height, cols, bufs = streams[s]
        (_, own, twin_out, twin_in, out1, in1, out2, in2, out3, in3, s0, r0, s1, r1, s2, r2, s3) = bufs
        half = cols_of(s) // 2
        c = copies(s, i)
        for d in range(2):
            c["second"](d).wait_recv()
        left = own[i, row, :, :half] + in1[i, 0, down].astype(F32) + in2[i, 0].astype(F32)
        right = own[i, row, :, half:] + in1[i, 1, across].astype(F32) + in2[i, 1].astype(F32)

        @pl.when(i < chips - 1)
        def _():
            out3[i, :, :half] = left.astype(BF16)
            out3[i, :, half:] = right.astype(BF16)
            c["last"]().start()

        @pl.when(i == chips - 1)
        def _():
            outs[s][:, :half] = left
            outs[s][:, half:] = right

    def round_step(n, _):
        for stage, work in enumerate((make, first_stage, second_stage, third_stage)):

            @pl.when((n >= stage) & (n < chips + stage))
            def _():
                for s in range(count):
                    work(s, n - stage)

        return 0

    lax.fori_loop(0, chips + 3, round_step, 0)
    for s in range(count):
        in3 = streams[s][2][9]
        for i in range(chips - 1):
            copies(s, i)["last"]().wait_recv()
            outs[s][...] = outs[s][...] + in3[i].astype(F32)

    def finish(i, _):
        for s in range(count):
            c = copies(s, i)
            c["twin"]().wait_send()
            for d in range(2):
                c["first"](d).wait_send()
                c["second"](d).wait_send()

            @pl.when(i < chips - 1)
            def _():
                c["last"]().wait_send()

        return 0

    lax.fori_loop(0, chips, finish, 0)


def reduce_products(pairs, gains):
    chips = lax.axis_size("mp") // 2
    shards = lax.axis_size("rows") * lax.axis_size("mp")
    heights = tuple(left.shape[1] // shards for left, _ in pairs)
    dma = pltpu.SemaphoreType.DMA
    out_shape, scratch = [], []
    for s, (left, right) in enumerate(pairs):
        height = heights[s]
        cols = -(-right.shape[1] // 256) * 256
        half = cols // 2
        out_shape.append(jax.ShapeDtypeStruct((height, cols), F32))
        scratch += [
            pltpu.VMEM((left.shape[1], left.shape[0]), BF16),
            pltpu.VMEM((chips, 4, height, cols), F32),
            pltpu.VMEM((chips, 4, height, cols), BF16),
            pltpu.VMEM((chips, 4, height, cols), BF16),
            pltpu.VMEM((chips, 2, 2, height, half), BF16),
            pltpu.VMEM((chips, 2, 2, height, half), BF16),
            pltpu.VMEM((chips, 2, height, half), BF16),
            pltpu.VMEM((chips, 2, height, half), BF16),
            pltpu.VMEM((chips - 1, height, cols), BF16),
            pltpu.VMEM((chips - 1, height, cols), BF16),
            dma((chips,)),
            dma((chips,)),
            dma((chips, 2)),
            dma((chips, 2)),
            dma((chips, 2)),
            dma((chips, 2)),
            dma((2, chips)),
        ]
    vmem = pl.BlockSpec(memory_space=pltpu.VMEM)
    return pl.pallas_call(
        functools.partial(reduce_kernel, heights),
        out_shape=tuple(out_shape),
        in_specs=[vmem] * (2 * len(pairs) + 1),
        out_specs=(vmem,) * len(pairs),
        scratch_shapes=scratch,
        compiler_params=pltpu.CompilerParams(
            collective_id=2, has_side_effects=True, vmem_limit_bytes=VMEM_LIMIT
        ),
        cost_estimate=pl.CostEstimate(
            flops=50_000_000_000, bytes_accessed=10_000_000, transcendentals=0
        ),
        name="reduce_products",
    )(*[left for left, _ in pairs], *[right for _, right in pairs], gains)


def natural(device, sub, subs):
    if subs == 2:
        return sub * (2 * lax.axis_size("mp") - 1 - 2 * device) + (1 - sub) * 2 * device
    return subs * device + sub


def front_kernel(
    shard_ref,
    x_ref,
    cos_q,
    sin_q,
    cos_kv,
    sin_kv,
    w_out,
    extra_ref,
    xf_ref,
    normed_ref,
    inv_ref,
    q_ref,
    kv_out,
    w_all,
    x_in,
    kv_all,
    swap_send,
    swap_recv,
    z_send,
    z_recv,
    xy_send,
    xy_recv,
    far_send,
    far_recv,
    twin_send,
    twin_recv,
    kz_send,
    kz_recv,
    kt_send,
    kt_recv,
    out_sem,
):
    mp = lax.axis_size("mp")
    chips = mp // 2
    me = lax.axis_index("mp")
    row = lax.axis_index("rows")
    chip = me // 2
    core = me % 2
    down, across = row // 2, row % 2
    subs = x_ref.shape[0] // BLOCK
    height = shard_ref.shape[0]
    half = w_all.shape[1] // 2
    beside_row = row + 1 - 2 * across
    above_row = (1 - down) * 2 + across
    far_row = (1 - down) * 2 + 1 - across
    twin = (row, me + 1 - 2 * core)
    beside = (beside_row, me)
    above = (above_row, me)
    mirror = (row, mp - 1 - me)

    barrier = pltpu.get_barrier_semaphore()
    for device in (twin, beside, above, mirror):
        pl.semaphore_signal(barrier, inc=1, device_id=device, device_id_type=MESH)

    @pl.when(chip < chips - 1)
    def _():
        pl.semaphore_signal(barrier, inc=1, device_id=(row, me + 2), device_id_type=MESH)

    @pl.when(chip > 0)
    def _():
        pl.semaphore_signal(barrier, inc=1, device_id=(row, me - 2), device_id_type=MESH)

    ends = jnp.where(chip < chips - 1, 1, 0) + jnp.where(chip > 0, 1, 0)
    pl.semaphore_wait(barrier, 4 + ends)

    def remote(source, dest, send, recv, device):
        return pltpu.make_async_remote_copy(
            src_ref=source,
            dst_ref=dest,
            send_sem=send,
            recv_sem=recv,
            device_id=device,
            device_id_type=MESH,
        )

    def spot(r, k, side=None):
        lines = pl.ds(pl.multiple_of((r * mp + 2 * k + core) * height, height), height)
        if side is None:
            return w_all.at[lines]
        return w_all.at[lines, pl.ds(side * half, half)]

    def z_copy(k, side):
        return remote(
            spot(row, k),
            spot(row, k),
            z_send.at[(side + 1) // 2, k],
            z_recv.at[k],
            (row, me + 2 * side),
        )

    def near_copy(k, d):
        return remote(
            spot(row, k), spot(row, k), xy_send.at[d, k], xy_recv.at[d, k], (beside, above)[d]
        )

    def near_row(d):
        return (beside_row, above_row)[d]

    def far_copy(k, d):
        place = spot(near_row(d), k, d)
        return remote(place, place, far_send.at[d, k], far_recv.at[d, k], (above, beside)[d])

    def twin_copy(k, kind):
        if kind < 3:
            place = spot((row, beside_row, above_row)[kind], k)
        else:
            place = spot(far_row, k, kind - 3)
        return remote(place, place, twin_send.at[kind, k], twin_recv.at[kind, k], twin)

    def order(i):
        near = jnp.minimum(chip, chips - 1 - chip)
        long_side = jnp.where(chip < chips - 1 - chip, 1, -1)
        paired = i <= 2 * near
        dist = jnp.where(paired, (i + 1) // 2, i - near)
        side = jnp.where(paired, 2 * (i % 2) - 1, long_side)
        return chip + side * dist

    if subs == 2:
        swap = remote(x_ref.at[pl.ds(BLOCK, BLOCK)], x_in, swap_send, swap_recv, mirror)
        swap.start()
    own_lines = pl.ds(pl.multiple_of((row * mp + me) * height, height), height)
    w_all[own_lines, :] = shard_ref[...]

    def gather_step(n, _):
        @pl.when(n < chips)
        def _():
            k = order(n)

            @pl.when(n > 0)
            def _():
                z_copy(k, 1).wait_recv()

            for d in range(2):
                near_copy(k, d).start()

            @pl.when((k >= chip) & (chip > 0))
            def _():
                z_copy(k, -1).start()

            @pl.when((k <= chip) & (chip < chips - 1))
            def _():
                z_copy(k, 1).start()

            twin_copy(k, 0).start()

        @pl.when((n >= 1) & (n < chips + 1))
        def _():
            k = order(n - 1)
            for d in range(2):
                near_copy(k, d).wait_recv()
                far_copy(k, d).start()
                twin_copy(k, 1 + d).start()

        @pl.when(n >= 2)
        def _():
            k = order(n - 2)
            for d in range(2):
                far_copy(k, d).wait_recv()
                twin_copy(k, 3 + d).start()

        return 0

    lax.fori_loop(0, chips + 2, gather_step, 0)

    xf_ref[:BLOCK, :] = x_ref[:BLOCK, :]
    if subs == 2:
        swap.wait_recv()
        xf_ref[BLOCK:, :] = x_in[...]

    def drain_step(k, _):
        for kind in range(5):
            twin_copy(k, kind).wait_recv()
        return 0

    lax.fori_loop(0, chips, drain_step, 0)
    save = pltpu.make_async_copy(w_all, w_out, out_sem)
    save.start()
    cols = Q_WIDTH + 2 * KV_WIDTH
    extra = w_all[:, cols:].astype(F32).T[:8, :]
    extra_ref[...] = extra
    x = xf_ref[...].astype(F32)
    inverse = lax.rsqrt(jnp.mean(x * x, axis=-1, keepdims=True) + EPS)
    inv_ref[...] = inverse
    normed_ref[...] = (x * inverse * extra[0:1, :]).astype(BF16)

    def place_of(device, sub):
        first = natural(device, sub, subs) * BLOCK
        return kv_all.at[pl.ds(pl.multiple_of(first, BLOCK), BLOCK)]

    part = dot(normed_ref[...], w_all[:, Q_WIDTH:cols])
    for g in range(KV_HEADS):
        slab = part[:, g * SLAB : (g + 1) * SLAB]
        turned = (slab * cos_kv[...] + swap_halves(slab) * sin_kv[...]).astype(BF16)
        for sub in range(subs):
            place_of(me, sub)[:, g * SLAB : (g + 1) * SLAB] = turned[
                sub * BLOCK : (sub + 1) * BLOCK, :
            ]

    def kz_copy(k, sub, side):
        place = place_of(2 * k + core, sub)
        return remote(
            place,
            place,
            kz_send.at[(side + 1) // 2, k * subs + sub],
            kz_recv.at[k * subs + sub],
            (row, me + 2 * side),
        )

    def kt_copy(k, sub):
        place = place_of(2 * k + core, sub)
        return remote(
            place, place, kt_send.at[k * subs + sub], kt_recv.at[k * subs + sub], twin
        )

    def spread(n, _):
        k = order(n)
        for sub in range(subs):

            @pl.when(n > 0)
            def _():
                kz_copy(k, sub, 1).wait_recv()

            @pl.when((k >= chip) & (chip > 0))
            def _():
                kz_copy(k, sub, -1).start()

            @pl.when((k <= chip) & (chip < chips - 1))
            def _():
                kz_copy(k, sub, 1).start()

            kt_copy(k, sub).start()

        return 0

    spread(0, 0)
    for s in range(Q_WIDTH // 256):
        part = dot(normed_ref[...], w_all[:, s * 256 : (s + 1) * 256])
        for t in range(2):
            slab = part[:, t * SLAB : (t + 1) * SLAB]
            col = s * 256 + t * SLAB
            turned = slab * cos_q[...] + swap_halves(slab) * sin_q[...]
            q_ref[:, col : col + SLAB] = (
                turned.astype(BF16).astype(F32) * HEAD_DIM ** (-0.5)
            ).astype(BF16)
    lax.fori_loop(1, chips, spread, 0)

    def finish(k, _):
        for sub in range(subs):
            kt_copy(k, sub).wait_recv()
            kt_copy(k, sub).wait_send()
        for kind in range(5):
            twin_copy(k, kind).wait_send()
        for d in range(2):
            near_copy(k, d).wait_send()
            far_copy(k, d).wait_send()

        @pl.when((k >= chip) & (chip > 0))
        def _():
            z_copy(k, -1).wait_send()
            for sub in range(subs):
                kz_copy(k, sub, -1).wait_send()

        @pl.when((k <= chip) & (chip < chips - 1))
        def _():
            z_copy(k, 1).wait_send()
            for sub in range(subs):
                kz_copy(k, sub, 1).wait_send()

        return 0

    lax.fori_loop(0, chips, finish, 0)
    if subs == 2:
        swap.wait_send()
    kv_out[...] = kv_all[...]
    save.wait()


def front(shard, x, tables):
    rows, width = x.shape
    subs = rows // BLOCK
    chips = lax.axis_size("mp") // 2
    cols = shard.shape[1]
    total = shard.shape[0] * lax.axis_size("rows") * lax.axis_size("mp")
    vmem = pl.BlockSpec(memory_space=pltpu.VMEM)
    hbm = pl.BlockSpec(memory_space=pl.ANY)
    dma = pltpu.SemaphoreType.DMA
    return pl.pallas_call(
        front_kernel,
        out_shape=(
            jax.ShapeDtypeStruct((total, cols), BF16),
            jax.ShapeDtypeStruct((8, total), F32),
            jax.ShapeDtypeStruct((rows, width), BF16),
            jax.ShapeDtypeStruct((rows, width), BF16),
            jax.ShapeDtypeStruct((rows, 1), F32),
            jax.ShapeDtypeStruct((rows, Q_WIDTH), BF16),
            jax.ShapeDtypeStruct((LEN, 2 * KV_WIDTH), BF16),
        ),
        in_specs=[vmem] * 6,
        out_specs=(hbm,) + (vmem,) * 6,
        scratch_shapes=[
            pltpu.VMEM((total, cols), BF16),
            pltpu.VMEM((BLOCK, width), BF16),
            pltpu.VMEM((LEN, 2 * KV_WIDTH), BF16),
            dma,
            dma,
            dma((2, chips)),
            dma((chips,)),
            dma((2, chips)),
            dma((2, chips)),
            dma((2, chips)),
            dma((2, chips)),
            dma((5, chips)),
            dma((5, chips)),
            dma((2, chips * subs)),
            dma((chips * subs,)),
            dma((chips * subs,)),
            dma((chips * subs,)),
            dma,
        ],
        compiler_params=pltpu.CompilerParams(
            collective_id=4, has_side_effects=True, vmem_limit_bytes=VMEM_LIMIT
        ),
        cost_estimate=pl.CostEstimate(
            flops=30_000_000_000, bytes_accessed=12_000_000, transcendentals=0
        ),
        name="front",
    )(shard, x, *tables)


def on_device(
    inputs,
    cotangent,
    corpus_ids,
    corpus_weight,
    attn_gain,
    qkv_weight,
    out_weight,
    ffn_gain,
    gate_weight,
    up_weight,
    down_weight,
):
    both = ("rows", "mp")
    rows_dev, width = inputs.shape
    mp = lax.axis_size("mp")
    me = lax.axis_index("mp")
    row_groups = lax.axis_size("rows")
    corpora = corpus_weight.shape[0]
    subs = rows_dev // BLOCK
    folded = subs == 2
    mirror = [(i, mp - 1 - i) for i in range(mp)]

    def fold(rows):
        if not folded:
            return rows
        return jnp.concatenate(
            [rows[:BLOCK], lax.ppermute(rows[BLOCK:], "mp", mirror)], axis=0
        )

    def to_order(gathered):
        if not folded:
            return gathered
        parts = gathered.reshape(mp, 2, BLOCK, gathered.shape[-1])
        return jnp.stack([parts[:, 0], parts[::-1, 1]], axis=1).reshape(gathered.shape)

    if folded:
        blocks = jnp.stack([2 * me, 2 * mp - 1 - 2 * me]).astype(jnp.int32)
    else:
        blocks = (subs * me + jnp.arange(subs)).astype(jnp.int32)
    positions = (blocks[:, None] * BLOCK + jnp.arange(BLOCK)[None, :]).reshape(-1)

    shard_rows = qkv_weight.shape[0]
    ident = jnp.broadcast_to(corpus_ids.astype(BF16)[:1, None], (shard_rows, 1))
    spare = (-(Q_WIDTH + 2 * KV_WIDTH + 3)) % 128
    shard = jnp.concatenate(
        [
            pack_kv(qkv_weight),
            attn_gain[:, None],
            ffn_gain[:, None],
            ident,
            jnp.zeros((shard_rows, spare), BF16),
        ],
        axis=1,
    )
    qkv_cols = Q_WIDTH + 2 * KV_WIDTH
    cot_all = lax.all_gather(cotangent, "mp", axis=0, tiled=True)
    out_full = lax.all_gather(out_weight, both, axis=0, tiled=True)
    tables = rope_tables(positions)
    if row_groups == 4:
        qkv_ext, extras, x, normed_one, inverse_one, q, kv_all = front(shard, inputs, tables)
        qkv_full = qkv_ext[:, :qkv_cols]
    else:
        qkv_ext = lax.all_gather(shard, both, axis=0, tiled=True)
        qkv_full = qkv_ext[:, :qkv_cols]
        extras = qkv_ext[:, qkv_cols:].astype(F32).T
        x = fold(inputs)
        normed_one, inverse_one, q, kv = qkv_project(x, extras[0:1], qkv_full, tables)
        kv_all = to_order(lax.all_gather(kv, "mp", axis=0, tiled=True))
    gain_one, gain_two = extras[0:1], extras[1:2]
    all_ids = extras[2].reshape(row_groups, -1)[:, 0]
    my_id = corpus_ids[0].astype(F32)
    count = jnp.sum((all_ids == my_id).astype(F32))
    weight_seq = jnp.sum(
        jnp.where(jnp.arange(corpora) == corpus_ids[0], corpus_weight, 0.0)
    )
    seq_scale = weight_seq * row_groups / (corpora * count)
    o, totals = attend(blocks, q, kv_all)

    residual = x.astype(F32)
    middle = residual + dot(o, out_full)
    inverse_two = lax.rsqrt(jnp.mean(middle * middle, axis=-1, keepdims=True) + EPS)
    normed_two = (middle * inverse_two * gain_two).astype(BF16)
    ffn_sum, grad_normed_two, gate_grad, up_grad, down_grad = ffn(
        seq_scale, normed_two, cot_all, gate_weight, up_weight, down_weight
    )
    outputs = fold((middle + ffn_sum).astype(BF16))

    cot = jnp.concatenate(
        [
            lax.dynamic_slice(cot_all, (blocks[sub] * BLOCK, 0), (BLOCK, width))
            for sub in range(subs)
        ],
        axis=0,
    )
    grad_out = cot.astype(F32) * seq_scale
    scaled_two = grad_normed_two * gain_two
    ffn_gain_part = jnp.sum(grad_normed_two * middle * inverse_two, axis=0)
    grad_middle = (
        grad_out
        + inverse_two * scaled_two
        - middle * inverse_two**3 * jnp.mean(scaled_two * middle, axis=-1, keepdims=True)
    )
    grad_middle_low = grad_middle.astype(BF16)
    if row_groups == 4:
        gate_grad, up_grad, down_grad, grad_middle_low = lax.optimization_barrier(
            (gate_grad, up_grad, down_grad, grad_middle_low)
        )
        gate_grad, up_grad, down_grad = (
            lax.all_gather(g, "rows", axis=0, tiled=True)
            for g in (gate_grad, up_grad, down_grad)
        )
    grad_o = dot_nt(grad_middle_low, out_full).astype(BF16)
    grad_qkv = attend_back(q, kv_all, o, grad_o, totals, tables)
    grad_normed_one = dot_nt(grad_qkv, qkv_full)
    scaled_one = grad_normed_one * gain_one
    attn_gain_part = jnp.sum(grad_normed_one * residual * inverse_one, axis=0)
    input_grad = (
        grad_middle
        + inverse_one * scaled_one
        - residual * inverse_one**3 * jnp.mean(scaled_one * residual, axis=-1, keepdims=True)
    )
    if folded:
        input_grad = jnp.concatenate(
            [
                input_grad[:BLOCK],
                lax.ppermute(input_grad[BLOCK:].astype(BF16), "mp", mirror).astype(F32),
            ],
            axis=0,
        )
    gain_parts = jnp.concatenate(
        [attn_gain_part[None], ffn_gain_part[None], jnp.zeros((6, width), F32)], axis=0
    )
    if row_groups == 4:
        part, proj_grad = reduce_products(
            ((normed_one, grad_qkv), (o, grad_middle_low)), gain_parts
        )
    else:
        part = jnp.concatenate(
            [dot_tn(normed_one, grad_qkv), gain_parts.T, jnp.zeros((width, 120), F32)], axis=1
        )
        part, proj_grad = (
            lax.psum_scatter(p.astype(BF16), both, scatter_dimension=0, tiled=True).astype(F32)
            for p in (part, dot_tn(o, grad_middle_low))
        )
    qkv_grad = unpack_kv(part[:, :qkv_cols])
    attn_gain_grad = part[:, qkv_cols]
    ffn_gain_grad = part[:, qkv_cols + 1]
    gate_grad, up_grad, down_grad, part = lax.optimization_barrier(
        (gate_grad, up_grad, down_grad, part)
    )
    gate_grad, up_grad, down_grad = (g.astype(F32) for g in (gate_grad, up_grad, down_grad))
    qkv_grad = unpack_kv(part[:, :qkv_cols])
    attn_gain_grad = part[:, qkv_cols]
    ffn_gain_grad = part[:, qkv_cols + 1]
    return (
        outputs,
        input_grad,
        qkv_grad,
        proj_grad,
        gate_grad,
        up_grad,
        down_grad,
        attn_gain_grad,
        ffn_gain_grad,
    )


def solution(mesh):
    split = P(("rows", "mp"), None)
    line = P(("rows", "mp"))
    in_specs = (
        split,
        split,
        P("rows"),
        P(),
        line,
        split,
        split,
        line,
        P(None, "mp"),
        P(None, "mp"),
        P("mp", None),
    )
    out_specs = (
        split,
        split,
        split,
        split,
        P(None, "mp"),
        P(None, "mp"),
        P("mp", None),
        line,
        line,
    )
    return jax.shard_map(
        on_device, mesh=mesh, in_specs=in_specs, out_specs=out_specs, check_vma=False
    )
```

```python
import functools

import jax
import jax.numpy as jnp
from jax import lax
from jax.experimental import pallas as pl
from jax.experimental.pallas import tpu as pltpu
from jax.sharding import PartitionSpec as P

HEADS = 20
KV_HEADS = 5
HEAD_DIM = 64
GROUP = HEADS // KV_HEADS
Q_WIDTH = HEADS * HEAD_DIM
KV_WIDTH = KV_HEADS * HEAD_DIM
LEN = 2048
BLOCK = 128
KTILE = 256
EPS = 1e-05
THETA = 10000.0
LANES = GROUP * BLOCK
SLAB = 2 * HEAD_DIM

MESH = pl.DeviceIdType.MESH
F32 = jnp.float32
BF16 = jnp.bfloat16
VMEM_LIMIT = 62 * 1024 * 1024


def rope_tables(positions):
    half_dim = HEAD_DIM // 2
    freqs = jnp.exp(-jnp.log(THETA) * (2.0 * jnp.arange(half_dim, dtype=F32)) / HEAD_DIM)
    angles = positions.astype(F32)[:, None] * freqs[None, :]
    cosine, sine = jnp.cos(angles), jnp.sin(angles)
    ones, zeros = jnp.ones_like(cosine), jnp.zeros_like(cosine)
    head_cos = jnp.concatenate([cosine, cosine], axis=1)
    head_sin = jnp.concatenate([-sine, sine], axis=1)
    cos_q = jnp.concatenate([head_cos, head_cos], axis=1)
    sin_q = jnp.concatenate([head_sin, head_sin], axis=1)
    cos_kv = jnp.concatenate([head_cos, ones, ones], axis=1)
    sin_kv = jnp.concatenate([head_sin, zeros, zeros], axis=1)
    return (cos_q, sin_q, cos_kv, sin_kv)


def swap_halves(slab):
    lane = lax.broadcasted_iota(jnp.int32, slab.shape, 1)
    half_dim = HEAD_DIM // 2
    up = pltpu.roll(slab, SLAB - half_dim, 1)
    down = pltpu.roll(slab, half_dim, 1)
    return jnp.where(lane % HEAD_DIM < half_dim, up, down)


def qkv_kernel(x_ref, gain_ref, w_ref, cos_q, sin_q, cos_kv, sin_kv, normed_ref, inv_ref, q_ref, kv_ref):
    x = x_ref[...].astype(F32)
    inverse = lax.rsqrt(jnp.mean(x * x, axis=-1, keepdims=True) + EPS)
    normed = (x * inverse * gain_ref[...]).astype(BF16)
    normed_ref[...] = normed
    inv_ref[...] = inverse
    for s in range(Q_WIDTH // 256):
        part = jnp.dot(normed, w_ref[:, s * 256 : (s + 1) * 256], preferred_element_type=F32)
        for t in range(2):
            slab = part[:, t * SLAB : (t + 1) * SLAB]
            col = s * 256 + t * SLAB
            turned = slab * cos_q[...] + swap_halves(slab) * sin_q[...]
            q_ref[:, col : col + SLAB] = (turned.astype(BF16).astype(F32) * HEAD_DIM ** (-0.5)).astype(BF16)
    part = jnp.dot(normed, w_ref[:, Q_WIDTH : Q_WIDTH + 2 * KV_WIDTH], preferred_element_type=F32)
    for g in range(KV_HEADS):
        slab = part[:, g * SLAB : (g + 1) * SLAB]
        turned = slab * cos_kv[...] + swap_halves(slab) * sin_kv[...]
        kv_ref[:, g * SLAB : (g + 1) * SLAB] = turned.astype(BF16)


def qkv_project(x, gain, weight, tables):
    rows, width = x.shape
    return pl.pallas_call(
        qkv_kernel,
        out_shape=(
            jax.ShapeDtypeStruct((rows, width), BF16),
            jax.ShapeDtypeStruct((rows, 1), F32),
            jax.ShapeDtypeStruct((rows, Q_WIDTH), BF16),
            jax.ShapeDtypeStruct((rows, 2 * KV_WIDTH), BF16),
        ),
        compiler_params=pltpu.CompilerParams(vmem_limit_bytes=VMEM_LIMIT),
        name="qkv_project",
    )(x, gain, weight, *tables)


def heads_to_lanes(rows_part):
    turned = rows_part.T
    return jnp.concatenate(
        [turned[h * HEAD_DIM : (h + 1) * HEAD_DIM, :] for h in range(GROUP)], axis=1
    )


def lanes_to_heads(lanes_part):
    stacked = jnp.concatenate(
        [lanes_part[:, h * BLOCK : (h + 1) * BLOCK] for h in range(GROUP)], axis=0
    )
    return stacked.T


def causal(tile, block):
    key_pos = tile * KTILE + lax.broadcasted_iota(jnp.int32, (KTILE, LANES), 0)
    query_pos = block * BLOCK + lax.broadcasted_iota(jnp.int32, (KTILE, LANES), 1) % BLOCK
    return key_pos <= query_pos


def over_rows(left, right):
    return lax.dot_general(left, right, (((0,), (0,)), ((), ())), preferred_element_type=F32)


def attend_kernel(block_ref, q_ref, kv_ref, o_ref, total_ref):
    subs = q_ref.shape[0] // BLOCK
    for sub in range(subs):
        block = block_ref[sub]
        queries = heads_to_lanes(q_ref[sub * BLOCK : (sub + 1) * BLOCK, :].astype(F32))
        queries = jnp.concatenate([queries, jnp.zeros_like(queries)], axis=0).astype(BF16)

        def step(tile, carry, masked):
            top, total, acc = carry
            kv = kv_ref[pl.ds(pl.multiple_of(tile * KTILE, KTILE), KTILE), :]
            scores = jnp.dot(kv, queries, preferred_element_type=F32)
            if masked:
                scores = jnp.where(causal(tile, block), scores, -1e30)
            new_top = jnp.maximum(top, jnp.max(scores, axis=0, keepdims=True))
            decay = jnp.exp(top - new_top)
            probs = jnp.exp(scores - new_top)
            total = decay * total + jnp.sum(probs, axis=0, keepdims=True)
            acc = decay * acc + over_rows(kv, probs.astype(BF16))
            return (new_top, total, acc)

        start = (
            jnp.full((1, LANES), -1e30, F32),
            jnp.zeros((1, LANES), F32),
            jnp.zeros((SLAB, LANES), F32),
        )
        full = block * BLOCK // KTILE
        carry = lax.fori_loop(0, full, lambda t, c: step(t, c, False), start)
        top, total, acc = step(full, carry, True)
        out = acc[HEAD_DIM:, :] / total
        o_ref[sub * BLOCK : (sub + 1) * BLOCK, :] = lanes_to_heads(out).astype(BF16)
        total_ref[sub : sub + 1, :] = top + jnp.log(total)


def attend(blocks, q, kv_all):
    rows = q.shape[0]
    subs = rows // BLOCK
    return pl.pallas_call(
        attend_kernel,
        grid_spec=pltpu.PrefetchScalarGridSpec(
            num_scalar_prefetch=1,
            grid=(KV_HEADS,),
            in_specs=[
                pl.BlockSpec((rows, GROUP * HEAD_DIM), lambda g, b: (0, g)),
                pl.BlockSpec((LEN, SLAB), lambda g, b: (0, g)),
            ],
            out_specs=[
                pl.BlockSpec((rows, GROUP * HEAD_DIM), lambda g, b: (0, g)),
                pl.BlockSpec((None, subs, LANES), lambda g, b: (g, 0, 0)),
            ],
        ),
        out_shape=(
            jax.ShapeDtypeStruct((rows, Q_WIDTH), BF16),
            jax.ShapeDtypeStruct((KV_HEADS, subs, LANES), F32),
        ),
        compiler_params=pltpu.CompilerParams(vmem_limit_bytes=VMEM_LIMIT),
        cost_estimate=pl.CostEstimate(
            flops=60_000_000_000, bytes_accessed=8_000_000, transcendentals=6_000_000
        ),
        name="attend",
    )(blocks, q, kv_all)


def attend_back_kernel(height, *refs):
    if height:
        low_ref, grad_ref, proj_ref = refs[9:12]
        attend_back_body(refs[:9], grad_ref, refs[12:23], (height, low_ref, proj_ref, refs[23:]))
    else:
        attend_back_body(refs[:9], refs[9], refs[10:], None)


def attend_back_body(inputs, grad_ref, scratch, product):
    q_ref, kv_ref, o_ref, do_ref, total_ref, cos_q, sin_q, cos_kv, sin_kv = inputs
    (dkv_acc, own_part, twin_out, twin_in, sum_out, sum_in, mine) = scratch[:7]
    (twin_send, twin_recv, sum_send, sum_recv) = scratch[7:]
    subs = q_ref.shape[0] // BLOCK
    chips = lax.axis_size("mp") // 2
    me = lax.axis_index("mp")
    row = lax.axis_index("rows")
    chip = me // 2
    core = me % 2
    twin = (row, me + 1 - 2 * core)
    width = GROUP * HEAD_DIM

    barrier = pltpu.get_barrier_semaphore()
    pl.semaphore_signal(barrier, inc=1, device_id=twin, device_id_type=MESH)
    for step in range(1, chips):
        pl.semaphore_signal(
            barrier,
            inc=1,
            device_id=(row, 2 * ((chip + step) % chips) + core),
            device_id_type=MESH,
        )
    if product:
        down, across = row // 2, row % 2
        for device in ((row + 1 - 2 * across, me), ((1 - down) * 2 + across, me)):
            pl.semaphore_signal(barrier, inc=1, device_id=device, device_id_type=MESH)
    pl.semaphore_wait(barrier, chips + 2 if product else chips)
    if product:
        reducer = Reducer(product[0], o_ref, product[1], None, product[2], product[3])

    def twin_copy(g):
        return pltpu.make_async_remote_copy(
            src_ref=twin_out.at[g % 2],
            dst_ref=twin_in.at[g],
            send_sem=twin_send.at[g % 2],
            recv_sem=twin_recv.at[g],
            device_id=twin,
            device_id_type=MESH,
        )

    def sum_copy(g, step):
        return pltpu.make_async_remote_copy(
            src_ref=sum_out.at[g, step - 1],
            dst_ref=sum_in.at[g, step - 1],
            send_sem=sum_send.at[g, step - 1],
            recv_sem=sum_recv.at[g, step - 1],
            device_id=(row, 2 * ((chip + step) % chips) + core),
            device_id_type=MESH,
        )

    def combine(g):
        twin_copy(g).wait_recv()
        for step in range(1, chips):
            goal = (chip + step) % chips
            sum_out[g, step - 1] = (
                own_part[g % 2, goal] + twin_in[g, goal].astype(F32)
            ).astype(BF16)
            sum_copy(g, step).start()
        mine[g] = own_part[g % 2, chip] + twin_in[g, chip].astype(F32)

    def head_step(g, _):
        if product:
            reducer.round(g)
        cols = pl.ds(pl.multiple_of(g * width, width), width)
        pair = pl.ds(pl.multiple_of(g * SLAB, SLAB), SLAB)
        dkv_acc[...] = jnp.zeros_like(dkv_acc)
        for sub in range(subs):
            rows = slice(sub * BLOCK, (sub + 1) * BLOCK)
            block = natural(me, sub, subs)
            queries = heads_to_lanes(q_ref[rows, cols].astype(F32))
            grads = heads_to_lanes(do_ref[rows, cols].astype(F32))
            outs = heads_to_lanes(o_ref[rows, cols].astype(F32))
            delta = jnp.sum(grads * outs, axis=0, keepdims=True)
            empty = jnp.zeros_like(queries)
            queries = jnp.concatenate([queries, empty], axis=0)
            grads = jnp.concatenate([empty, grads], axis=0)
            query_rows = queries.T.astype(BF16)
            grad_rows = grads.T.astype(BF16)
            queries = queries.astype(BF16)
            grads = grads.astype(BF16)
            log_total = total_ref[g, sub : sub + 1, :]

            def step(tile, dq, masked):
                keys = pl.ds(pl.multiple_of(tile * KTILE, KTILE), KTILE)
                kv = kv_ref[keys, pair]
                scores = jnp.dot(kv, queries, preferred_element_type=F32)
                probs = jnp.exp(scores - log_total)
                if masked:
                    probs = jnp.where(causal(tile, block), probs, 0.0)
                grad_probs = jnp.dot(kv, grads, preferred_element_type=F32)
                grad_scores = (probs * (grad_probs - delta)).astype(BF16)
                dkv_acc[keys, :] += jnp.dot(
                    grad_scores, query_rows, preferred_element_type=F32
                ) + jnp.dot(probs.astype(BF16), grad_rows, preferred_element_type=F32)
                return dq + over_rows(kv, grad_scores)

            full = block * BLOCK // KTILE
            dq = lax.fori_loop(
                0, full, lambda t, c: step(t, c, False), jnp.zeros((SLAB, LANES), F32)
            )
            dq = step(full, dq, True)
            dq = lanes_to_heads(dq[:HEAD_DIM, :]) * HEAD_DIM ** (-0.5)
            for t in range(width // SLAB):
                slab = dq[:, t * SLAB : (t + 1) * SLAB]
                turned = slab * cos_q[rows, :] - swap_halves(slab) * sin_q[rows, :]
                first = pl.multiple_of(g * width + t * SLAB, SLAB)
                grad_ref[rows, pl.ds(first, SLAB)] = turned.astype(BF16)

        @pl.when(g >= 2)
        def _():
            twin_copy(g - 2).wait_send()

        for goal in range(chips):
            for sub in range(subs):
                first = natural(2 * goal + core, sub, subs) * BLOCK
                own_part[g % 2, goal, sub] = dkv_acc[pl.ds(pl.multiple_of(first, BLOCK), BLOCK), :]
                first = natural(2 * goal + 1 - core, sub, subs) * BLOCK
                twin_out[g % 2, goal, sub] = dkv_acc[
                    pl.ds(pl.multiple_of(first, BLOCK), BLOCK), :
                ].astype(BF16)
        twin_copy(g).start()

        @pl.when(g >= 1)
        def _():
            combine(g - 1)

        return 0

    lax.fori_loop(0, KV_HEADS, head_step, 0)
    combine(KV_HEADS - 1)
    if product:
        lax.fori_loop(KV_HEADS, chips + 3, reducer.round, 0)

    for g in range(KV_HEADS):
        total = mine[g]
        for step in range(1, chips):
            sum_copy(g, step).wait_recv()
            total = total + sum_in[g, step - 1].astype(F32)
        slab = total.reshape(subs * BLOCK, SLAB)
        turned = slab * cos_kv[...] - swap_halves(slab) * sin_kv[...]
        first = Q_WIDTH + g * SLAB
        grad_ref[:, first : first + SLAB] = turned.astype(BF16)
    for g in range(KV_HEADS):
        for step in range(1, chips):
            sum_copy(g, step).wait_send()
    for g in range(KV_HEADS - 2, KV_HEADS):
        twin_copy(g).wait_send()
    if product:
        reducer.close()


def attend_back(q, kv_all, o, grad_o, totals, tables, low):
    rows = q.shape[0]
    subs = rows // BLOCK
    chips = lax.axis_size("mp") // 2
    vmem = pl.BlockSpec(memory_space=pltpu.VMEM)
    dma = pltpu.SemaphoreType.DMA
    part = (chips, subs, BLOCK, SLAB)
    args = (q, kv_all, o, grad_o, totals, *tables)
    out_shape = (jax.ShapeDtypeStruct((rows, Q_WIDTH + 2 * KV_WIDTH), BF16),)
    height, more = 0, []
    if lax.axis_size("rows") == 4:
        height, product, more = reducer_buffers(o, low)
        args += (low,)
        out_shape += (product,)
    return pl.pallas_call(
        functools.partial(attend_back_kernel, height),
        in_specs=[vmem] * len(args),
        out_specs=(vmem,) * len(out_shape),
        out_shape=out_shape,
        scratch_shapes=[
            pltpu.VMEM((LEN, SLAB), F32),
            pltpu.VMEM((2,) + part, F32),
            pltpu.VMEM((2,) + part, BF16),
            pltpu.VMEM((KV_HEADS,) + part, BF16),
            pltpu.VMEM((KV_HEADS, chips - 1) + part[1:], BF16),
            pltpu.VMEM((KV_HEADS, chips - 1) + part[1:], BF16),
            pltpu.VMEM((KV_HEADS,) + part[1:], F32),
            dma((2,)),
            dma((KV_HEADS,)),
            dma((KV_HEADS, chips - 1)),
            dma((KV_HEADS, chips - 1)),
        ]
        + more,
        compiler_params=pltpu.CompilerParams(
            collective_id=3, has_side_effects=True, vmem_limit_bytes=VMEM_LIMIT
        ),
        cost_estimate=pl.CostEstimate(
            flops=120_000_000_000, bytes_accessed=12_000_000, transcendentals=6_000_000
        ),
        name="attend_back",
    )(*args)


def pack_kv(columns):
    lead = columns.shape[:-1]
    kv = columns[..., Q_WIDTH:].reshape(*lead, 2, KV_HEADS, HEAD_DIM)
    kv = jnp.swapaxes(kv, -3, -2).reshape(*lead, 2 * KV_WIDTH)
    return jnp.concatenate([columns[..., :Q_WIDTH], kv], axis=-1)


def unpack_kv(columns):
    lead = columns.shape[:-1]
    kv = columns[..., Q_WIDTH:].reshape(*lead, KV_HEADS, 2, HEAD_DIM)
    kv = jnp.swapaxes(kv, -3, -2).reshape(*lead, 2 * KV_WIDTH)
    return jnp.concatenate([columns[..., :Q_WIDTH], kv], axis=-1)


def dot(left, right):
    return jnp.dot(left, right, preferred_element_type=F32)


def dot_nt(left, right):
    return lax.dot_general(left, right, (((1,), (1,)), ((), ())), preferred_element_type=F32)


def dot_tn(left, right):
    return lax.dot_general(left, right, (((0,), (0,)), ((), ())), preferred_element_type=F32)


def half_of(ref, chip, core, sub, rows):
    subs = ref.shape[0] // (rows * lax.axis_size("mp"))
    start = natural(2 * chip + core, sub, subs) * rows
    return ref.at[pl.ds(pl.multiple_of(start, rows), rows)]


def part_of(ref, chip, core, sub, rows):
    subs = ref.shape[0] // (rows * lax.axis_size("mp"))
    start = (subs * (2 * chip + core) + sub) * rows
    return ref.at[pl.ds(pl.multiple_of(start, rows), rows)]


def ffn_kernel(
    subs,
    quad,
    scale_ref,
    x_ref,
    cot_ref,
    gate_ref,
    up_ref,
    down_ref,
    part_ref,
    part_in,
    relay_in,
    part_sum,
    sum_ref,
    gate_out,
    up_out,
    down_out,
    *rest,
):
    slots = rest[:9] if quad else ()
    scratch = rest[9:] if quad else rest
    ffn_body(
        subs,
        quad,
        slots,
        scale_ref,
        x_ref,
        cot_ref,
        gate_ref,
        up_ref,
        down_ref,
        part_ref,
        part_in,
        relay_in,
        part_sum,
        sum_ref,
        gate_out,
        up_out,
        down_out,
        *scratch,
    )


def ffn_body(
    subs,
    quad,
    slots,
    scale_ref,
    x_ref,
    cot_ref,
    gate_ref,
    up_ref,
    down_ref,
    part_ref,
    part_in,
    relay_in,
    part_sum,
    sum_ref,
    gate_out,
    up_out,
    down_out,
    x_all,
    hid,
    dgate,
    dup,
    cot_buf,
    part_own,
    twin_buf,
    twin_in,
    send_buf,
    sums_in,
    cot_cols,
    wide_buf,
    tall_buf,
    x_send,
    x_recv,
    twin_x_send,
    twin_x_recv,
    twin_send,
    twin_recv,
    sum_send,
    sum_recv,
    p_send,
    p_recv,
    relay_recv,
    relay_sem,
    cot_sem,
    part_sem,
    cols_sem,
    out_sem,
    *row_scratch,
):
    chips = lax.axis_size("mp") // 2
    me = lax.axis_index("mp")
    row = lax.axis_index("rows")
    chip = me // 2
    core = me % 2
    rows = x_ref.shape[0] // subs
    units = chips * subs
    twin = (row, me + 1 - 2 * core)

    def on_chip(other):
        return (row, 2 * other + core)

    barrier = pltpu.get_barrier_semaphore()
    pl.semaphore_signal(barrier, inc=1, device_id=twin, device_id_type=MESH)
    for step in range(1, chips):
        pl.semaphore_signal(
            barrier, inc=1, device_id=on_chip((chip + step) % chips), device_id_type=MESH
        )
    down, across = row // 2, row % 2
    beside_row = row + 1 - 2 * across
    above_row = (1 - down) * 2 + across
    neighbours = ((beside_row, me), (above_row, me))
    if quad:
        for device in neighbours:
            pl.semaphore_signal(barrier, inc=1, device_id=device, device_id_type=MESH)
    pl.semaphore_wait(barrier, chips + 2 if quad else chips)

    def order(i):
        near = jnp.minimum(chip, chips - 1 - chip)
        long_side = jnp.where(chip < chips - 1 - chip, 1, -1)
        j = i - subs
        paired = j < 2 * subs * near
        rest = j - 2 * subs * near
        dist = jnp.where(paired, j // (2 * subs) + 1, near + 1 + rest // subs)
        sub = jnp.where(paired, (j % (2 * subs)) // 2, rest % subs)
        side = jnp.where(paired, 1 - 2 * (j % 2), long_side)
        own = i < subs
        return (jnp.where(own, chip, chip + side * dist), jnp.where(own, i, sub))

    def x_copy(other, sub, side, source=None):
        spot = half_of(x_all, other, core, sub, rows)
        return pltpu.make_async_remote_copy(
            src_ref=spot if source is None else source,
            dst_ref=spot,
            send_sem=x_send.at[(side + 1) // 2, other * subs + sub],
            recv_sem=x_recv.at[other * subs + sub],
            device_id=on_chip(chip + side),
            device_id_type=MESH,
        )

    def twin_x_copy(other, sub, source=None):
        spot = half_of(x_all, other, core, sub, rows)
        return pltpu.make_async_remote_copy(
            src_ref=spot if source is None else source,
            dst_ref=spot,
            send_sem=twin_x_send.at[other * subs + sub],
            recv_sem=twin_x_recv.at[other * subs + sub],
            device_id=twin,
            device_id_type=MESH,
        )

    def twin_sum_copy(slot):
        return pltpu.make_async_remote_copy(
            src_ref=twin_buf.at[slot],
            dst_ref=twin_in.at[slot],
            send_sem=twin_send.at[slot],
            recv_sem=twin_recv.at[slot],
            device_id=twin,
            device_id_type=MESH,
        )

    def sum_copy(other, sub):
        side = jnp.where(other > chip, 1, -1)
        slot = jnp.where((side == 1) & (other == chip + 1), chips, other)
        return pltpu.make_async_remote_copy(
            src_ref=send_buf.at[other * subs + sub],
            dst_ref=sums_in.at[slot, sub],
            send_sem=sum_send.at[other * subs + sub],
            recv_sem=sum_recv.at[slot, sub],
            device_id=on_chip(chip + side),
            device_id_type=MESH,
        )

    def sum_arrival(slot, sub):
        return pltpu.make_async_remote_copy(
            src_ref=send_buf.at[0],
            dst_ref=sums_in.at[slot, sub],
            send_sem=sum_send.at[0],
            recv_sem=sum_recv.at[slot, sub],
            device_id=twin,
            device_id_type=MESH,
        )

    def cot_copies(other, sub, slot):
        return [
            pltpu.make_async_copy(
                half_of(cot_ref, other, c, sub, rows),
                cot_buf.at[slot, pl.ds(c * rows, rows)],
                cot_sem.at[slot, c],
            )
            for c in range(2)
        ]

    def part_copy(i):
        other, sub = order(i)
        return pltpu.make_async_copy(
            part_own.at[i % 2], part_ref.at[other * subs + sub], part_sem.at[i % 2]
        )

    for sub in range(subs):
        source = x_ref.at[pl.ds(sub * rows, rows)]

        @pl.when(chip < chips - 1)
        def _():
            x_copy(chip, sub, 1, source).start()

        @pl.when(chip > 0)
        def _():
            x_copy(chip, sub, -1, source).start()

        twin_x_copy(chip, sub, source).start()
    for copy in cot_copies(chip, 0, 0):
        copy.start()
    for sub in range(subs):
        half_of(x_all, chip, core, sub, rows)[...] = x_ref[sub * rows : (sub + 1) * rows, :]

    def reduce_unit(i):
        other, sub = order(i)
        unit = other * subs + sub
        slot = i % 2
        twin_sum_copy(slot).wait_recv()
        part_own[slot] = (
            part_own[slot].astype(F32) + twin_in[slot, 1].astype(F32)
        ).astype(BF16)
        part_copy(i).start()
        arrived = twin_in[slot, 0].astype(F32)
        lines = pl.ds(pl.multiple_of(sub * rows, rows), rows)

        @pl.when(other == chip)
        def _():
            sum_ref[lines, :] = sum_ref[lines, :] + arrived

        @pl.when(other != chip)
        def _():
            send_buf[unit] = (send_buf[unit].astype(F32) + arrived).astype(BF16)

        @pl.when(((other > chip) & (chip == 0)) | ((other < chip) & (chip == chips - 1)))
        def _():
            sum_copy(other, sub).start()

    def pass_on(e):
        right, left = chips - 1 - chip, chip
        right_first = chip < chips // 2
        ahead = jnp.where(right_first, right, left)
        step = jnp.where(e < ahead, e + 1, e - ahead + 1)
        toward = jnp.where((e < ahead) == right_first, 1, -1)
        other = chip + toward * step

        @pl.when((chip > 0) & (chip < chips - 1))
        def _():
            for sub in range(subs):
                unit = other * subs + sub
                sum_arrival(other, sub).wait_recv()
                send_buf[unit] = (
                    send_buf[unit].astype(F32) + sums_in[other, sub].astype(F32)
                ).astype(BF16)
                sum_copy(other, sub).start()

    def unit_step(i, _):
        other, sub = order(i)
        slot = i % 2

        @pl.when(i + 1 < units)
        def _():
            for copy in cot_copies(*order(i + 1), 1 - slot):
                copy.start()

        @pl.when(other != chip)
        def _():
            x_copy(other, sub, 1).wait_recv()
            twin_x_copy(other, sub).start()

            @pl.when((other > chip) & (chip > 0))
            def _():
                x_copy(other, sub, -1).start()

            @pl.when((other < chip) & (chip < chips - 1))
            def _():
                x_copy(other, sub, 1).start()

        twin_x_copy(other, sub).wait_recv()
        for copy in cot_copies(other, sub, slot):
            copy.wait()
        halves = [half_of(x_all, other, c, sub, rows)[...] for c in range(2)]
        x = jnp.concatenate(halves, axis=0)
        gate = dot(x, gate_ref[...])
        up = dot(x, up_ref[...])
        grad = dot_nt(cot_buf[slot], down_ref[...]) * scale_ref[0]
        sig = 1.0 / (1.0 + jnp.exp(-gate))
        act = gate * sig
        h = (act * up).astype(BF16)
        dg = (grad * up * (sig * (1.0 + gate * (1.0 - sig)))).astype(BF16)
        du = (grad * act).astype(BF16)
        for c in range(2):
            piece = slice(c * rows, (c + 1) * rows)
            half_of(hid, other, c, sub, rows)[...] = h[piece]
            half_of(dgate, other, c, sub, rows)[...] = dg[piece]
            half_of(dup, other, c, sub, rows)[...] = du[piece]

        @pl.when(i >= 2)
        def _():
            part_copy(i - 2).wait()
            twin_sum_copy(slot).wait_send()

        part = dot(h, down_ref[...])

        def keep_part(own, away):
            part_own[slot] = own.astype(BF16)
            twin_buf[slot, 1] = away.astype(BF16)

        @pl.when(core == 0)
        def _():
            keep_part(part[:rows], part[rows:])

        @pl.when(core == 1)
        def _():
            keep_part(part[rows:], part[:rows])

        dx = dot_nt(dg, gate_ref[...]) + dot_nt(du, up_ref[...])

        def keep(own, away):
            twin_buf[slot, 0] = away.astype(BF16)

            @pl.when(other == chip)
            def _():
                sum_ref[pl.ds(pl.multiple_of(sub * rows, rows), rows), :] = own

            @pl.when(other != chip)
            def _():
                send_buf[other * subs + sub] = own.astype(BF16)

        @pl.when(core == 0)
        def _():
            keep(dx[:rows], dx[rows:])

        @pl.when(core == 1)
        def _():
            keep(dx[rows:], dx[:rows])

        twin_sum_copy(slot).start()

        @pl.when(i >= 1)
        def _():
            reduce_unit(i - 1)

        return 0

    lax.fori_loop(0, units, unit_step, 0)
    reduce_unit(units - 1)
    for i in (units - 2, units - 1):
        part_copy(i).wait()
        twin_sum_copy(i % 2).wait_send()

    width = x_ref.shape[1]
    ff = gate_ref.shape[1]
    tall = tall_buf.shape[1]
    narrow = tall_buf.shape[2]
    down_cols = cot_cols.shape[2]
    col_steps = width // down_cols
    pieces = width // tall
    steps = pieces * (ff // narrow)
    wholes = (gate_out, up_out, down_out)

    if quad:
        firsts, seconds, finals = slots[0:3], slots[3:6], slots[6:9]
        tall_in, wide_in, moved, one_send, one_recv, two_send, two_recv, load_sem, fin_sem = (
            row_scratch[:2] + (row_scratch[2:5],) + row_scratch[5:]
        )

    def remote(source, dest, send, recv, device):
        return pltpu.make_async_remote_copy(
            src_ref=source,
            dst_ref=dest,
            send_sem=send,
            recv_sem=recv,
            device_id=device,
            device_id_type=MESH,
        )

    def block_at(a, block, d):
        high, wide = firsts[a].shape[2:]
        lines = pl.ds(pl.multiple_of(block * high, high), high)
        return wholes[a].at[lines, pl.ds(d * wide, wide)]

    def one_copy(a, d, k):
        block = k * 2 + 1 - across if d == 0 else (1 - down) * 2 + k
        return remote(
            block_at(a, block, d),
            firsts[a].at[d, k],
            one_send.at[a, d, k],
            one_recv.at[a, d, k],
            neighbours[d],
        )

    def two_copy(a, d):
        return remote(
            moved[a].at[d],
            seconds[a].at[d],
            two_send.at[a, d],
            two_recv.at[a, d],
            neighbours[1 - d],
        )

    def fin_copy(a, d):
        wide = firsts[a].shape[3]
        return pltpu.make_async_copy(
            (wide_in if a == 2 else tall_in).at[0],
            finals[a].at[:, pl.ds(d * wide, wide)],
            fin_sem.at[d],
        )

    def load(sources, buf):
        copies = [
            pltpu.make_async_copy(source, buf.at[i], load_sem.at[i])
            for i, source in enumerate(sources)
        ]
        for copy in copies:
            copy.start()
        for copy in copies:
            copy.wait()

    def stage_one(a):
        if quad:
            for d in range(2):
                for k in range(2):
                    one_copy(a, d, k).start()

    def stage_two(a):
        if quad:
            buf = wide_in if a == 2 else tall_in
            for d in range(2):
                for k in range(2):
                    one_copy(a, d, k).wait_recv()
                block = above_row if d == 0 else beside_row
                other = 1 - down if d == 0 else 1 - across
                load([block_at(a, block, d), firsts[a].at[d, other]], buf)
                moved[a][d] = (buf[0].astype(F32) + buf[1].astype(F32)).astype(BF16)
                two_copy(a, d).start()

    def stage_three(a):
        if quad:
            buf = wide_in if a == 2 else tall_in
            for d in range(2):
                two_copy(a, d).wait_recv()
                other = down if d == 0 else across
                load([block_at(a, row, d), firsts[a].at[d, other], seconds[a].at[d]], buf)
                buf[0] = (
                    buf[0].astype(F32) + buf[1].astype(F32) + buf[2].astype(F32)
                ).astype(BF16)
                fin_copy(a, d).start()
                fin_copy(a, d).wait()

    def end_far(source, other):
        return ((source == 0) & (other >= 2)) | ((source == chips - 1) & (other <= chips - 3))

    def relayed(source, other):
        return ((source == 1) & (other >= 2)) | ((source == chips - 2) & (other <= chips - 3))

    def p_copy(other, sub, source=None):
        return remote(
            part_ref.at[other * subs + sub] if source is None else source,
            part_in.at[chip, sub],
            p_send.at[other * subs + sub],
            p_recv.at[chip, sub],
            on_chip(other),
        )

    def relay_copy(other, sub):
        return remote(
            part_ref.at[other * subs + sub],
            relay_in.at[other, sub],
            p_send.at[other * subs + sub],
            relay_recv.at[other, sub],
            on_chip(jnp.where(chip == 0, 1, chips - 2)),
        )

    def send_parts(far):
        if True:
            for step in range(1, chips):
                other = (chip + step) % chips
                beyond = end_far(chip, other)
                for sub in range(subs):
                    if far:

                        @pl.when(beyond)
                        def _():
                            relay_copy(other, sub).start()

                    else:

                        @pl.when(jnp.logical_not(beyond | relayed(chip, other)))
                        def _():
                            p_copy(other, sub).start()

    def piece(index):
        return cot_buf.at[index // 2, pl.ds(index % 2 * rows, rows)]

    def fetch(source, index):
        copy = pltpu.make_async_copy(source, piece(index), relay_sem.at[index])
        copy.start()
        return copy

    def relay_parts():
        for step in range(1, chips):
            other = (chip + step) % chips

            @pl.when(relayed(chip, other))
            def _():
                for sub in range(subs):
                    mine = fetch(part_ref.at[other * subs + sub], 2 * sub)
                    remote(
                        part_ref.at[0],
                        relay_in.at[other, sub],
                        p_send.at[0],
                        relay_recv.at[other, sub],
                        twin,
                    ).wait_recv()
                    theirs = fetch(relay_in.at[other, sub], 2 * sub + 1)
                    mine.wait()
                    theirs.wait()
                    part_ref_sum = piece(2 * sub)[...].astype(F32) + piece(2 * sub + 1)[
                        ...
                    ].astype(F32)
                    piece(2 * sub)[...] = part_ref_sum.astype(BF16)
                    back = pltpu.make_async_copy(
                        piece(2 * sub), part_ref.at[other * subs + sub], relay_sem.at[2 * sub]
                    )
                    back.start()
                    back.wait()
                    p_copy(other, sub).start()

    def total_parts():
        for sub in range(subs):
            lines = slice(sub * rows, (sub + 1) * rows)
            fetch(part_ref.at[chip * subs + sub], 0).wait()
            part_sum[lines, :] = piece(0)[...].astype(F32)
            for step in range(1, chips):
                other = (chip + step) % chips

                @pl.when(jnp.logical_not(end_far(other, chip)))
                def _():
                    remote(
                        part_ref.at[0],
                        part_in.at[other, sub],
                        p_send.at[0],
                        p_recv.at[other, sub],
                        twin,
                    ).wait_recv()
                    fetch(part_in.at[other, sub], 0).wait()
                    part_sum[lines, :] = part_sum[lines, :] + piece(0)[...].astype(F32)

    send_parts(True)
    for a, source in enumerate((dgate, dup)):

        def tall_out(j):
            first = pl.multiple_of(j % pieces * tall, tall)
            col = pl.multiple_of(j // pieces * narrow, narrow)
            return pltpu.make_async_copy(
                tall_buf.at[j % 2],
                wholes[a].at[pl.ds(first, tall), pl.ds(col, narrow)],
                out_sem.at[j % 2],
            )

        def tall_step(j, _):
            @pl.when(j >= 2)
            def _():
                tall_out(j - 2).wait()

            first = pl.multiple_of(j % pieces * tall, tall)
            col = pl.multiple_of(j // pieces * narrow, narrow)
            tall_buf[j % 2] = dot_tn(
                x_all[:, pl.ds(first, tall)], source[:, pl.ds(col, narrow)]
            ).astype(BF16)
            tall_out(j).start()
            return 0

        lax.fori_loop(0, steps, tall_step, 0)
        for j in range(steps - 2, steps):
            tall_out(j).wait()
        stage_one(a)
        for e in range(a * (chips - 1) // 3, (a + 1) * (chips - 1) // 3):
            pass_on(e)
    send_parts(False)

    def cols_copy(j):
        return pltpu.make_async_copy(
            cot_ref.at[:, pl.ds(pl.multiple_of(j * down_cols, down_cols), down_cols)],
            cot_cols.at[j % 2],
            cols_sem.at[j % 2],
        )

    def wide_out(j):
        return pltpu.make_async_copy(
            wide_buf.at[j % 2],
            down_out.at[:, pl.ds(pl.multiple_of(j * down_cols, down_cols), down_cols)],
            out_sem.at[j % 2],
        )

    cols_copy(0).start()

    def down_step(j, _):
        @pl.when(j + 1 < col_steps)
        def _():
            cols_copy(j + 1).start()

        cols_copy(j).wait()

        @pl.when(j >= 2)
        def _():
            wide_out(j - 2).wait()

        wide_buf[j % 2] = (dot_tn(hid[...], cot_cols[j % 2]) * scale_ref[0]).astype(BF16)
        wide_out(j).start()
        return 0

    lax.fori_loop(0, col_steps, down_step, 0)
    for j in range(max(0, col_steps - 2), col_steps):
        wide_out(j).wait()
    stage_one(2)
    for e in range(2 * (chips - 1) // 3, chips - 1):
        pass_on(e)
    stage_two(0)
    relay_parts()
    stage_two(1)
    stage_three(0)
    stage_two(2)
    stage_three(1)
    stage_three(2)
    total_parts()
    if quad:
        for a in range(3):
            for d in range(2):
                two_copy(a, d).wait_send()
                for k in range(2):
                    one_copy(a, d, k).wait_send()

    for sub in range(subs):
        lines = slice(sub * rows, (sub + 1) * rows)

        @pl.when(chip < chips - 1)
        def _():
            sum_arrival(chip, sub).wait_recv()
            sum_ref[lines, :] = sum_ref[lines, :] + sums_in[chip, sub].astype(F32)

        @pl.when(chip > 0)
        def _():
            sum_arrival(chips, sub).wait_recv()
            sum_ref[lines, :] = sum_ref[lines, :] + sums_in[chips, sub].astype(F32)

    def finish(i, _):
        other, sub = order(i)
        twin_x_copy(other, sub).wait_send()

        @pl.when(((other >= chip) & (chip > 0)))
        def _():
            x_copy(other, sub, -1).wait_send()

        @pl.when(((other <= chip) & (chip < chips - 1)))
        def _():
            x_copy(other, sub, 1).wait_send()

        @pl.when(other != chip)
        def _():
            sum_copy(other, sub).wait_send()
            p_copy(other, sub).wait_send()

        return 0

    lax.fori_loop(0, units, finish, 0)


def ffn(scale, x, cot_all, gate_weight, up_weight, down_weight):
    tokens, width = cot_all.shape
    rows_dev = x.shape[0]
    chips = lax.axis_size("mp") // 2
    ff = gate_weight.shape[1]
    subs = max(1, rows_dev // BLOCK)
    rows = rows_dev // subs
    units = chips * subs
    narrow = ff // 3
    tall = 512
    down_cols = 256
    quad = lax.axis_size("rows") == 4
    extra_out, row_scratch = (), []
    vmem = pl.BlockSpec(memory_space=pltpu.VMEM)
    hbm = pl.BlockSpec(memory_space=pl.ANY)
    dma = pltpu.SemaphoreType.DMA
    if quad:
        sizes = ((width // 4, ff // 2), (width // 4, ff // 2), (ff // 4, width // 2))
        extra_out = (
            tuple(jax.ShapeDtypeStruct((2, 2, *size), BF16) for size in sizes)
            + tuple(jax.ShapeDtypeStruct((2, *size), BF16) for size in sizes)
            + tuple(jax.ShapeDtypeStruct((size[0], 2 * size[1]), BF16) for size in sizes)
        )
        row_scratch = (
            [pltpu.VMEM((3, *sizes[0]), BF16), pltpu.VMEM((3, *sizes[2]), BF16)]
            + [pltpu.VMEM((2, *size), BF16) for size in sizes]
            + [dma((3, 2, 2)), dma((3, 2, 2)), dma((3, 2)), dma((3, 2)), dma((3,)), dma((2,))]
        )
    out = pl.pallas_call(
        functools.partial(ffn_kernel, subs, quad),
        out_shape=(
            jax.ShapeDtypeStruct((units, rows, width), BF16),
            jax.ShapeDtypeStruct((chips, subs, rows, width), BF16),
            jax.ShapeDtypeStruct((chips, subs, rows, width), BF16),
            jax.ShapeDtypeStruct((rows_dev, width), F32),
            jax.ShapeDtypeStruct((rows_dev, width), F32),
            jax.ShapeDtypeStruct((width, ff), BF16),
            jax.ShapeDtypeStruct((width, ff), BF16),
            jax.ShapeDtypeStruct((ff, width), BF16),
        )
        + extra_out,
        in_specs=[pl.BlockSpec(memory_space=pltpu.SMEM), vmem, hbm, vmem, vmem, vmem],
        out_specs=(hbm, hbm, hbm, vmem, vmem, hbm, hbm, hbm) + (hbm,) * len(extra_out),
        scratch_shapes=[
            pltpu.VMEM((tokens, width), BF16),
            pltpu.VMEM((tokens, ff), BF16),
            pltpu.VMEM((tokens, ff), BF16),
            pltpu.VMEM((tokens, ff), BF16),
            pltpu.VMEM((2, 2 * rows, width), BF16),
            pltpu.VMEM((2, rows, width), BF16),
            pltpu.VMEM((2, 2, rows, width), BF16),
            pltpu.VMEM((2, 2, rows, width), BF16),
            pltpu.VMEM((units, rows, width), BF16),
            pltpu.VMEM((chips + 1, subs, rows, width), BF16),
            pltpu.VMEM((2, tokens, down_cols), BF16),
            pltpu.VMEM((2, ff, down_cols), BF16),
            pltpu.VMEM((2, tall, narrow), BF16),
            dma((2, units)),
            dma((units,)),
            dma((units,)),
            dma((units,)),
            dma((2,)),
            dma((2,)),
            dma((units,)),
            dma((chips + 1, subs)),
            dma((units,)),
            dma((chips, subs)),
            dma((chips, subs)),
            dma((4,)),
            dma((2, 2)),
            dma((2,)),
            dma((2,)),
            dma((2,)),
        ]
        + row_scratch,
        compiler_params=pltpu.CompilerParams(
            collective_id=1, has_side_effects=True, vmem_limit_bytes=VMEM_LIMIT
        ),
        cost_estimate=pl.CostEstimate(
            flops=60_000_000_000, bytes_accessed=60_000_000, transcendentals=2_000_000
        ),
        name="ffn",
    )(scale.reshape(1), x, cot_all, gate_weight, up_weight, down_weight)
    if quad:
        shards = out[14:17]
    else:
        shards = [lax.psum(part, "rows") for part in out[5:8]]
    return (*out[3:5], *shards)


class Reducer:
    def __init__(self, height, left, right, gains, out, bufs):
        self.height, self.right, self.gains, self.out = height, right, gains, out
        (self.turned, self.own, self.twin_out, self.twin_in, self.out1, self.in1) = bufs[:6]
        (self.out2, self.in2, self.out3, self.in3) = bufs[6:10]
        (self.s0, self.r0, self.s1, self.r1, self.s2, self.r2, self.s3) = bufs[10:]
        self.cols = self.own.shape[-1]
        self.chips = lax.axis_size("mp") // 2
        me = lax.axis_index("mp")
        self.row = lax.axis_index("rows")
        self.chip, self.core = me // 2, me % 2
        self.down, self.across = self.row // 2, self.row % 2
        self.twin = (self.row, me + 1 - 2 * self.core)
        self.beside = (self.row + 1 - 2 * self.across, me)
        self.above = ((1 - self.down) * 2 + self.across, me)
        self.turned[...] = left[...].T

    def remote(self, source, dest, send, recv, device):
        return pltpu.make_async_remote_copy(
            src_ref=source,
            dst_ref=dest,
            send_sem=send,
            recv_sem=recv,
            device_id=device,
            device_id_type=MESH,
        )

    def goal(self, i):
        return (self.chip + 1 + i) % self.chips

    def twin_copy(self, i):
        return self.remote(
            self.twin_out.at[i], self.twin_in.at[i], self.s0.at[i], self.r0.at[i], self.twin
        )

    def first_copy(self, i, d):
        return self.remote(
            self.out1.at[i, d],
            self.in1.at[i, d],
            self.s1.at[i, d],
            self.r1.at[i, d],
            (self.beside, self.above)[d],
        )

    def second_copy(self, i, d):
        return self.remote(
            self.out2.at[i, d],
            self.in2.at[i, d],
            self.s2.at[i, d],
            self.r2.at[i, d],
            (self.above, self.beside)[d],
        )

    def last_copy(self, i):
        return self.remote(
            self.out3.at[i],
            self.in3.at[i],
            self.s3.at[0, i],
            self.s3.at[1, i],
            (self.row, 2 * self.goal(i) + self.core),
        )

    def make(self, i):
        height = self.height
        for r in range(4):
            first = (r * self.chips + self.goal(i)) * 2 * height
            lines = pl.ds(pl.multiple_of(first, 16), 2 * height)
            block = dot(self.turned[lines, :], self.right[...])
            spare = self.cols - block.shape[1]
            if spare:
                piece = self.gains[:, pl.ds(pl.multiple_of(first, 128), 2 * height)]
                piece = jnp.concatenate(
                    [piece, jnp.zeros((spare - piece.shape[0], 2 * height), F32)], axis=0
                ).T
                block = jnp.concatenate([block, piece], axis=1)

            @pl.when(self.core == 0)
            def _():
                self.own[i, r] = block[:height]
                self.twin_out[i, r] = block[height:].astype(BF16)

            @pl.when(self.core == 1)
            def _():
                self.own[i, r] = block[height:]
                self.twin_out[i, r] = block[:height].astype(BF16)

        self.twin_copy(i).start()

    def first_stage(self, i):
        half = self.cols // 2
        own = self.own
        self.twin_copy(i).wait_recv()
        for r in range(4):
            own[i, r] = own[i, r] + self.twin_in[i, r].astype(F32)
        for k in range(2):
            self.out1[i, 0, k] = own[i, k * 2 + 1 - self.across, :, :half].astype(BF16)
            self.out1[i, 1, k] = own[i, (1 - self.down) * 2 + k, :, half:].astype(BF16)
        for d in range(2):
            self.first_copy(i, d).start()

    def second_stage(self, i):
        half = self.cols // 2
        for d in range(2):
            self.first_copy(i, d).wait_recv()
        above = (1 - self.down) * 2 + self.across
        beside = self.down * 2 + 1 - self.across
        self.out2[i, 0] = (
            self.own[i, above, :, :half] + self.in1[i, 0, 1 - self.down].astype(F32)
        ).astype(BF16)
        self.out2[i, 1] = (
            self.own[i, beside, :, half:] + self.in1[i, 1, 1 - self.across].astype(F32)
        ).astype(BF16)
        for d in range(2):
            self.second_copy(i, d).start()

    def third_stage(self, i):
        half = self.cols // 2
        for d in range(2):
            self.second_copy(i, d).wait_recv()
        left = (
            self.own[i, self.row, :, :half]
            + self.in1[i, 0, self.down].astype(F32)
            + self.in2[i, 0].astype(F32)
        )
        right = (
            self.own[i, self.row, :, half:]
            + self.in1[i, 1, self.across].astype(F32)
            + self.in2[i, 1].astype(F32)
        )

        @pl.when(i < self.chips - 1)
        def _():
            self.out3[i, :, :half] = left.astype(BF16)
            self.out3[i, :, half:] = right.astype(BF16)
            self.last_copy(i).start()

        @pl.when(i == self.chips - 1)
        def _():
            self.out[:, :half] = left
            self.out[:, half:] = right

    def round(self, n, _=None):
        stages = (self.make, self.first_stage, self.second_stage, self.third_stage)
        for stage, work in enumerate(stages):

            @pl.when((n >= stage) & (n < self.chips + stage))
            def _():
                work(n - stage)

        return 0

    def close(self):
        for i in range(self.chips - 1):
            self.last_copy(i).wait_recv()
            self.out[...] = self.out[...] + self.in3[i].astype(F32)

        def finish(i, _):
            self.twin_copy(i).wait_send()
            for d in range(2):
                self.first_copy(i, d).wait_send()
                self.second_copy(i, d).wait_send()

            @pl.when(i < self.chips - 1)
            def _():
                self.last_copy(i).wait_send()

            return 0

        lax.fori_loop(0, self.chips, finish, 0)


def reducer_buffers(left, right):
    chips = lax.axis_size("mp") // 2
    shards = lax.axis_size("rows") * lax.axis_size("mp")
    height = left.shape[1] // shards
    cols = -(-right.shape[1] // 256) * 256
    half = cols // 2
    dma = pltpu.SemaphoreType.DMA
    return (
        height,
        jax.ShapeDtypeStruct((height, cols), F32),
        [
            pltpu.VMEM((left.shape[1], left.shape[0]), BF16),
            pltpu.VMEM((chips, 4, height, cols), F32),
            pltpu.VMEM((chips, 4, height, cols), BF16),
            pltpu.VMEM((chips, 4, height, cols), BF16),
            pltpu.VMEM((chips, 2, 2, height, half), BF16),
            pltpu.VMEM((chips, 2, 2, height, half), BF16),
            pltpu.VMEM((chips, 2, height, half), BF16),
            pltpu.VMEM((chips, 2, height, half), BF16),
            pltpu.VMEM((chips - 1, height, cols), BF16),
            pltpu.VMEM((chips - 1, height, cols), BF16),
            dma((chips,)),
            dma((chips,)),
            dma((chips, 2)),
            dma((chips, 2)),
            dma((chips, 2)),
            dma((chips, 2)),
            dma((2, chips)),
        ],
    )


def reduce_kernel(height, left, right, gains, out, *bufs):
    chips = lax.axis_size("mp") // 2
    me = lax.axis_index("mp")
    row = lax.axis_index("rows")
    chip, core = me // 2, me % 2
    down, across = row // 2, row % 2
    barrier = pltpu.get_barrier_semaphore()
    devices = [
        (row, me + 1 - 2 * core),
        (row + 1 - 2 * across, me),
        ((1 - down) * 2 + across, me),
    ] + [(row, 2 * ((chip + step) % chips) + core) for step in range(1, chips)]
    for device in devices:
        pl.semaphore_signal(barrier, inc=1, device_id=device, device_id_type=MESH)
    pl.semaphore_wait(barrier, chips + 2)
    reducer = Reducer(height, left, right, gains, out, bufs)
    lax.fori_loop(0, chips + 3, reducer.round, 0)
    reducer.close()


def reduce_product(left, right, gains):
    height, out_shape, scratch = reducer_buffers(left, right)
    vmem = pl.BlockSpec(memory_space=pltpu.VMEM)
    return pl.pallas_call(
        functools.partial(reduce_kernel, height),
        out_shape=out_shape,
        in_specs=[vmem] * 3,
        out_specs=vmem,
        scratch_shapes=scratch,
        compiler_params=pltpu.CompilerParams(
            collective_id=2, has_side_effects=True, vmem_limit_bytes=VMEM_LIMIT
        ),
        cost_estimate=pl.CostEstimate(
            flops=50_000_000_000, bytes_accessed=10_000_000, transcendentals=0
        ),
        name="reduce_product",
    )(left, right, gains)


def natural(device, sub, subs):
    if subs == 2:
        return sub * (2 * lax.axis_size("mp") - 1 - 2 * device) + (1 - sub) * 2 * device
    return subs * device + sub


def front_kernel(
    shard_ref,
    x_ref,
    cos_q,
    sin_q,
    cos_kv,
    sin_kv,
    w_out,
    extra_ref,
    xf_ref,
    normed_ref,
    inv_ref,
    q_ref,
    kv_out,
    w_all,
    x_in,
    kv_all,
    swap_send,
    swap_recv,
    z_send,
    z_recv,
    xy_send,
    xy_recv,
    far_send,
    far_recv,
    twin_send,
    twin_recv,
    kz_send,
    kz_recv,
    kt_send,
    kt_recv,
    out_sem,
):
    mp = lax.axis_size("mp")
    chips = mp // 2
    me = lax.axis_index("mp")
    row = lax.axis_index("rows")
    chip = me // 2
    core = me % 2
    down, across = row // 2, row % 2
    subs = x_ref.shape[0] // BLOCK
    height = shard_ref.shape[0]
    half = w_all.shape[1] // 2
    beside_row = row + 1 - 2 * across
    above_row = (1 - down) * 2 + across
    far_row = (1 - down) * 2 + 1 - across
    twin = (row, me + 1 - 2 * core)
    beside = (beside_row, me)
    above = (above_row, me)
    mirror = (row, mp - 1 - me)

    barrier = pltpu.get_barrier_semaphore()
    for device in (twin, beside, above, mirror):
        pl.semaphore_signal(barrier, inc=1, device_id=device, device_id_type=MESH)

    @pl.when(chip < chips - 1)
    def _():
        pl.semaphore_signal(barrier, inc=1, device_id=(row, me + 2), device_id_type=MESH)

    @pl.when(chip > 0)
    def _():
        pl.semaphore_signal(barrier, inc=1, device_id=(row, me - 2), device_id_type=MESH)

    ends = jnp.where(chip < chips - 1, 1, 0) + jnp.where(chip > 0, 1, 0)
    pl.semaphore_wait(barrier, 4 + ends)

    def remote(source, dest, send, recv, device):
        return pltpu.make_async_remote_copy(
            src_ref=source,
            dst_ref=dest,
            send_sem=send,
            recv_sem=recv,
            device_id=device,
            device_id_type=MESH,
        )

    def spot(r, k, side=None):
        lines = pl.ds(pl.multiple_of((r * mp + 2 * k + core) * height, height), height)
        if side is None:
            return w_all.at[lines]
        return w_all.at[lines, pl.ds(side * half, half)]

    def z_copy(k, side):
        return remote(
            spot(row, k),
            spot(row, k),
            z_send.at[(side + 1) // 2, k],
            z_recv.at[k],
            (row, me + 2 * side),
        )

    def near_copy(k, d):
        return remote(
            spot(row, k), spot(row, k), xy_send.at[d, k], xy_recv.at[d, k], (beside, above)[d]
        )

    def near_row(d):
        return (beside_row, above_row)[d]

    def far_copy(k, d):
        place = spot(near_row(d), k, d)
        return remote(place, place, far_send.at[d, k], far_recv.at[d, k], (above, beside)[d])

    def twin_copy(k, kind):
        if kind < 3:
            place = spot((row, beside_row, above_row)[kind], k)
        else:
            place = spot(far_row, k, kind - 3)
        return remote(place, place, twin_send.at[kind, k], twin_recv.at[kind, k], twin)

    def order(i):
        near = jnp.minimum(chip, chips - 1 - chip)
        long_side = jnp.where(chip < chips - 1 - chip, 1, -1)
        paired = i <= 2 * near
        dist = jnp.where(paired, (i + 1) // 2, i - near)
        side = jnp.where(paired, 2 * (i % 2) - 1, long_side)
        return chip + side * dist

    if subs == 2:
        swap = remote(x_ref.at[pl.ds(BLOCK, BLOCK)], x_in, swap_send, swap_recv, mirror)
        swap.start()
    own_lines = pl.ds(pl.multiple_of((row * mp + me) * height, height), height)
    w_all[own_lines, :] = shard_ref[...]

    def gather_step(n, _):
        @pl.when(n < chips)
        def _():
            k = order(n)

            @pl.when(n > 0)
            def _():
                z_copy(k, 1).wait_recv()

            for d in range(2):
                near_copy(k, d).start()

            @pl.when((k >= chip) & (chip > 0))
            def _():
                z_copy(k, -1).start()

            @pl.when((k <= chip) & (chip < chips - 1))
            def _():
                z_copy(k, 1).start()

            twin_copy(k, 0).start()

        @pl.when((n >= 1) & (n < chips + 1))
        def _():
            k = order(n - 1)
            for d in range(2):
                near_copy(k, d).wait_recv()
                far_copy(k, d).start()
                twin_copy(k, 1 + d).start()

        @pl.when(n >= 2)
        def _():
            k = order(n - 2)
            for d in range(2):
                far_copy(k, d).wait_recv()
                twin_copy(k, 3 + d).start()

        return 0

    lax.fori_loop(0, chips + 2, gather_step, 0)

    xf_ref[:BLOCK, :] = x_ref[:BLOCK, :]
    if subs == 2:
        swap.wait_recv()
        xf_ref[BLOCK:, :] = x_in[...]

    def drain_step(k, _):
        for kind in range(5):
            twin_copy(k, kind).wait_recv()
        return 0

    lax.fori_loop(0, chips, drain_step, 0)
    save = pltpu.make_async_copy(w_all, w_out, out_sem)
    save.start()
    cols = Q_WIDTH + 2 * KV_WIDTH
    extra = w_all[:, cols:].astype(F32).T[:8, :]
    extra_ref[...] = extra
    x = xf_ref[...].astype(F32)
    inverse = lax.rsqrt(jnp.mean(x * x, axis=-1, keepdims=True) + EPS)
    inv_ref[...] = inverse
    normed_ref[...] = (x * inverse * extra[0:1, :]).astype(BF16)

    def place_of(device, sub):
        first = natural(device, sub, subs) * BLOCK
        return kv_all.at[pl.ds(pl.multiple_of(first, BLOCK), BLOCK)]

    part = dot(normed_ref[...], w_all[:, Q_WIDTH:cols])
    for g in range(KV_HEADS):
        slab = part[:, g * SLAB : (g + 1) * SLAB]
        turned = (slab * cos_kv[...] + swap_halves(slab) * sin_kv[...]).astype(BF16)
        for sub in range(subs):
            place_of(me, sub)[:, g * SLAB : (g + 1) * SLAB] = turned[
                sub * BLOCK : (sub + 1) * BLOCK, :
            ]

    def kz_copy(k, sub, side):
        place = place_of(2 * k + core, sub)
        return remote(
            place,
            place,
            kz_send.at[(side + 1) // 2, k * subs + sub],
            kz_recv.at[k * subs + sub],
            (row, me + 2 * side),
        )

    def kt_copy(k, sub):
        place = place_of(2 * k + core, sub)
        return remote(
            place, place, kt_send.at[k * subs + sub], kt_recv.at[k * subs + sub], twin
        )

    def spread(n, _):
        k = order(n)
        for sub in range(subs):

            @pl.when(n > 0)
            def _():
                kz_copy(k, sub, 1).wait_recv()

            @pl.when((k >= chip) & (chip > 0))
            def _():
                kz_copy(k, sub, -1).start()

            @pl.when((k <= chip) & (chip < chips - 1))
            def _():
                kz_copy(k, sub, 1).start()

            kt_copy(k, sub).start()

        return 0

    spread(0, 0)
    for s in range(Q_WIDTH // 256):
        part = dot(normed_ref[...], w_all[:, s * 256 : (s + 1) * 256])
        for t in range(2):
            slab = part[:, t * SLAB : (t + 1) * SLAB]
            col = s * 256 + t * SLAB
            turned = slab * cos_q[...] + swap_halves(slab) * sin_q[...]
            q_ref[:, col : col + SLAB] = (
                turned.astype(BF16).astype(F32) * HEAD_DIM ** (-0.5)
            ).astype(BF16)
    lax.fori_loop(1, chips, spread, 0)

    def finish(k, _):
        for sub in range(subs):
            kt_copy(k, sub).wait_recv()
            kt_copy(k, sub).wait_send()
        for kind in range(5):
            twin_copy(k, kind).wait_send()
        for d in range(2):
            near_copy(k, d).wait_send()
            far_copy(k, d).wait_send()

        @pl.when((k >= chip) & (chip > 0))
        def _():
            z_copy(k, -1).wait_send()
            for sub in range(subs):
                kz_copy(k, sub, -1).wait_send()

        @pl.when((k <= chip) & (chip < chips - 1))
        def _():
            z_copy(k, 1).wait_send()
            for sub in range(subs):
                kz_copy(k, sub, 1).wait_send()

        return 0

    lax.fori_loop(0, chips, finish, 0)
    if subs == 2:
        swap.wait_send()
    kv_out[...] = kv_all[...]
    save.wait()


def front(shard, x, tables):
    rows, width = x.shape
    subs = rows // BLOCK
    chips = lax.axis_size("mp") // 2
    cols = shard.shape[1]
    total = shard.shape[0] * lax.axis_size("rows") * lax.axis_size("mp")
    vmem = pl.BlockSpec(memory_space=pltpu.VMEM)
    hbm = pl.BlockSpec(memory_space=pl.ANY)
    dma = pltpu.SemaphoreType.DMA
    return pl.pallas_call(
        front_kernel,
        out_shape=(
            jax.ShapeDtypeStruct((total, cols), BF16),
            jax.ShapeDtypeStruct((8, total), F32),
            jax.ShapeDtypeStruct((rows, width), BF16),
            jax.ShapeDtypeStruct((rows, width), BF16),
            jax.ShapeDtypeStruct((rows, 1), F32),
            jax.ShapeDtypeStruct((rows, Q_WIDTH), BF16),
            jax.ShapeDtypeStruct((LEN, 2 * KV_WIDTH), BF16),
        ),
        in_specs=[vmem] * 6,
        out_specs=(hbm,) + (vmem,) * 6,
        scratch_shapes=[
            pltpu.VMEM((total, cols), BF16),
            pltpu.VMEM((BLOCK, width), BF16),
            pltpu.VMEM((LEN, 2 * KV_WIDTH), BF16),
            dma,
            dma,
            dma((2, chips)),
            dma((chips,)),
            dma((2, chips)),
            dma((2, chips)),
            dma((2, chips)),
            dma((2, chips)),
            dma((5, chips)),
            dma((5, chips)),
            dma((2, chips * subs)),
            dma((chips * subs,)),
            dma((chips * subs,)),
            dma((chips * subs,)),
            dma,
        ],
        compiler_params=pltpu.CompilerParams(
            collective_id=4, has_side_effects=True, vmem_limit_bytes=VMEM_LIMIT
        ),
        cost_estimate=pl.CostEstimate(
            flops=30_000_000_000, bytes_accessed=12_000_000, transcendentals=0
        ),
        name="front",
    )(shard, x, *tables)


def on_device(
    inputs,
    cotangent,
    corpus_ids,
    corpus_weight,
    attn_gain,
    qkv_weight,
    out_weight,
    ffn_gain,
    gate_weight,
    up_weight,
    down_weight,
):
    both = ("rows", "mp")
    rows_dev, width = inputs.shape
    mp = lax.axis_size("mp")
    me = lax.axis_index("mp")
    row_groups = lax.axis_size("rows")
    corpora = corpus_weight.shape[0]
    subs = rows_dev // BLOCK
    folded = subs == 2
    mirror = [(i, mp - 1 - i) for i in range(mp)]

    def fold(rows):
        if not folded:
            return rows
        return jnp.concatenate(
            [rows[:BLOCK], lax.ppermute(rows[BLOCK:], "mp", mirror)], axis=0
        )

    def to_order(gathered):
        if not folded:
            return gathered
        parts = gathered.reshape(mp, 2, BLOCK, gathered.shape[-1])
        return jnp.stack([parts[:, 0], parts[::-1, 1]], axis=1).reshape(gathered.shape)

    if folded:
        blocks = jnp.stack([2 * me, 2 * mp - 1 - 2 * me]).astype(jnp.int32)
    else:
        blocks = (subs * me + jnp.arange(subs)).astype(jnp.int32)
    positions = (blocks[:, None] * BLOCK + jnp.arange(BLOCK)[None, :]).reshape(-1)

    shard_rows = qkv_weight.shape[0]
    ident = jnp.broadcast_to(corpus_ids.astype(BF16)[:1, None], (shard_rows, 1))
    spare = (-(Q_WIDTH + 2 * KV_WIDTH + 3)) % 128
    shard = jnp.concatenate(
        [
            pack_kv(qkv_weight),
            attn_gain[:, None],
            ffn_gain[:, None],
            ident,
            jnp.zeros((shard_rows, spare), BF16),
        ],
        axis=1,
    )
    qkv_cols = Q_WIDTH + 2 * KV_WIDTH
    cot_all = lax.all_gather(cotangent, "mp", axis=0, tiled=True)
    out_full = lax.all_gather(out_weight, both, axis=0, tiled=True)
    tables = rope_tables(positions)
    if row_groups == 4:
        qkv_ext, extras, x, normed_one, inverse_one, q, kv_all = front(shard, inputs, tables)
        qkv_full = qkv_ext[:, :qkv_cols]
    else:
        qkv_ext = lax.all_gather(shard, both, axis=0, tiled=True)
        qkv_full = qkv_ext[:, :qkv_cols]
        extras = qkv_ext[:, qkv_cols:].astype(F32).T
        x = fold(inputs)
        normed_one, inverse_one, q, kv = qkv_project(x, extras[0:1], qkv_full, tables)
        kv_all = to_order(lax.all_gather(kv, "mp", axis=0, tiled=True))
    gain_one, gain_two = extras[0:1], extras[1:2]
    all_ids = extras[2].reshape(row_groups, -1)[:, 0]
    my_id = corpus_ids[0].astype(F32)
    count = jnp.sum((all_ids == my_id).astype(F32))
    weight_seq = jnp.sum(
        jnp.where(jnp.arange(corpora) == corpus_ids[0], corpus_weight, 0.0)
    )
    seq_scale = weight_seq * row_groups / (corpora * count)
    o, totals = attend(blocks, q, kv_all)

    residual = x.astype(F32)
    middle = residual + dot(o, out_full)
    inverse_two = lax.rsqrt(jnp.mean(middle * middle, axis=-1, keepdims=True) + EPS)
    normed_two = (middle * inverse_two * gain_two).astype(BF16)
    ffn_sum, grad_normed_two, gate_grad, up_grad, down_grad = ffn(
        seq_scale, normed_two, cot_all, gate_weight, up_weight, down_weight
    )
    outputs = fold((middle + ffn_sum).astype(BF16))

    cot = jnp.concatenate(
        [
            lax.dynamic_slice(cot_all, (blocks[sub] * BLOCK, 0), (BLOCK, width))
            for sub in range(subs)
        ],
        axis=0,
    )
    grad_out = cot.astype(F32) * seq_scale
    scaled_two = grad_normed_two * gain_two
    ffn_gain_part = jnp.sum(grad_normed_two * middle * inverse_two, axis=0)
    grad_middle = (
        grad_out
        + inverse_two * scaled_two
        - middle * inverse_two**3 * jnp.mean(scaled_two * middle, axis=-1, keepdims=True)
    )
    grad_middle_low = grad_middle.astype(BF16)
    if row_groups == 4:
        gate_grad, up_grad, down_grad = (
            lax.all_gather(g, "rows", axis=0, tiled=True)
            for g in (gate_grad, up_grad, down_grad)
        )
    grad_o = dot_nt(grad_middle_low, out_full).astype(BF16)
    grad_qkv, *proj = attend_back(q, kv_all, o, grad_o, totals, tables, grad_middle_low)
    grad_normed_one = dot_nt(grad_qkv, qkv_full)
    scaled_one = grad_normed_one * gain_one
    attn_gain_part = jnp.sum(grad_normed_one * residual * inverse_one, axis=0)
    input_grad = (
        grad_middle
        + inverse_one * scaled_one
        - residual * inverse_one**3 * jnp.mean(scaled_one * residual, axis=-1, keepdims=True)
    )
    if folded:
        input_grad = jnp.concatenate(
            [
                input_grad[:BLOCK],
                lax.ppermute(input_grad[BLOCK:].astype(BF16), "mp", mirror).astype(F32),
            ],
            axis=0,
        )
    gain_parts = jnp.concatenate(
        [attn_gain_part[None], ffn_gain_part[None], jnp.zeros((6, width), F32)], axis=0
    )
    if row_groups == 4:
        proj_grad = proj[0]
        part = reduce_product(normed_one, grad_qkv, gain_parts)
    else:
        part = jnp.concatenate(
            [dot_tn(normed_one, grad_qkv), gain_parts.T, jnp.zeros((width, 120), F32)], axis=1
        )
        part, proj_grad = (
            lax.psum_scatter(p.astype(BF16), both, scatter_dimension=0, tiled=True).astype(F32)
            for p in (part, dot_tn(o, grad_middle_low))
        )
    qkv_grad = unpack_kv(part[:, :qkv_cols])
    attn_gain_grad = part[:, qkv_cols]
    ffn_gain_grad = part[:, qkv_cols + 1]
    gate_grad, part = lax.optimization_barrier((gate_grad, part))
    gate_grad = gate_grad.astype(F32)
    up_grad, part = lax.optimization_barrier((up_grad, part))
    up_grad = up_grad.astype(F32)
    down_grad, part = lax.optimization_barrier((down_grad, part))
    down_grad = down_grad.astype(F32)
    qkv_grad = unpack_kv(part[:, :qkv_cols])
    attn_gain_grad = part[:, qkv_cols]
    ffn_gain_grad = part[:, qkv_cols + 1]
    return (
        outputs,
        input_grad,
        qkv_grad,
        proj_grad,
        gate_grad,
        up_grad,
        down_grad,
        attn_gain_grad,
        ffn_gain_grad,
    )


def solution(mesh):
    split = P(("rows", "mp"), None)
    line = P(("rows", "mp"))
    in_specs = (
        split,
        split,
        P("rows"),
        P(),
        line,
        split,
        split,
        line,
        P(None, "mp"),
        P(None, "mp"),
        P("mp", None),
    )
    out_specs = (
        split,
        split,
        split,
        split,
        P(None, "mp"),
        P(None, "mp"),
        P("mp", None),
        line,
        line,
    )
    return jax.shard_map(
        on_device, mesh=mesh, in_specs=in_specs, out_specs=out_specs, check_vma=False
    )
```

```python
import functools

import jax
import jax.numpy as jnp
from jax import lax
from jax.experimental import pallas as pl
from jax.experimental.pallas import tpu as pltpu
from jax.sharding import PartitionSpec as P

HEADS = 20
KV_HEADS = 5
HEAD_DIM = 64
GROUP = HEADS // KV_HEADS
Q_WIDTH = HEADS * HEAD_DIM
KV_WIDTH = KV_HEADS * HEAD_DIM
LEN = 2048
BLOCK = 128
KTILE = 256
EPS = 1e-05
THETA = 10000.0
LANES = GROUP * BLOCK
SLAB = 2 * HEAD_DIM

MESH = pl.DeviceIdType.MESH
F32 = jnp.float32
BF16 = jnp.bfloat16
VMEM_LIMIT = 62 * 1024 * 1024


def rope_tables(positions):
    half_dim = HEAD_DIM // 2
    freqs = jnp.exp(-jnp.log(THETA) * (2.0 * jnp.arange(half_dim, dtype=F32)) / HEAD_DIM)
    angles = positions.astype(F32)[:, None] * freqs[None, :]
    cosine, sine = jnp.cos(angles), jnp.sin(angles)
    ones, zeros = jnp.ones_like(cosine), jnp.zeros_like(cosine)
    head_cos = jnp.concatenate([cosine, cosine], axis=1)
    head_sin = jnp.concatenate([-sine, sine], axis=1)
    cos_q = jnp.concatenate([head_cos, head_cos], axis=1)
    sin_q = jnp.concatenate([head_sin, head_sin], axis=1)
    cos_kv = jnp.concatenate([head_cos, ones, ones], axis=1)
    sin_kv = jnp.concatenate([head_sin, zeros, zeros], axis=1)
    return (cos_q, sin_q, cos_kv, sin_kv)


def swap_halves(slab):
    lane = lax.broadcasted_iota(jnp.int32, slab.shape, 1)
    half_dim = HEAD_DIM // 2
    up = pltpu.roll(slab, SLAB - half_dim, 1)
    down = pltpu.roll(slab, half_dim, 1)
    return jnp.where(lane % HEAD_DIM < half_dim, up, down)


def qkv_kernel(x_ref, gain_ref, w_ref, cos_q, sin_q, cos_kv, sin_kv, normed_ref, inv_ref, q_ref, kv_ref):
    x = x_ref[...].astype(F32)
    inverse = lax.rsqrt(jnp.mean(x * x, axis=-1, keepdims=True) + EPS)
    normed = (x * inverse * gain_ref[...]).astype(BF16)
    normed_ref[...] = normed
    inv_ref[...] = inverse
    for s in range(Q_WIDTH // 256):
        part = jnp.dot(normed, w_ref[:, s * 256 : (s + 1) * 256], preferred_element_type=F32)
        for t in range(2):
            slab = part[:, t * SLAB : (t + 1) * SLAB]
            col = s * 256 + t * SLAB
            turned = slab * cos_q[...] + swap_halves(slab) * sin_q[...]
            q_ref[:, col : col + SLAB] = (turned.astype(BF16).astype(F32) * HEAD_DIM ** (-0.5)).astype(BF16)
    part = jnp.dot(normed, w_ref[:, Q_WIDTH : Q_WIDTH + 2 * KV_WIDTH], preferred_element_type=F32)
    for g in range(KV_HEADS):
        slab = part[:, g * SLAB : (g + 1) * SLAB]
        turned = slab * cos_kv[...] + swap_halves(slab) * sin_kv[...]
        kv_ref[:, g * SLAB : (g + 1) * SLAB] = turned.astype(BF16)


def qkv_project(x, gain, weight, tables):
    rows, width = x.shape
    return pl.pallas_call(
        qkv_kernel,
        out_shape=(
            jax.ShapeDtypeStruct((rows, width), BF16),
            jax.ShapeDtypeStruct((rows, 1), F32),
            jax.ShapeDtypeStruct((rows, Q_WIDTH), BF16),
            jax.ShapeDtypeStruct((rows, 2 * KV_WIDTH), BF16),
        ),
        compiler_params=pltpu.CompilerParams(vmem_limit_bytes=VMEM_LIMIT),
        name="qkv_project",
    )(x, gain, weight, *tables)


def heads_to_lanes(rows_part):
    turned = rows_part.T
    return jnp.concatenate(
        [turned[h * HEAD_DIM : (h + 1) * HEAD_DIM, :] for h in range(GROUP)], axis=1
    )


def lanes_to_heads(lanes_part):
    stacked = jnp.concatenate(
        [lanes_part[:, h * BLOCK : (h + 1) * BLOCK] for h in range(GROUP)], axis=0
    )
    return stacked.T


def causal(tile, block):
    key_pos = tile * KTILE + lax.broadcasted_iota(jnp.int32, (KTILE, LANES), 0)
    query_pos = block * BLOCK + lax.broadcasted_iota(jnp.int32, (KTILE, LANES), 1) % BLOCK
    return key_pos <= query_pos


def over_rows(left, right):
    return lax.dot_general(left, right, (((0,), (0,)), ((), ())), preferred_element_type=F32)


def attend_kernel(block_ref, q_ref, kv_ref, o_ref, total_ref):
    subs = q_ref.shape[0] // BLOCK
    for sub in range(subs):
        block = block_ref[sub]
        queries = heads_to_lanes(q_ref[sub * BLOCK : (sub + 1) * BLOCK, :].astype(F32))
        queries = jnp.concatenate([queries, jnp.zeros_like(queries)], axis=0).astype(BF16)

        def step(tile, carry, masked):
            top, total, acc = carry
            kv = kv_ref[pl.ds(pl.multiple_of(tile * KTILE, KTILE), KTILE), :]
            scores = jnp.dot(kv, queries, preferred_element_type=F32)
            if masked:
                scores = jnp.where(causal(tile, block), scores, -1e30)
            new_top = jnp.maximum(top, jnp.max(scores, axis=0, keepdims=True))
            decay = jnp.exp(top - new_top)
            probs = jnp.exp(scores - new_top)
            total = decay * total + jnp.sum(probs, axis=0, keepdims=True)
            acc = decay * acc + over_rows(kv, probs.astype(BF16))
            return (new_top, total, acc)

        start = (
            jnp.full((1, LANES), -1e30, F32),
            jnp.zeros((1, LANES), F32),
            jnp.zeros((SLAB, LANES), F32),
        )
        full = block * BLOCK // KTILE
        carry = lax.fori_loop(0, full, lambda t, c: step(t, c, False), start)
        top, total, acc = step(full, carry, True)
        out = acc[HEAD_DIM:, :] / total
        o_ref[sub * BLOCK : (sub + 1) * BLOCK, :] = lanes_to_heads(out).astype(BF16)
        total_ref[sub : sub + 1, :] = top + jnp.log(total)


def attend(blocks, q, kv_all):
    rows = q.shape[0]
    subs = rows // BLOCK
    return pl.pallas_call(
        attend_kernel,
        grid_spec=pltpu.PrefetchScalarGridSpec(
            num_scalar_prefetch=1,
            grid=(KV_HEADS,),
            in_specs=[
                pl.BlockSpec((rows, GROUP * HEAD_DIM), lambda g, b: (0, g)),
                pl.BlockSpec((LEN, SLAB), lambda g, b: (0, g)),
            ],
            out_specs=[
                pl.BlockSpec((rows, GROUP * HEAD_DIM), lambda g, b: (0, g)),
                pl.BlockSpec((None, subs, LANES), lambda g, b: (g, 0, 0)),
            ],
        ),
        out_shape=(
            jax.ShapeDtypeStruct((rows, Q_WIDTH), BF16),
            jax.ShapeDtypeStruct((KV_HEADS, subs, LANES), F32),
        ),
        compiler_params=pltpu.CompilerParams(vmem_limit_bytes=VMEM_LIMIT),
        cost_estimate=pl.CostEstimate(
            flops=60_000_000_000, bytes_accessed=8_000_000, transcendentals=6_000_000
        ),
        name="attend",
    )(blocks, q, kv_all)


def attend_back_kernel(height, *refs):
    if height:
        low_ref, grad_ref, proj_ref = refs[9:12]
        attend_back_body(refs[:9], grad_ref, refs[12:23], (height, low_ref, proj_ref, refs[23:]))
    else:
        attend_back_body(refs[:9], refs[9], refs[10:], None)


def attend_back_body(inputs, grad_ref, scratch, product):
    q_ref, kv_ref, o_ref, do_ref, total_ref, cos_q, sin_q, cos_kv, sin_kv = inputs
    (dkv_acc, own_part, twin_out, twin_in, sum_out, sum_in, mine) = scratch[:7]
    (twin_send, twin_recv, sum_send, sum_recv) = scratch[7:]
    subs = q_ref.shape[0] // BLOCK
    chips = lax.axis_size("mp") // 2
    me = lax.axis_index("mp")
    row = lax.axis_index("rows")
    chip = me // 2
    core = me % 2
    twin = (row, me + 1 - 2 * core)
    width = GROUP * HEAD_DIM

    barrier = pltpu.get_barrier_semaphore()
    pl.semaphore_signal(barrier, inc=1, device_id=twin, device_id_type=MESH)
    for step in range(1, chips):
        pl.semaphore_signal(
            barrier,
            inc=1,
            device_id=(row, 2 * ((chip + step) % chips) + core),
            device_id_type=MESH,
        )
    if product:
        down, across = row // 2, row % 2
        for device in ((row + 1 - 2 * across, me), ((1 - down) * 2 + across, me)):
            pl.semaphore_signal(barrier, inc=1, device_id=device, device_id_type=MESH)
    pl.semaphore_wait(barrier, chips + 2 if product else chips)
    if product:
        reducer = Reducer(product[0], o_ref, product[1], None, product[2], product[3])

    def twin_copy(g):
        return pltpu.make_async_remote_copy(
            src_ref=twin_out.at[g % 2],
            dst_ref=twin_in.at[g],
            send_sem=twin_send.at[g % 2],
            recv_sem=twin_recv.at[g],
            device_id=twin,
            device_id_type=MESH,
        )

    def sum_copy(g, step):
        return pltpu.make_async_remote_copy(
            src_ref=sum_out.at[g, step - 1],
            dst_ref=sum_in.at[g, step - 1],
            send_sem=sum_send.at[g, step - 1],
            recv_sem=sum_recv.at[g, step - 1],
            device_id=(row, 2 * ((chip + step) % chips) + core),
            device_id_type=MESH,
        )

    def combine(g):
        twin_copy(g).wait_recv()
        for step in range(1, chips):
            goal = (chip + step) % chips
            sum_out[g, step - 1] = (
                own_part[g % 2, goal] + twin_in[g, goal].astype(F32)
            ).astype(BF16)
            sum_copy(g, step).start()
        mine[g] = own_part[g % 2, chip] + twin_in[g, chip].astype(F32)

    def head_step(g, _):
        if product:
            reducer.round(g)
        cols = pl.ds(pl.multiple_of(g * width, width), width)
        pair = pl.ds(pl.multiple_of(g * SLAB, SLAB), SLAB)
        dkv_acc[...] = jnp.zeros_like(dkv_acc)
        for sub in range(subs):
            rows = slice(sub * BLOCK, (sub + 1) * BLOCK)
            block = natural(me, sub, subs)
            queries = heads_to_lanes(q_ref[rows, cols].astype(F32))
            grads = heads_to_lanes(do_ref[rows, cols].astype(F32))
            outs = heads_to_lanes(o_ref[rows, cols].astype(F32))
            delta = jnp.sum(grads * outs, axis=0, keepdims=True)
            empty = jnp.zeros_like(queries)
            queries = jnp.concatenate([queries, empty], axis=0)
            grads = jnp.concatenate([empty, grads], axis=0)
            query_rows = queries.T.astype(BF16)
            grad_rows = grads.T.astype(BF16)
            queries = queries.astype(BF16)
            grads = grads.astype(BF16)
            log_total = total_ref[g, sub : sub + 1, :]

            def step(tile, dq, masked):
                keys = pl.ds(pl.multiple_of(tile * KTILE, KTILE), KTILE)
                kv = kv_ref[keys, pair]
                scores = jnp.dot(kv, queries, preferred_element_type=F32)
                probs = jnp.exp(scores - log_total)
                if masked:
                    probs = jnp.where(causal(tile, block), probs, 0.0)
                grad_probs = jnp.dot(kv, grads, preferred_element_type=F32)
                grad_scores = (probs * (grad_probs - delta)).astype(BF16)
                dkv_acc[keys, :] += jnp.dot(
                    grad_scores, query_rows, preferred_element_type=F32
                ) + jnp.dot(probs.astype(BF16), grad_rows, preferred_element_type=F32)
                return dq + over_rows(kv, grad_scores)

            full = block * BLOCK // KTILE
            dq = lax.fori_loop(
                0, full, lambda t, c: step(t, c, False), jnp.zeros((SLAB, LANES), F32)
            )
            dq = step(full, dq, True)
            dq = lanes_to_heads(dq[:HEAD_DIM, :]) * HEAD_DIM ** (-0.5)
            for t in range(width // SLAB):
                slab = dq[:, t * SLAB : (t + 1) * SLAB]
                turned = slab * cos_q[rows, :] - swap_halves(slab) * sin_q[rows, :]
                first = pl.multiple_of(g * width + t * SLAB, SLAB)
                grad_ref[rows, pl.ds(first, SLAB)] = turned.astype(BF16)

        @pl.when(g >= 2)
        def _():
            twin_copy(g - 2).wait_send()

        for goal in range(chips):
            for sub in range(subs):
                first = natural(2 * goal + core, sub, subs) * BLOCK
                own_part[g % 2, goal, sub] = dkv_acc[pl.ds(pl.multiple_of(first, BLOCK), BLOCK), :]
                first = natural(2 * goal + 1 - core, sub, subs) * BLOCK
                twin_out[g % 2, goal, sub] = dkv_acc[
                    pl.ds(pl.multiple_of(first, BLOCK), BLOCK), :
                ].astype(BF16)
        twin_copy(g).start()

        @pl.when(g >= 1)
        def _():
            combine(g - 1)

        return 0

    lax.fori_loop(0, KV_HEADS, head_step, 0)
    combine(KV_HEADS - 1)
    if product:
        lax.fori_loop(KV_HEADS, chips + 3, reducer.round, 0)

    for g in range(KV_HEADS):
        total = mine[g]
        for step in range(1, chips):
            sum_copy(g, step).wait_recv()
            total = total + sum_in[g, step - 1].astype(F32)
        slab = total.reshape(subs * BLOCK, SLAB)
        turned = slab * cos_kv[...] - swap_halves(slab) * sin_kv[...]
        first = Q_WIDTH + g * SLAB
        grad_ref[:, first : first + SLAB] = turned.astype(BF16)
    for g in range(KV_HEADS):
        for step in range(1, chips):
            sum_copy(g, step).wait_send()
    for g in range(KV_HEADS - 2, KV_HEADS):
        twin_copy(g).wait_send()
    if product:
        reducer.close()


def attend_back(q, kv_all, o, grad_o, totals, tables, low):
    rows = q.shape[0]
    subs = rows // BLOCK
    chips = lax.axis_size("mp") // 2
    vmem = pl.BlockSpec(memory_space=pltpu.VMEM)
    dma = pltpu.SemaphoreType.DMA
    part = (chips, subs, BLOCK, SLAB)
    args = (q, kv_all, o, grad_o, totals, *tables)
    out_shape = (jax.ShapeDtypeStruct((rows, Q_WIDTH + 2 * KV_WIDTH), BF16),)
    height, more = 0, []
    if lax.axis_size("rows") == 4:
        height, product, more = reducer_buffers(o, low)
        args += (low,)
        out_shape += (product,)
    return pl.pallas_call(
        functools.partial(attend_back_kernel, height),
        in_specs=[vmem] * len(args),
        out_specs=(vmem,) * len(out_shape),
        out_shape=out_shape,
        scratch_shapes=[
            pltpu.VMEM((LEN, SLAB), F32),
            pltpu.VMEM((2,) + part, F32),
            pltpu.VMEM((2,) + part, BF16),
            pltpu.VMEM((KV_HEADS,) + part, BF16),
            pltpu.VMEM((KV_HEADS, chips - 1) + part[1:], BF16),
            pltpu.VMEM((KV_HEADS, chips - 1) + part[1:], BF16),
            pltpu.VMEM((KV_HEADS,) + part[1:], F32),
            dma((2,)),
            dma((KV_HEADS,)),
            dma((KV_HEADS, chips - 1)),
            dma((KV_HEADS, chips - 1)),
        ]
        + more,
        compiler_params=pltpu.CompilerParams(
            collective_id=3, has_side_effects=True, vmem_limit_bytes=VMEM_LIMIT
        ),
        cost_estimate=pl.CostEstimate(
            flops=120_000_000_000, bytes_accessed=12_000_000, transcendentals=6_000_000
        ),
        name="attend_back",
    )(*args)


def pack_kv(columns):
    lead = columns.shape[:-1]
    kv = columns[..., Q_WIDTH:].reshape(*lead, 2, KV_HEADS, HEAD_DIM)
    kv = jnp.swapaxes(kv, -3, -2).reshape(*lead, 2 * KV_WIDTH)
    return jnp.concatenate([columns[..., :Q_WIDTH], kv], axis=-1)


def unpack_kv(columns):
    lead = columns.shape[:-1]
    kv = columns[..., Q_WIDTH:].reshape(*lead, KV_HEADS, 2, HEAD_DIM)
    kv = jnp.swapaxes(kv, -3, -2).reshape(*lead, 2 * KV_WIDTH)
    return jnp.concatenate([columns[..., :Q_WIDTH], kv], axis=-1)


def dot(left, right):
    return jnp.dot(left, right, preferred_element_type=F32)


def dot_nt(left, right):
    return lax.dot_general(left, right, (((1,), (1,)), ((), ())), preferred_element_type=F32)


def dot_tn(left, right):
    return lax.dot_general(left, right, (((0,), (0,)), ((), ())), preferred_element_type=F32)


def half_of(ref, chip, core, sub, rows):
    subs = ref.shape[0] // (rows * lax.axis_size("mp"))
    start = natural(2 * chip + core, sub, subs) * rows
    return ref.at[pl.ds(pl.multiple_of(start, rows), rows)]


def part_of(ref, chip, core, sub, rows):
    subs = ref.shape[0] // (rows * lax.axis_size("mp"))
    start = (subs * (2 * chip + core) + sub) * rows
    return ref.at[pl.ds(pl.multiple_of(start, rows), rows)]


def ffn_kernel(
    subs,
    quad,
    scale_ref,
    x_ref,
    cot_ref,
    gate_ref,
    up_ref,
    down_ref,
    part_ref,
    part_in,
    relay_in,
    part_sum,
    sum_ref,
    gate_out,
    up_out,
    down_out,
    *rest,
):
    rest, weights, weight_sem = rest[:-4], rest[-4:-1], rest[-1]
    loads = [
        pltpu.make_async_copy(source, target, weight_sem.at[i])
        for i, (source, target) in enumerate(zip((gate_ref, up_ref, down_ref), weights))
    ]
    for copy in loads:
        copy.start()
    gate_ref, up_ref, down_ref = weights
    slots = rest[:9] if quad else ()
    scratch = rest[9:] if quad else rest
    ffn_body(
        subs,
        quad,
        slots,
        loads,
        scale_ref,
        x_ref,
        cot_ref,
        gate_ref,
        up_ref,
        down_ref,
        part_ref,
        part_in,
        relay_in,
        part_sum,
        sum_ref,
        gate_out,
        up_out,
        down_out,
        *scratch,
    )


def ffn_body(
    subs,
    quad,
    slots,
    loads,
    scale_ref,
    x_ref,
    cot_ref,
    gate_ref,
    up_ref,
    down_ref,
    part_ref,
    part_in,
    relay_in,
    part_sum,
    sum_ref,
    gate_out,
    up_out,
    down_out,
    x_all,
    hid,
    dgate,
    dup,
    cot_buf,
    part_own,
    twin_buf,
    twin_in,
    send_buf,
    sums_in,
    cot_cols,
    wide_buf,
    tall_buf,
    x_send,
    x_recv,
    twin_x_send,
    twin_x_recv,
    twin_send,
    twin_recv,
    sum_send,
    sum_recv,
    p_send,
    p_recv,
    relay_recv,
    relay_sem,
    cot_sem,
    part_sem,
    cols_sem,
    out_sem,
    *row_scratch,
):
    chips = lax.axis_size("mp") // 2
    me = lax.axis_index("mp")
    row = lax.axis_index("rows")
    chip = me // 2
    core = me % 2
    rows = x_ref.shape[0] // subs
    units = chips * subs
    twin = (row, me + 1 - 2 * core)

    def on_chip(other):
        return (row, 2 * other + core)

    barrier = pltpu.get_barrier_semaphore()
    pl.semaphore_signal(barrier, inc=1, device_id=twin, device_id_type=MESH)
    for step in range(1, chips):
        pl.semaphore_signal(
            barrier, inc=1, device_id=on_chip((chip + step) % chips), device_id_type=MESH
        )
    down, across = row // 2, row % 2
    beside_row = row + 1 - 2 * across
    above_row = (1 - down) * 2 + across
    neighbours = ((beside_row, me), (above_row, me))
    if quad:
        for device in neighbours:
            pl.semaphore_signal(barrier, inc=1, device_id=device, device_id_type=MESH)
    pl.semaphore_wait(barrier, chips + 2 if quad else chips)

    def order(i):
        near = jnp.minimum(chip, chips - 1 - chip)
        long_side = jnp.where(chip < chips - 1 - chip, 1, -1)
        j = i - subs
        paired = j < 2 * subs * near
        rest = j - 2 * subs * near
        dist = jnp.where(paired, j // (2 * subs) + 1, near + 1 + rest // subs)
        sub = jnp.where(paired, (j % (2 * subs)) // 2, rest % subs)
        side = jnp.where(paired, 1 - 2 * (j % 2), long_side)
        own = i < subs
        return (jnp.where(own, chip, chip + side * dist), jnp.where(own, i, sub))

    def x_copy(other, sub, side, source=None):
        spot = half_of(x_all, other, core, sub, rows)
        return pltpu.make_async_remote_copy(
            src_ref=spot if source is None else source,
            dst_ref=spot,
            send_sem=x_send.at[(side + 1) // 2, other * subs + sub],
            recv_sem=x_recv.at[other * subs + sub],
            device_id=on_chip(chip + side),
            device_id_type=MESH,
        )

    def twin_x_copy(other, sub, source=None):
        spot = half_of(x_all, other, core, sub, rows)
        return pltpu.make_async_remote_copy(
            src_ref=spot if source is None else source,
            dst_ref=spot,
            send_sem=twin_x_send.at[other * subs + sub],
            recv_sem=twin_x_recv.at[other * subs + sub],
            device_id=twin,
            device_id_type=MESH,
        )

    def twin_sum_copy(slot):
        return pltpu.make_async_remote_copy(
            src_ref=twin_buf.at[slot],
            dst_ref=twin_in.at[slot],
            send_sem=twin_send.at[slot],
            recv_sem=twin_recv.at[slot],
            device_id=twin,
            device_id_type=MESH,
        )

    def sum_copy(other, sub):
        side = jnp.where(other > chip, 1, -1)
        slot = jnp.where((side == 1) & (other == chip + 1), chips, other)
        return pltpu.make_async_remote_copy(
            src_ref=send_buf.at[other * subs + sub],
            dst_ref=sums_in.at[slot, sub],
            send_sem=sum_send.at[other * subs + sub],
            recv_sem=sum_recv.at[slot, sub],
            device_id=on_chip(chip + side),
            device_id_type=MESH,
        )

    def sum_arrival(slot, sub):
        return pltpu.make_async_remote_copy(
            src_ref=send_buf.at[0],
            dst_ref=sums_in.at[slot, sub],
            send_sem=sum_send.at[0],
            recv_sem=sum_recv.at[slot, sub],
            device_id=twin,
            device_id_type=MESH,
        )

    def cot_copies(other, sub, slot):
        return [
            pltpu.make_async_copy(
                half_of(cot_ref, other, c, sub, rows),
                cot_buf.at[slot, pl.ds(c * rows, rows)],
                cot_sem.at[slot, c],
            )
            for c in range(2)
        ]

    def part_copy(i):
        other, sub = order(i)
        return pltpu.make_async_copy(
            part_own.at[i % 2], part_ref.at[other * subs + sub], part_sem.at[i % 2]
        )

    for sub in range(subs):
        source = x_ref.at[pl.ds(sub * rows, rows)]

        @pl.when(chip < chips - 1)
        def _():
            x_copy(chip, sub, 1, source).start()

        @pl.when(chip > 0)
        def _():
            x_copy(chip, sub, -1, source).start()

        twin_x_copy(chip, sub, source).start()
    for copy in cot_copies(chip, 0, 0):
        copy.start()
    for sub in range(subs):
        half_of(x_all, chip, core, sub, rows)[...] = x_ref[sub * rows : (sub + 1) * rows, :]

    def reduce_unit(i):
        other, sub = order(i)
        unit = other * subs + sub
        slot = i % 2
        twin_sum_copy(slot).wait_recv()
        part_own[slot] = (
            part_own[slot].astype(F32) + twin_in[slot, 1].astype(F32)
        ).astype(BF16)
        part_copy(i).start()
        arrived = twin_in[slot, 0].astype(F32)
        lines = pl.ds(pl.multiple_of(sub * rows, rows), rows)

        @pl.when(other == chip)
        def _():
            sum_ref[lines, :] = sum_ref[lines, :] + arrived

        @pl.when(other != chip)
        def _():
            send_buf[unit] = (send_buf[unit].astype(F32) + arrived).astype(BF16)

        @pl.when(((other > chip) & (chip == 0)) | ((other < chip) & (chip == chips - 1)))
        def _():
            sum_copy(other, sub).start()

    def pass_on(e):
        right, left = chips - 1 - chip, chip
        right_first = chip < chips // 2
        ahead = jnp.where(right_first, right, left)
        step = jnp.where(e < ahead, e + 1, e - ahead + 1)
        toward = jnp.where((e < ahead) == right_first, 1, -1)
        other = chip + toward * step

        @pl.when((chip > 0) & (chip < chips - 1))
        def _():
            for sub in range(subs):
                unit = other * subs + sub
                sum_arrival(other, sub).wait_recv()
                send_buf[unit] = (
                    send_buf[unit].astype(F32) + sums_in[other, sub].astype(F32)
                ).astype(BF16)
                sum_copy(other, sub).start()

    def unit_step(i, _):
        other, sub = order(i)
        slot = i % 2

        @pl.when(i + 1 < units)
        def _():
            for copy in cot_copies(*order(i + 1), 1 - slot):
                copy.start()

        @pl.when(other != chip)
        def _():
            x_copy(other, sub, 1).wait_recv()
            twin_x_copy(other, sub).start()

            @pl.when((other > chip) & (chip > 0))
            def _():
                x_copy(other, sub, -1).start()

            @pl.when((other < chip) & (chip < chips - 1))
            def _():
                x_copy(other, sub, 1).start()

        twin_x_copy(other, sub).wait_recv()
        for copy in cot_copies(other, sub, slot):
            copy.wait()
        halves = [half_of(x_all, other, c, sub, rows)[...] for c in range(2)]
        x = jnp.concatenate(halves, axis=0)
        gate = dot(x, gate_ref[...])
        up = dot(x, up_ref[...])
        grad = dot_nt(cot_buf[slot], down_ref[...]) * scale_ref[0]
        sig = 1.0 / (1.0 + jnp.exp(-gate))
        act = gate * sig
        h = (act * up).astype(BF16)
        dg = (grad * up * (sig * (1.0 + gate * (1.0 - sig)))).astype(BF16)
        du = (grad * act).astype(BF16)
        for c in range(2):
            piece = slice(c * rows, (c + 1) * rows)
            half_of(hid, other, c, sub, rows)[...] = h[piece]
            half_of(dgate, other, c, sub, rows)[...] = dg[piece]
            half_of(dup, other, c, sub, rows)[...] = du[piece]

        @pl.when(i >= 2)
        def _():
            part_copy(i - 2).wait()
            twin_sum_copy(slot).wait_send()

        part = dot(h, down_ref[...])

        def keep_part(own, away):
            part_own[slot] = own.astype(BF16)
            twin_buf[slot, 1] = away.astype(BF16)

        @pl.when(core == 0)
        def _():
            keep_part(part[:rows], part[rows:])

        @pl.when(core == 1)
        def _():
            keep_part(part[rows:], part[:rows])

        dx = dot_nt(dg, gate_ref[...]) + dot_nt(du, up_ref[...])

        def keep(own, away):
            twin_buf[slot, 0] = away.astype(BF16)

            @pl.when(other == chip)
            def _():
                sum_ref[pl.ds(pl.multiple_of(sub * rows, rows), rows), :] = own

            @pl.when(other != chip)
            def _():
                send_buf[other * subs + sub] = own.astype(BF16)

        @pl.when(core == 0)
        def _():
            keep(dx[:rows], dx[rows:])

        @pl.when(core == 1)
        def _():
            keep(dx[rows:], dx[:rows])

        twin_sum_copy(slot).start()

        @pl.when(i >= 1)
        def _():
            reduce_unit(i - 1)

        return 0

    for copy in loads:
        copy.wait()
    lax.fori_loop(0, units, unit_step, 0)
    reduce_unit(units - 1)
    for i in (units - 2, units - 1):
        part_copy(i).wait()
        twin_sum_copy(i % 2).wait_send()

    width = x_ref.shape[1]
    ff = gate_ref.shape[1]
    tall = tall_buf.shape[1]
    narrow = tall_buf.shape[2]
    down_cols = cot_cols.shape[2]
    col_steps = width // down_cols
    pieces = width // tall
    steps = pieces * (ff // narrow)
    wholes = (gate_out, up_out, down_out)

    if quad:
        firsts, seconds, finals = slots[0:3], slots[3:6], slots[6:9]
        tall_in, wide_in, moved, one_send, one_recv, two_send, two_recv, load_sem, fin_sem = (
            row_scratch[:2] + (row_scratch[2:5],) + row_scratch[5:]
        )

    def remote(source, dest, send, recv, device):
        return pltpu.make_async_remote_copy(
            src_ref=source,
            dst_ref=dest,
            send_sem=send,
            recv_sem=recv,
            device_id=device,
            device_id_type=MESH,
        )

    def block_at(a, block, d):
        high, wide = firsts[a].shape[2:]
        lines = pl.ds(pl.multiple_of(block * high, high), high)
        return wholes[a].at[lines, pl.ds(d * wide, wide)]

    def one_copy(a, d, k):
        block = k * 2 + 1 - across if d == 0 else (1 - down) * 2 + k
        return remote(
            block_at(a, block, d),
            firsts[a].at[d, k],
            one_send.at[a, d, k],
            one_recv.at[a, d, k],
            neighbours[d],
        )

    def two_copy(a, d):
        return remote(
            moved[a].at[d],
            seconds[a].at[d],
            two_send.at[a, d],
            two_recv.at[a, d],
            neighbours[1 - d],
        )

    def fin_copy(a, d):
        wide = firsts[a].shape[3]
        return pltpu.make_async_copy(
            (wide_in if a == 2 else tall_in).at[0],
            finals[a].at[:, pl.ds(d * wide, wide)],
            fin_sem.at[d],
        )

    def load(sources, buf):
        copies = [
            pltpu.make_async_copy(source, buf.at[i], load_sem.at[i])
            for i, source in enumerate(sources)
        ]
        for copy in copies:
            copy.start()
        for copy in copies:
            copy.wait()

    def stage_two(a):
        if quad:
            buf = wide_in if a == 2 else tall_in
            for d in range(2):
                for k in range(2):
                    one_copy(a, d, k).wait_recv()
                block = above_row if d == 0 else beside_row
                other = 1 - down if d == 0 else 1 - across
                load([block_at(a, block, d), firsts[a].at[d, other]], buf)
                moved[a][d] = (buf[0].astype(F32) + buf[1].astype(F32)).astype(BF16)
                two_copy(a, d).start()

    def stage_three(a):
        if quad:
            buf = wide_in if a == 2 else tall_in
            for d in range(2):
                two_copy(a, d).wait_recv()
                other = down if d == 0 else across
                load([block_at(a, row, d), firsts[a].at[d, other], seconds[a].at[d]], buf)
                buf[0] = (
                    buf[0].astype(F32) + buf[1].astype(F32) + buf[2].astype(F32)
                ).astype(BF16)
                fin_copy(a, d).start()
                fin_copy(a, d).wait()

    def end_far(source, other):
        return ((source == 0) & (other >= 2)) | ((source == chips - 1) & (other <= chips - 3))

    def relayed(source, other):
        return ((source == 1) & (other >= 2)) | ((source == chips - 2) & (other <= chips - 3))

    def p_copy(other, sub, source=None):
        return remote(
            part_ref.at[other * subs + sub] if source is None else source,
            part_in.at[chip, sub],
            p_send.at[other * subs + sub],
            p_recv.at[chip, sub],
            on_chip(other),
        )

    def relay_copy(other, sub):
        return remote(
            part_ref.at[other * subs + sub],
            relay_in.at[other, sub],
            p_send.at[other * subs + sub],
            relay_recv.at[other, sub],
            on_chip(jnp.where(chip == 0, 1, chips - 2)),
        )

    def send_parts(far):
        if True:
            for step in range(1, chips):
                other = (chip + step) % chips
                beyond = end_far(chip, other)
                for sub in range(subs):
                    if far:

                        @pl.when(beyond)
                        def _():
                            relay_copy(other, sub).start()

                    else:

                        @pl.when(jnp.logical_not(beyond | relayed(chip, other)))
                        def _():
                            p_copy(other, sub).start()

    def piece(index):
        return cot_buf.at[index // 2, pl.ds(index % 2 * rows, rows)]

    def fetch(source, index):
        copy = pltpu.make_async_copy(source, piece(index), relay_sem.at[index])
        copy.start()
        return copy

    def relay_parts():
        for step in range(1, chips):
            other = (chip + step) % chips

            @pl.when(relayed(chip, other))
            def _():
                for sub in range(subs):
                    mine = fetch(part_ref.at[other * subs + sub], 2 * sub)
                    remote(
                        part_ref.at[0],
                        relay_in.at[other, sub],
                        p_send.at[0],
                        relay_recv.at[other, sub],
                        twin,
                    ).wait_recv()
                    theirs = fetch(relay_in.at[other, sub], 2 * sub + 1)
                    mine.wait()
                    theirs.wait()
                    part_ref_sum = piece(2 * sub)[...].astype(F32) + piece(2 * sub + 1)[
                        ...
                    ].astype(F32)
                    piece(2 * sub)[...] = part_ref_sum.astype(BF16)
                    back = pltpu.make_async_copy(
                        piece(2 * sub), part_ref.at[other * subs + sub], relay_sem.at[2 * sub]
                    )
                    back.start()
                    back.wait()
                    p_copy(other, sub).start()

    def total_parts():
        for sub in range(subs):
            lines = slice(sub * rows, (sub + 1) * rows)
            for base in range(1, chips, 3):
                group = range(base, min(base + 3, chips))
                if base == 1:
                    mine = fetch(part_ref.at[chip * subs + sub], 0)
                for step in group:
                    other = (chip + step) % chips

                    @pl.when(jnp.logical_not(end_far(other, chip)))
                    def _():
                        remote(
                            part_ref.at[0],
                            part_in.at[other, sub],
                            p_send.at[0],
                            p_recv.at[other, sub],
                            twin,
                        ).wait_recv()
                        fetch(part_in.at[other, sub], step - base + 1)

                if base == 1:
                    mine.wait()
                    part_sum[lines, :] = piece(0)[...].astype(F32)
                for step in group:
                    other = (chip + step) % chips
                    index = step - base + 1

                    @pl.when(jnp.logical_not(end_far(other, chip)))
                    def _():
                        pltpu.make_async_copy(
                            part_in.at[other, sub], piece(index), relay_sem.at[index]
                        ).wait()
                        part_sum[lines, :] = part_sum[lines, :] + piece(index)[...].astype(F32)

    def spread_blocks(a, source):
        def where(j):
            d, k = j % 2, (j // 2) % 2
            first = jnp.where(d == 0, k * 2 + 1 - across, (1 - down) * 2 + k)
            late = jnp.where(j < 6, jnp.where(d == 0, above_row, beside_row), row)
            return jnp.where(j < 4, first, late), d, k

        def place(ref, block, d):
            lines = pl.ds(pl.multiple_of(block * tall, tall), tall)
            return ref.at[lines, pl.ds(pl.multiple_of(d * narrow, narrow), narrow)]

        def block_out(j):
            block, d, _ = where(j)
            return pltpu.make_async_copy(
                tall_buf.at[j % 2], place(wholes[a], block, d), out_sem.at[j % 2]
            )

        def block_send(j):
            block, d, k = where(j)
            target = jnp.where(d == 0, beside_row, above_row)
            return remote(
                place(wholes[a], block, d),
                firsts[a].at[d, k],
                one_send.at[a, d, k],
                one_recv.at[a, d, k],
                (target, me),
            )

        def block_step(j, _):
            block, d, _ = where(j)
            lines = pl.ds(pl.multiple_of(block * tall, tall), tall)
            cols = pl.ds(pl.multiple_of(d * narrow, narrow), narrow)
            tall_buf[j % 2] = dot_tn(x_all[:, lines], source[:, cols]).astype(BF16)

            @pl.when(j >= 1)
            def _():
                block_out(j - 1).wait()

            @pl.when((j >= 1) & (j <= 4))
            def _():
                block_send(j - 1).start()

            block_out(j).start()
            return 0

        lax.fori_loop(0, 8, block_step, 0)
        block_out(7).wait()

    send_parts(True)
    for a, source in enumerate((dgate, dup)):

        def tall_out(j):
            first = pl.multiple_of(j % pieces * tall, tall)
            col = pl.multiple_of(j // pieces * narrow, narrow)
            return pltpu.make_async_copy(
                tall_buf.at[j % 2],
                wholes[a].at[pl.ds(first, tall), pl.ds(col, narrow)],
                out_sem.at[j % 2],
            )

        def tall_step(j, _):
            @pl.when(j >= 2)
            def _():
                tall_out(j - 2).wait()

            first = pl.multiple_of(j % pieces * tall, tall)
            col = pl.multiple_of(j // pieces * narrow, narrow)
            tall_buf[j % 2] = dot_tn(
                x_all[:, pl.ds(first, tall)], source[:, pl.ds(col, narrow)]
            ).astype(BF16)
            tall_out(j).start()
            return 0

        if quad:
            spread_blocks(a, source)
        else:
            lax.fori_loop(0, steps, tall_step, 0)
            for j in range(steps - 2, steps):
                tall_out(j).wait()
        for e in range(a * (chips - 1) // 3, (a + 1) * (chips - 1) // 3):
            pass_on(e)
    send_parts(False)

    def cols_copy(j):
        return pltpu.make_async_copy(
            cot_ref.at[:, pl.ds(pl.multiple_of(j * down_cols, down_cols), down_cols)],
            cot_cols.at[j % 2],
            cols_sem.at[j % 2],
        )

    def wide_out(j):
        return pltpu.make_async_copy(
            wide_buf.at[j % 2],
            down_out.at[:, pl.ds(pl.multiple_of(j * down_cols, down_cols), down_cols)],
            out_sem.at[j % 2],
        )

    cols_copy(0).start()

    def down_step(j, _):
        @pl.when(j + 1 < col_steps)
        def _():
            cols_copy(j + 1).start()

        cols_copy(j).wait()

        @pl.when(j >= 2)
        def _():
            wide_out(j - 2).wait()

        if quad:

            @pl.when(j == col_steps // 2 + 1)
            def _():
                for k in range(2):
                    one_copy(2, 0, k).start()

        wide_buf[j % 2] = (dot_tn(hid[...], cot_cols[j % 2]) * scale_ref[0]).astype(BF16)
        wide_out(j).start()
        return 0

    lax.fori_loop(0, col_steps, down_step, 0)
    for j in range(max(0, col_steps - 2), col_steps):
        wide_out(j).wait()
    if quad:
        for k in range(2):
            one_copy(2, 1, k).start()
    for e in range(2 * (chips - 1) // 3, chips - 1):
        pass_on(e)
    stage_two(0)
    relay_parts()
    stage_two(1)
    stage_three(0)
    stage_two(2)
    stage_three(1)
    stage_three(2)
    total_parts()
    if quad:
        for a in range(3):
            for d in range(2):
                two_copy(a, d).wait_send()
                for k in range(2):
                    one_copy(a, d, k).wait_send()

    for sub in range(subs):
        lines = slice(sub * rows, (sub + 1) * rows)

        @pl.when(chip < chips - 1)
        def _():
            sum_arrival(chip, sub).wait_recv()
            sum_ref[lines, :] = sum_ref[lines, :] + sums_in[chip, sub].astype(F32)

        @pl.when(chip > 0)
        def _():
            sum_arrival(chips, sub).wait_recv()
            sum_ref[lines, :] = sum_ref[lines, :] + sums_in[chips, sub].astype(F32)

    def finish(i, _):
        other, sub = order(i)
        twin_x_copy(other, sub).wait_send()

        @pl.when(((other >= chip) & (chip > 0)))
        def _():
            x_copy(other, sub, -1).wait_send()

        @pl.when(((other <= chip) & (chip < chips - 1)))
        def _():
            x_copy(other, sub, 1).wait_send()

        @pl.when(other != chip)
        def _():
            sum_copy(other, sub).wait_send()
            p_copy(other, sub).wait_send()

        return 0

    lax.fori_loop(0, units, finish, 0)


def ffn(scale, x, cot_all, gate_weight, up_weight, down_weight):
    tokens, width = cot_all.shape
    rows_dev = x.shape[0]
    chips = lax.axis_size("mp") // 2
    ff = gate_weight.shape[1]
    subs = max(1, rows_dev // BLOCK)
    rows = rows_dev // subs
    units = chips * subs
    quad = lax.axis_size("rows") == 4
    narrow = ff // 2 if quad else ff // 3
    tall = width // 4
    down_cols = 256
    extra_out, row_scratch = (), []
    vmem = pl.BlockSpec(memory_space=pltpu.VMEM)
    hbm = pl.BlockSpec(memory_space=pl.ANY)
    dma = pltpu.SemaphoreType.DMA
    if quad:
        sizes = ((width // 4, ff // 2), (width // 4, ff // 2), (ff // 4, width // 2))
        extra_out = (
            tuple(jax.ShapeDtypeStruct((2, 2, *size), BF16) for size in sizes)
            + tuple(jax.ShapeDtypeStruct((2, *size), BF16) for size in sizes)
            + tuple(jax.ShapeDtypeStruct((size[0], 2 * size[1]), BF16) for size in sizes)
        )
        row_scratch = (
            [pltpu.VMEM((3, *sizes[0]), BF16), pltpu.VMEM((3, *sizes[2]), BF16)]
            + [pltpu.VMEM((2, *size), BF16) for size in sizes]
            + [dma((3, 2, 2)), dma((3, 2, 2)), dma((3, 2)), dma((3, 2)), dma((3,)), dma((2,))]
        )
    out = pl.pallas_call(
        functools.partial(ffn_kernel, subs, quad),
        out_shape=(
            jax.ShapeDtypeStruct((units, rows, width), BF16),
            jax.ShapeDtypeStruct((chips, subs, rows, width), BF16),
            jax.ShapeDtypeStruct((chips, subs, rows, width), BF16),
            jax.ShapeDtypeStruct((rows_dev, width), F32),
            jax.ShapeDtypeStruct((rows_dev, width), F32),
            jax.ShapeDtypeStruct((width, ff), BF16),
            jax.ShapeDtypeStruct((width, ff), BF16),
            jax.ShapeDtypeStruct((ff, width), BF16),
        )
        + extra_out,
        in_specs=[pl.BlockSpec(memory_space=pltpu.SMEM), vmem, hbm, hbm, hbm, hbm],
        out_specs=(hbm, hbm, hbm, vmem, vmem, hbm, hbm, hbm) + (hbm,) * len(extra_out),
        scratch_shapes=[
            pltpu.VMEM((tokens, width), BF16),
            pltpu.VMEM((tokens, ff), BF16),
            pltpu.VMEM((tokens, ff), BF16),
            pltpu.VMEM((tokens, ff), BF16),
            pltpu.VMEM((2, 2 * rows, width), BF16),
            pltpu.VMEM((2, rows, width), BF16),
            pltpu.VMEM((2, 2, rows, width), BF16),
            pltpu.VMEM((2, 2, rows, width), BF16),
            pltpu.VMEM((units, rows, width), BF16),
            pltpu.VMEM((chips + 1, subs, rows, width), BF16),
            pltpu.VMEM((2, tokens, down_cols), BF16),
            pltpu.VMEM((2, ff, down_cols), BF16),
            pltpu.VMEM((2, tall, narrow), BF16),
            dma((2, units)),
            dma((units,)),
            dma((units,)),
            dma((units,)),
            dma((2,)),
            dma((2,)),
            dma((units,)),
            dma((chips + 1, subs)),
            dma((units,)),
            dma((chips, subs)),
            dma((chips, subs)),
            dma((4,)),
            dma((2, 2)),
            dma((2,)),
            dma((2,)),
            dma((2,)),
        ]
        + row_scratch
        + [
            pltpu.VMEM((width, ff), BF16),
            pltpu.VMEM((width, ff), BF16),
            pltpu.VMEM((ff, width), BF16),
            dma((3,)),
        ],
        compiler_params=pltpu.CompilerParams(
            collective_id=1, has_side_effects=True, vmem_limit_bytes=VMEM_LIMIT
        ),
        cost_estimate=pl.CostEstimate(
            flops=60_000_000_000, bytes_accessed=60_000_000, transcendentals=2_000_000
        ),
        name="ffn",
    )(scale.reshape(1), x, cot_all, gate_weight, up_weight, down_weight)
    if quad:
        shards = out[14:17]
    else:
        shards = [lax.psum(part, "rows") for part in out[5:8]]
    return (*out[3:5], *shards)


class Reducer:
    def __init__(self, height, left, right, gains, out, bufs):
        self.height, self.right, self.gains, self.out = height, right, gains, out
        (self.turned, self.own, self.twin_out, self.twin_in, self.out1, self.in1) = bufs[:6]
        (self.out2, self.in2, self.out3, self.in3) = bufs[6:10]
        (self.s0, self.r0, self.s1, self.r1, self.s2, self.r2, self.s3) = bufs[10:]
        self.cols = self.own.shape[-1]
        self.chips = lax.axis_size("mp") // 2
        me = lax.axis_index("mp")
        self.row = lax.axis_index("rows")
        self.chip, self.core = me // 2, me % 2
        self.down, self.across = self.row // 2, self.row % 2
        self.twin = (self.row, me + 1 - 2 * self.core)
        self.beside = (self.row + 1 - 2 * self.across, me)
        self.above = ((1 - self.down) * 2 + self.across, me)
        self.turned[...] = left[...].T

    def remote(self, source, dest, send, recv, device):
        return pltpu.make_async_remote_copy(
            src_ref=source,
            dst_ref=dest,
            send_sem=send,
            recv_sem=recv,
            device_id=device,
            device_id_type=MESH,
        )

    def goal(self, i):
        return (self.chip + 1 + i) % self.chips

    def twin_copy(self, i):
        return self.remote(
            self.twin_out.at[i], self.twin_in.at[i], self.s0.at[i], self.r0.at[i], self.twin
        )

    def first_copy(self, i, d):
        return self.remote(
            self.out1.at[i, d],
            self.in1.at[i, d],
            self.s1.at[i, d],
            self.r1.at[i, d],
            (self.beside, self.above)[d],
        )

    def second_copy(self, i, d):
        return self.remote(
            self.out2.at[i, d],
            self.in2.at[i, d],
            self.s2.at[i, d],
            self.r2.at[i, d],
            (self.above, self.beside)[d],
        )

    def last_copy(self, i):
        return self.remote(
            self.out3.at[i],
            self.in3.at[i],
            self.s3.at[0, i],
            self.s3.at[1, i],
            (self.row, 2 * self.goal(i) + self.core),
        )

    def make(self, i):
        height = self.height
        for r in range(4):
            first = (r * self.chips + self.goal(i)) * 2 * height
            lines = pl.ds(pl.multiple_of(first, 16), 2 * height)
            block = dot(self.turned[lines, :], self.right[...])
            spare = self.cols - block.shape[1]
            if spare:
                piece = self.gains[:, pl.ds(pl.multiple_of(first, 128), 2 * height)]
                piece = jnp.concatenate(
                    [piece, jnp.zeros((spare - piece.shape[0], 2 * height), F32)], axis=0
                ).T
                block = jnp.concatenate([block, piece], axis=1)

            @pl.when(self.core == 0)
            def _():
                self.own[i, r] = block[:height]
                self.twin_out[i, r] = block[height:].astype(BF16)

            @pl.when(self.core == 1)
            def _():
                self.own[i, r] = block[height:]
                self.twin_out[i, r] = block[:height].astype(BF16)

        self.twin_copy(i).start()

    def first_stage(self, i):
        half = self.cols // 2
        own = self.own
        self.twin_copy(i).wait_recv()
        for r in range(4):
            own[i, r] = own[i, r] + self.twin_in[i, r].astype(F32)
        for k in range(2):
            self.out1[i, 0, k] = own[i, k * 2 + 1 - self.across, :, :half].astype(BF16)
            self.out1[i, 1, k] = own[i, (1 - self.down) * 2 + k, :, half:].astype(BF16)
        for d in range(2):
            self.first_copy(i, d).start()

    def second_stage(self, i):
        half = self.cols // 2
        for d in range(2):
            self.first_copy(i, d).wait_recv()
        above = (1 - self.down) * 2 + self.across
        beside = self.down * 2 + 1 - self.across
        self.out2[i, 0] = (
            self.own[i, above, :, :half] + self.in1[i, 0, 1 - self.down].astype(F32)
        ).astype(BF16)
        self.out2[i, 1] = (
            self.own[i, beside, :, half:] + self.in1[i, 1, 1 - self.across].astype(F32)
        ).astype(BF16)
        for d in range(2):
            self.second_copy(i, d).start()

    def third_stage(self, i):
        half = self.cols // 2
        for d in range(2):
            self.second_copy(i, d).wait_recv()
        left = (
            self.own[i, self.row, :, :half]
            + self.in1[i, 0, self.down].astype(F32)
            + self.in2[i, 0].astype(F32)
        )
        right = (
            self.own[i, self.row, :, half:]
            + self.in1[i, 1, self.across].astype(F32)
            + self.in2[i, 1].astype(F32)
        )

        @pl.when(i < self.chips - 1)
        def _():
            self.out3[i, :, :half] = left.astype(BF16)
            self.out3[i, :, half:] = right.astype(BF16)
            self.last_copy(i).start()

        @pl.when(i == self.chips - 1)
        def _():
            self.out[:, :half] = left
            self.out[:, half:] = right

    def round(self, n, _=None):
        stages = (self.make, self.first_stage, self.second_stage, self.third_stage)
        for stage, work in enumerate(stages):

            @pl.when((n >= stage) & (n < self.chips + stage))
            def _():
                work(n - stage)

        return 0

    def close(self):
        for i in range(self.chips - 1):
            self.last_copy(i).wait_recv()
            self.out[...] = self.out[...] + self.in3[i].astype(F32)

        def finish(i, _):
            self.twin_copy(i).wait_send()
            for d in range(2):
                self.first_copy(i, d).wait_send()
                self.second_copy(i, d).wait_send()

            @pl.when(i < self.chips - 1)
            def _():
                self.last_copy(i).wait_send()

            return 0

        lax.fori_loop(0, self.chips, finish, 0)


def reducer_buffers(left, right):
    chips = lax.axis_size("mp") // 2
    shards = lax.axis_size("rows") * lax.axis_size("mp")
    height = left.shape[1] // shards
    cols = -(-right.shape[1] // 256) * 256
    half = cols // 2
    dma = pltpu.SemaphoreType.DMA
    return (
        height,
        jax.ShapeDtypeStruct((height, cols), F32),
        [
            pltpu.VMEM((left.shape[1], left.shape[0]), BF16),
            pltpu.VMEM((chips, 4, height, cols), F32),
            pltpu.VMEM((chips, 4, height, cols), BF16),
            pltpu.VMEM((chips, 4, height, cols), BF16),
            pltpu.VMEM((chips, 2, 2, height, half), BF16),
            pltpu.VMEM((chips, 2, 2, height, half), BF16),
            pltpu.VMEM((chips, 2, height, half), BF16),
            pltpu.VMEM((chips, 2, height, half), BF16),
            pltpu.VMEM((chips - 1, height, cols), BF16),
            pltpu.VMEM((chips - 1, height, cols), BF16),
            dma((chips,)),
            dma((chips,)),
            dma((chips, 2)),
            dma((chips, 2)),
            dma((chips, 2)),
            dma((chips, 2)),
            dma((2, chips)),
        ],
    )


def reduce_kernel(height, left, right, gains, half_ref, low_ref, out, swapped, wide_ref, *bufs):
    bufs, (land, low_buf, wide_buf, swap_sems, low_sems, wide_sems) = bufs[:-6], bufs[-6:]
    mp = lax.axis_size("mp")
    chips = mp // 2
    me = lax.axis_index("mp")
    row = lax.axis_index("rows")
    chip, core = me // 2, me % 2
    down, across = row // 2, row % 2
    mirror = (row, mp - 1 - me)
    barrier = pltpu.get_barrier_semaphore()
    devices = [
        mirror,
        (row, me + 1 - 2 * core),
        (row + 1 - 2 * across, me),
        ((1 - down) * 2 + across, me),
    ] + [(row, 2 * ((chip + step) % chips) + core) for step in range(1, chips)]
    for device in devices:
        pl.semaphore_signal(barrier, inc=1, device_id=device, device_id_type=MESH)
    pl.semaphore_wait(barrier, chips + 3)
    swap = pltpu.make_async_remote_copy(
        src_ref=half_ref,
        dst_ref=land,
        send_sem=swap_sems.at[0],
        recv_sem=swap_sems.at[1],
        device_id=mirror,
        device_id_type=MESH,
    )
    swap.start()
    reducer = Reducer(height, left, right, gains, out, bufs)
    tall = low_buf.shape[1]
    pieces = low_ref.shape[0] // tall

    def low_copy(j):
        lines = pl.ds(pl.multiple_of(j * tall, tall), tall)
        return pltpu.make_async_copy(low_ref.at[lines], low_buf.at[j % 2], low_sems.at[j % 2])

    def wide_copy(j):
        lines = pl.ds(pl.multiple_of(j * tall, tall), tall)
        return pltpu.make_async_copy(wide_buf.at[j % 2], wide_ref.at[lines], wide_sems.at[j % 2])

    def widen(j, _=None):
        @pl.when(j + 1 < pieces)
        def _():
            low_copy(j + 1).start()

        low_copy(j).wait()

        @pl.when(j >= 2)
        def _():
            wide_copy(j - 2).wait()

        wide_buf[j % 2] = low_buf[j % 2].astype(F32)
        wide_copy(j).start()
        return 0

    low_copy(0).start()

    def both(n, _):
        reducer.round(n)
        widen(n)
        return 0

    rounds = chips + 3
    lax.fori_loop(0, min(rounds, pieces), both, 0)
    if pieces > rounds:
        lax.fori_loop(rounds, pieces, widen, 0)
    else:
        lax.fori_loop(pieces, rounds, reducer.round, 0)
    reducer.close()
    for j in (pieces - 2, pieces - 1):
        wide_copy(j).wait()
    swap.wait()
    swapped[...] = land[...].astype(F32)


def reduce_product(left, right, gains, half, low):
    height, out_shape, scratch = reducer_buffers(left, right)
    vmem = pl.BlockSpec(memory_space=pltpu.VMEM)
    hbm = pl.BlockSpec(memory_space=pl.ANY)
    dma = pltpu.SemaphoreType.DMA
    tall = low.shape[0] // 8
    return pl.pallas_call(
        functools.partial(reduce_kernel, height),
        out_shape=(
            out_shape,
            jax.ShapeDtypeStruct(half.shape, F32),
            jax.ShapeDtypeStruct(low.shape, F32),
        ),
        in_specs=[vmem] * 4 + [hbm],
        out_specs=(vmem, vmem, hbm),
        scratch_shapes=scratch
        + [
            pltpu.VMEM(half.shape, BF16),
            pltpu.VMEM((2, tall, low.shape[1]), BF16),
            pltpu.VMEM((2, tall, low.shape[1]), F32),
            dma((2,)),
            dma((2,)),
            dma((2,)),
        ],
        compiler_params=pltpu.CompilerParams(
            collective_id=2, has_side_effects=True, vmem_limit_bytes=VMEM_LIMIT
        ),
        cost_estimate=pl.CostEstimate(
            flops=50_000_000_000, bytes_accessed=10_000_000, transcendentals=0
        ),
        name="reduce_product",
    )(left, right, gains, half, low)


def natural(device, sub, subs):
    if subs == 2:
        return sub * (2 * lax.axis_size("mp") - 1 - 2 * device) + (1 - sub) * 2 * device
    return subs * device + sub


def front_kernel(
    shard_ref,
    x_ref,
    cos_q,
    sin_q,
    cos_kv,
    sin_kv,
    w_out,
    extra_ref,
    xf_ref,
    normed_ref,
    inv_ref,
    q_ref,
    kv_out,
    w_all,
    x_in,
    kv_all,
    swap_send,
    swap_recv,
    z_send,
    z_recv,
    xy_send,
    xy_recv,
    far_send,
    far_recv,
    twin_send,
    twin_recv,
    kz_send,
    kz_recv,
    kt_send,
    kt_recv,
    out_sem,
):
    mp = lax.axis_size("mp")
    chips = mp // 2
    me = lax.axis_index("mp")
    row = lax.axis_index("rows")
    chip = me // 2
    core = me % 2
    down, across = row // 2, row % 2
    subs = x_ref.shape[0] // BLOCK
    height = shard_ref.shape[0]
    half = w_all.shape[1] // 2
    beside_row = row + 1 - 2 * across
    above_row = (1 - down) * 2 + across
    far_row = (1 - down) * 2 + 1 - across
    twin = (row, me + 1 - 2 * core)
    beside = (beside_row, me)
    above = (above_row, me)
    mirror = (row, mp - 1 - me)

    barrier = pltpu.get_barrier_semaphore()
    for device in (twin, beside, above, mirror):
        pl.semaphore_signal(barrier, inc=1, device_id=device, device_id_type=MESH)

    @pl.when(chip < chips - 1)
    def _():
        pl.semaphore_signal(barrier, inc=1, device_id=(row, me + 2), device_id_type=MESH)

    @pl.when(chip > 0)
    def _():
        pl.semaphore_signal(barrier, inc=1, device_id=(row, me - 2), device_id_type=MESH)

    ends = jnp.where(chip < chips - 1, 1, 0) + jnp.where(chip > 0, 1, 0)
    pl.semaphore_wait(barrier, 4 + ends)

    def remote(source, dest, send, recv, device):
        return pltpu.make_async_remote_copy(
            src_ref=source,
            dst_ref=dest,
            send_sem=send,
            recv_sem=recv,
            device_id=device,
            device_id_type=MESH,
        )

    def spot(r, k, side=None):
        lines = pl.ds(pl.multiple_of((r * mp + 2 * k + core) * height, height), height)
        if side is None:
            return w_all.at[lines]
        return w_all.at[lines, pl.ds(side * half, half)]

    def z_copy(k, side):
        return remote(
            spot(row, k),
            spot(row, k),
            z_send.at[(side + 1) // 2, k],
            z_recv.at[k],
            (row, me + 2 * side),
        )

    def near_copy(k, d):
        return remote(
            spot(row, k), spot(row, k), xy_send.at[d, k], xy_recv.at[d, k], (beside, above)[d]
        )

    def near_row(d):
        return (beside_row, above_row)[d]

    def far_copy(k, d):
        place = spot(near_row(d), k, d)
        return remote(place, place, far_send.at[d, k], far_recv.at[d, k], (above, beside)[d])

    def twin_copy(k, kind):
        if kind < 3:
            place = spot((row, beside_row, above_row)[kind], k)
        else:
            place = spot(far_row, k, kind - 3)
        return remote(place, place, twin_send.at[kind, k], twin_recv.at[kind, k], twin)

    def order(i):
        near = jnp.minimum(chip, chips - 1 - chip)
        long_side = jnp.where(chip < chips - 1 - chip, 1, -1)
        paired = i <= 2 * near
        dist = jnp.where(paired, (i + 1) // 2, i - near)
        side = jnp.where(paired, 2 * (i % 2) - 1, long_side)
        return chip + side * dist

    if subs == 2:
        swap = remote(x_ref.at[pl.ds(BLOCK, BLOCK)], x_in, swap_send, swap_recv, mirror)
        swap.start()
    own_lines = pl.ds(pl.multiple_of((row * mp + me) * height, height), height)
    w_all[own_lines, :] = shard_ref[...]

    def gather_step(n, _):
        @pl.when(n < chips)
        def _():
            k = order(n)

            @pl.when(n > 0)
            def _():
                z_copy(k, 1).wait_recv()

            for d in range(2):
                near_copy(k, d).start()

            @pl.when((k >= chip) & (chip > 0))
            def _():
                z_copy(k, -1).start()

            @pl.when((k <= chip) & (chip < chips - 1))
            def _():
                z_copy(k, 1).start()

            twin_copy(k, 0).start()

        @pl.when((n >= 1) & (n < chips + 1))
        def _():
            k = order(n - 1)
            for d in range(2):
                near_copy(k, d).wait_recv()
                far_copy(k, d).start()
                twin_copy(k, 1 + d).start()

        @pl.when(n >= 2)
        def _():
            k = order(n - 2)
            for d in range(2):
                far_copy(k, d).wait_recv()
                twin_copy(k, 3 + d).start()

        return 0

    lax.fori_loop(0, chips + 2, gather_step, 0)

    xf_ref[:BLOCK, :] = x_ref[:BLOCK, :]
    if subs == 2:
        swap.wait_recv()
        xf_ref[BLOCK:, :] = x_in[...]

    def drain_step(k, _):
        for kind in range(5):
            twin_copy(k, kind).wait_recv()
        return 0

    lax.fori_loop(0, chips, drain_step, 0)
    save = pltpu.make_async_copy(w_all, w_out, out_sem)
    save.start()
    cols = Q_WIDTH + 2 * KV_WIDTH
    extra = w_all[:, cols:].astype(F32).T[:8, :]
    extra_ref[...] = extra
    x = xf_ref[...].astype(F32)
    inverse = lax.rsqrt(jnp.mean(x * x, axis=-1, keepdims=True) + EPS)
    inv_ref[...] = inverse
    normed_ref[...] = (x * inverse * extra[0:1, :]).astype(BF16)

    def place_of(device, sub):
        first = natural(device, sub, subs) * BLOCK
        return kv_all.at[pl.ds(pl.multiple_of(first, BLOCK), BLOCK)]

    part = dot(normed_ref[...], w_all[:, Q_WIDTH:cols])
    for g in range(KV_HEADS):
        slab = part[:, g * SLAB : (g + 1) * SLAB]
        turned = (slab * cos_kv[...] + swap_halves(slab) * sin_kv[...]).astype(BF16)
        for sub in range(subs):
            place_of(me, sub)[:, g * SLAB : (g + 1) * SLAB] = turned[
                sub * BLOCK : (sub + 1) * BLOCK, :
            ]

    def kz_copy(k, sub, side):
        place = place_of(2 * k + core, sub)
        return remote(
            place,
            place,
            kz_send.at[(side + 1) // 2, k * subs + sub],
            kz_recv.at[k * subs + sub],
            (row, me + 2 * side),
        )

    def kt_copy(k, sub):
        place = place_of(2 * k + core, sub)
        return remote(
            place, place, kt_send.at[k * subs + sub], kt_recv.at[k * subs + sub], twin
        )

    def spread(n, _):
        k = order(n)
        for sub in range(subs):

            @pl.when(n > 0)
            def _():
                kz_copy(k, sub, 1).wait_recv()

            @pl.when((k >= chip) & (chip > 0))
            def _():
                kz_copy(k, sub, -1).start()

            @pl.when((k <= chip) & (chip < chips - 1))
            def _():
                kz_copy(k, sub, 1).start()

            kt_copy(k, sub).start()

        return 0

    spread(0, 0)
    for s in range(Q_WIDTH // 256):
        part = dot(normed_ref[...], w_all[:, s * 256 : (s + 1) * 256])
        for t in range(2):
            slab = part[:, t * SLAB : (t + 1) * SLAB]
            col = s * 256 + t * SLAB
            turned = slab * cos_q[...] + swap_halves(slab) * sin_q[...]
            q_ref[:, col : col + SLAB] = (
                turned.astype(BF16).astype(F32) * HEAD_DIM ** (-0.5)
            ).astype(BF16)
    lax.fori_loop(1, chips, spread, 0)

    def finish(k, _):
        for sub in range(subs):
            kt_copy(k, sub).wait_recv()
            kt_copy(k, sub).wait_send()
        for kind in range(5):
            twin_copy(k, kind).wait_send()
        for d in range(2):
            near_copy(k, d).wait_send()
            far_copy(k, d).wait_send()

        @pl.when((k >= chip) & (chip > 0))
        def _():
            z_copy(k, -1).wait_send()
            for sub in range(subs):
                kz_copy(k, sub, -1).wait_send()

        @pl.when((k <= chip) & (chip < chips - 1))
        def _():
            z_copy(k, 1).wait_send()
            for sub in range(subs):
                kz_copy(k, sub, 1).wait_send()

        return 0

    lax.fori_loop(0, chips, finish, 0)
    if subs == 2:
        swap.wait_send()
    kv_out[...] = kv_all[...]
    save.wait()


def front(shard, x, tables):
    rows, width = x.shape
    subs = rows // BLOCK
    chips = lax.axis_size("mp") // 2
    cols = shard.shape[1]
    total = shard.shape[0] * lax.axis_size("rows") * lax.axis_size("mp")
    vmem = pl.BlockSpec(memory_space=pltpu.VMEM)
    hbm = pl.BlockSpec(memory_space=pl.ANY)
    dma = pltpu.SemaphoreType.DMA
    return pl.pallas_call(
        front_kernel,
        out_shape=(
            jax.ShapeDtypeStruct((total, cols), BF16),
            jax.ShapeDtypeStruct((8, total), F32),
            jax.ShapeDtypeStruct((rows, width), BF16),
            jax.ShapeDtypeStruct((rows, width), BF16),
            jax.ShapeDtypeStruct((rows, 1), F32),
            jax.ShapeDtypeStruct((rows, Q_WIDTH), BF16),
            jax.ShapeDtypeStruct((LEN, 2 * KV_WIDTH), BF16),
        ),
        in_specs=[vmem] * 6,
        out_specs=(hbm,) + (vmem,) * 6,
        scratch_shapes=[
            pltpu.VMEM((total, cols), BF16),
            pltpu.VMEM((BLOCK, width), BF16),
            pltpu.VMEM((LEN, 2 * KV_WIDTH), BF16),
            dma,
            dma,
            dma((2, chips)),
            dma((chips,)),
            dma((2, chips)),
            dma((2, chips)),
            dma((2, chips)),
            dma((2, chips)),
            dma((5, chips)),
            dma((5, chips)),
            dma((2, chips * subs)),
            dma((chips * subs,)),
            dma((chips * subs,)),
            dma((chips * subs,)),
            dma,
        ],
        compiler_params=pltpu.CompilerParams(
            collective_id=4, has_side_effects=True, vmem_limit_bytes=VMEM_LIMIT
        ),
        cost_estimate=pl.CostEstimate(
            flops=30_000_000_000, bytes_accessed=12_000_000, transcendentals=0
        ),
        name="front",
    )(shard, x, *tables)


def on_device(
    inputs,
    cotangent,
    corpus_ids,
    corpus_weight,
    attn_gain,
    qkv_weight,
    out_weight,
    ffn_gain,
    gate_weight,
    up_weight,
    down_weight,
):
    both = ("rows", "mp")
    rows_dev, width = inputs.shape
    mp = lax.axis_size("mp")
    me = lax.axis_index("mp")
    row_groups = lax.axis_size("rows")
    corpora = corpus_weight.shape[0]
    subs = rows_dev // BLOCK
    folded = subs == 2
    mirror = [(i, mp - 1 - i) for i in range(mp)]

    def fold(rows):
        if not folded:
            return rows
        return jnp.concatenate(
            [rows[:BLOCK], lax.ppermute(rows[BLOCK:], "mp", mirror)], axis=0
        )

    def to_order(gathered):
        if not folded:
            return gathered
        parts = gathered.reshape(mp, 2, BLOCK, gathered.shape[-1])
        return jnp.stack([parts[:, 0], parts[::-1, 1]], axis=1).reshape(gathered.shape)

    if folded:
        blocks = jnp.stack([2 * me, 2 * mp - 1 - 2 * me]).astype(jnp.int32)
    else:
        blocks = (subs * me + jnp.arange(subs)).astype(jnp.int32)
    positions = (blocks[:, None] * BLOCK + jnp.arange(BLOCK)[None, :]).reshape(-1)

    shard_rows = qkv_weight.shape[0]
    ident = jnp.broadcast_to(corpus_ids.astype(BF16)[:1, None], (shard_rows, 1))
    spare = (-(Q_WIDTH + 2 * KV_WIDTH + 3)) % 128
    shard = jnp.concatenate(
        [
            pack_kv(qkv_weight),
            attn_gain[:, None],
            ffn_gain[:, None],
            ident,
            jnp.zeros((shard_rows, spare), BF16),
        ],
        axis=1,
    )
    qkv_cols = Q_WIDTH + 2 * KV_WIDTH
    cot_all = lax.all_gather(cotangent, "mp", axis=0, tiled=True)
    out_full = lax.all_gather(out_weight, both, axis=0, tiled=True)
    tables = rope_tables(positions)
    if row_groups == 4:
        qkv_ext, extras, x, normed_one, inverse_one, q, kv_all = front(shard, inputs, tables)
        qkv_full = qkv_ext[:, :qkv_cols]
    else:
        qkv_ext = lax.all_gather(shard, both, axis=0, tiled=True)
        qkv_full = qkv_ext[:, :qkv_cols]
        extras = qkv_ext[:, qkv_cols:].astype(F32).T
        x = fold(inputs)
        normed_one, inverse_one, q, kv = qkv_project(x, extras[0:1], qkv_full, tables)
        kv_all = to_order(lax.all_gather(kv, "mp", axis=0, tiled=True))
    gain_one, gain_two = extras[0:1], extras[1:2]
    all_ids = extras[2].reshape(row_groups, -1)[:, 0]
    my_id = corpus_ids[0].astype(F32)
    count = jnp.sum((all_ids == my_id).astype(F32))
    weight_seq = jnp.sum(
        jnp.where(jnp.arange(corpora) == corpus_ids[0], corpus_weight, 0.0)
    )
    seq_scale = weight_seq * row_groups / (corpora * count)
    o, totals = attend(blocks, q, kv_all)

    residual = x.astype(F32)
    middle = residual + dot(o, out_full)
    inverse_two = lax.rsqrt(jnp.mean(middle * middle, axis=-1, keepdims=True) + EPS)
    normed_two = (middle * inverse_two * gain_two).astype(BF16)
    ffn_sum, grad_normed_two, gate_grad, up_grad, down_grad = ffn(
        seq_scale, normed_two, cot_all, gate_weight, up_weight, down_weight
    )
    outputs = fold((middle + ffn_sum).astype(BF16))

    cot = jnp.concatenate(
        [
            lax.dynamic_slice(cot_all, (blocks[sub] * BLOCK, 0), (BLOCK, width))
            for sub in range(subs)
        ],
        axis=0,
    )
    grad_out = cot.astype(F32) * seq_scale
    scaled_two = grad_normed_two * gain_two
    ffn_gain_part = jnp.sum(grad_normed_two * middle * inverse_two, axis=0)
    grad_middle = (
        grad_out
        + inverse_two * scaled_two
        - middle * inverse_two**3 * jnp.mean(scaled_two * middle, axis=-1, keepdims=True)
    )
    grad_middle_low = grad_middle.astype(BF16)
    if row_groups == 4:
        gate_grad, up_grad, down_grad = (
            lax.all_gather(g, "rows", axis=0, tiled=True)
            for g in (gate_grad, up_grad, down_grad)
        )
    grad_o = dot_nt(grad_middle_low, out_full).astype(BF16)
    grad_qkv, *proj = attend_back(q, kv_all, o, grad_o, totals, tables, grad_middle_low)
    grad_normed_one = dot_nt(grad_qkv, qkv_full)
    scaled_one = grad_normed_one * gain_one
    attn_gain_part = jnp.sum(grad_normed_one * residual * inverse_one, axis=0)
    input_grad = (
        grad_middle
        + inverse_one * scaled_one
        - residual * inverse_one**3 * jnp.mean(scaled_one * residual, axis=-1, keepdims=True)
    )
    if folded and row_groups != 4:
        input_grad = jnp.concatenate(
            [
                input_grad[:BLOCK],
                lax.ppermute(input_grad[BLOCK:].astype(BF16), "mp", mirror).astype(F32),
            ],
            axis=0,
        )
    gain_parts = jnp.concatenate(
        [attn_gain_part[None], ffn_gain_part[None], jnp.zeros((6, width), F32)], axis=0
    )
    if row_groups == 4:
        proj_grad = proj[0]
        part, swapped, gate_grad = reduce_product(
            normed_one, grad_qkv, gain_parts, input_grad[-BLOCK:].astype(BF16), gate_grad
        )
        if folded:
            input_grad = jnp.concatenate([input_grad[:BLOCK], swapped], axis=0)
    else:
        part = jnp.concatenate(
            [dot_tn(normed_one, grad_qkv), gain_parts.T, jnp.zeros((width, 120), F32)], axis=1
        )
        part, proj_grad = (
            lax.psum_scatter(p.astype(BF16), both, scatter_dimension=0, tiled=True).astype(F32)
            for p in (part, dot_tn(o, grad_middle_low))
        )
    qkv_grad = unpack_kv(part[:, :qkv_cols])
    attn_gain_grad = part[:, qkv_cols]
    ffn_gain_grad = part[:, qkv_cols + 1]
    if row_groups != 4:
        gate_grad = gate_grad.astype(F32)
    up_grad, part = lax.optimization_barrier((up_grad, part))
    up_grad = up_grad.astype(F32)
    down_grad, part = lax.optimization_barrier((down_grad, part))
    down_grad = down_grad.astype(F32)
    qkv_grad = unpack_kv(part[:, :qkv_cols])
    attn_gain_grad = part[:, qkv_cols]
    ffn_gain_grad = part[:, qkv_cols + 1]
    return (
        outputs,
        input_grad,
        qkv_grad,
        proj_grad,
        gate_grad,
        up_grad,
        down_grad,
        attn_gain_grad,
        ffn_gain_grad,
    )


def solution(mesh):
    split = P(("rows", "mp"), None)
    line = P(("rows", "mp"))
    in_specs = (
        split,
        split,
        P("rows"),
        P(),
        line,
        split,
        split,
        line,
        P(None, "mp"),
        P(None, "mp"),
        P("mp", None),
    )
    out_specs = (
        split,
        split,
        split,
        split,
        P(None, "mp"),
        P(None, "mp"),
        P("mp", None),
        line,
        line,
    )
    return jax.shard_map(
        on_device, mesh=mesh, in_specs=in_specs, out_specs=out_specs, check_vma=False
    )
```

```python
import functools

import jax
import jax.numpy as jnp
from jax import lax
from jax.experimental import pallas as pl
from jax.experimental.pallas import tpu as pltpu
from jax.sharding import PartitionSpec as P

HEADS = 20
KV_HEADS = 5
HEAD_DIM = 64
GROUP = HEADS // KV_HEADS
Q_WIDTH = HEADS * HEAD_DIM
KV_WIDTH = KV_HEADS * HEAD_DIM
LEN = 2048
BLOCK = 128
KTILE = 256
EPS = 1e-05
THETA = 10000.0
LANES = GROUP * BLOCK
SLAB = 2 * HEAD_DIM

MESH = pl.DeviceIdType.MESH
F32 = jnp.float32
BF16 = jnp.bfloat16
VMEM_LIMIT = 62 * 1024 * 1024


def rope_tables(positions):
    half_dim = HEAD_DIM // 2
    freqs = jnp.exp(-jnp.log(THETA) * (2.0 * jnp.arange(half_dim, dtype=F32)) / HEAD_DIM)
    angles = positions.astype(F32)[:, None] * freqs[None, :]
    cosine, sine = jnp.cos(angles), jnp.sin(angles)
    ones, zeros = jnp.ones_like(cosine), jnp.zeros_like(cosine)
    head_cos = jnp.concatenate([cosine, cosine], axis=1)
    head_sin = jnp.concatenate([-sine, sine], axis=1)
    cos_q = jnp.concatenate([head_cos, head_cos], axis=1)
    sin_q = jnp.concatenate([head_sin, head_sin], axis=1)
    cos_kv = jnp.concatenate([head_cos, ones, ones], axis=1)
    sin_kv = jnp.concatenate([head_sin, zeros, zeros], axis=1)
    return (cos_q, sin_q, cos_kv, sin_kv)


def swap_halves(slab):
    lane = lax.broadcasted_iota(jnp.int32, slab.shape, 1)
    half_dim = HEAD_DIM // 2
    up = pltpu.roll(slab, SLAB - half_dim, 1)
    down = pltpu.roll(slab, half_dim, 1)
    return jnp.where(lane % HEAD_DIM < half_dim, up, down)


def qkv_kernel(x_ref, gain_ref, w_ref, cos_q, sin_q, cos_kv, sin_kv, normed_ref, inv_ref, q_ref, kv_ref):
    x = x_ref[...].astype(F32)
    inverse = lax.rsqrt(jnp.mean(x * x, axis=-1, keepdims=True) + EPS)
    normed = (x * inverse * gain_ref[...]).astype(BF16)
    normed_ref[...] = normed
    inv_ref[...] = inverse
    for s in range(Q_WIDTH // 256):
        part = jnp.dot(normed, w_ref[:, s * 256 : (s + 1) * 256], preferred_element_type=F32)
        for t in range(2):
            slab = part[:, t * SLAB : (t + 1) * SLAB]
            col = s * 256 + t * SLAB
            turned = slab * cos_q[...] + swap_halves(slab) * sin_q[...]
            q_ref[:, col : col + SLAB] = (turned.astype(BF16).astype(F32) * HEAD_DIM ** (-0.5)).astype(BF16)
    part = jnp.dot(normed, w_ref[:, Q_WIDTH : Q_WIDTH + 2 * KV_WIDTH], preferred_element_type=F32)
    for g in range(KV_HEADS):
        slab = part[:, g * SLAB : (g + 1) * SLAB]
        turned = slab * cos_kv[...] + swap_halves(slab) * sin_kv[...]
        kv_ref[:, g * SLAB : (g + 1) * SLAB] = turned.astype(BF16)


def qkv_project(x, gain, weight, tables):
    rows, width = x.shape
    return pl.pallas_call(
        qkv_kernel,
        out_shape=(
            jax.ShapeDtypeStruct((rows, width), BF16),
            jax.ShapeDtypeStruct((rows, 1), F32),
            jax.ShapeDtypeStruct((rows, Q_WIDTH), BF16),
            jax.ShapeDtypeStruct((rows, 2 * KV_WIDTH), BF16),
        ),
        compiler_params=pltpu.CompilerParams(vmem_limit_bytes=VMEM_LIMIT),
        name="qkv_project",
    )(x, gain, weight, *tables)


def heads_to_lanes(rows_part):
    turned = rows_part.T
    return jnp.concatenate(
        [turned[h * HEAD_DIM : (h + 1) * HEAD_DIM, :] for h in range(GROUP)], axis=1
    )


def lanes_to_heads(lanes_part):
    stacked = jnp.concatenate(
        [lanes_part[:, h * BLOCK : (h + 1) * BLOCK] for h in range(GROUP)], axis=0
    )
    return stacked.T


def causal(tile, block):
    key_pos = tile * KTILE + lax.broadcasted_iota(jnp.int32, (KTILE, LANES), 0)
    query_pos = block * BLOCK + lax.broadcasted_iota(jnp.int32, (KTILE, LANES), 1) % BLOCK
    return key_pos <= query_pos


def over_rows(left, right):
    return lax.dot_general(left, right, (((0,), (0,)), ((), ())), preferred_element_type=F32)


def attend_kernel(block_ref, q_ref, kv_ref, o_ref, total_ref):
    subs = q_ref.shape[0] // BLOCK
    for sub in range(subs):
        block = block_ref[sub]
        queries = heads_to_lanes(q_ref[sub * BLOCK : (sub + 1) * BLOCK, :].astype(F32))
        queries = jnp.concatenate([queries, jnp.zeros_like(queries)], axis=0).astype(BF16)

        def step(tile, carry, masked):
            top, total, acc = carry
            kv = kv_ref[pl.ds(pl.multiple_of(tile * KTILE, KTILE), KTILE), :]
            scores = jnp.dot(kv, queries, preferred_element_type=F32)
            if masked:
                scores = jnp.where(causal(tile, block), scores, -1e30)
            new_top = jnp.maximum(top, jnp.max(scores, axis=0, keepdims=True))
            decay = jnp.exp(top - new_top)
            probs = jnp.exp(scores - new_top)
            total = decay * total + jnp.sum(probs, axis=0, keepdims=True)
            acc = decay * acc + over_rows(kv, probs.astype(BF16))
            return (new_top, total, acc)

        start = (
            jnp.full((1, LANES), -1e30, F32),
            jnp.zeros((1, LANES), F32),
            jnp.zeros((SLAB, LANES), F32),
        )
        full = block * BLOCK // KTILE
        carry = lax.fori_loop(0, full, lambda t, c: step(t, c, False), start)
        top, total, acc = step(full, carry, True)
        out = acc[HEAD_DIM:, :] / total
        o_ref[sub * BLOCK : (sub + 1) * BLOCK, :] = lanes_to_heads(out).astype(BF16)
        total_ref[sub : sub + 1, :] = top + jnp.log(total)


def attend(blocks, q, kv_all):
    rows = q.shape[0]
    subs = rows // BLOCK
    return pl.pallas_call(
        attend_kernel,
        grid_spec=pltpu.PrefetchScalarGridSpec(
            num_scalar_prefetch=1,
            grid=(KV_HEADS,),
            in_specs=[
                pl.BlockSpec((rows, GROUP * HEAD_DIM), lambda g, b: (0, g)),
                pl.BlockSpec((LEN, SLAB), lambda g, b: (0, g)),
            ],
            out_specs=[
                pl.BlockSpec((rows, GROUP * HEAD_DIM), lambda g, b: (0, g)),
                pl.BlockSpec((None, subs, LANES), lambda g, b: (g, 0, 0)),
            ],
        ),
        out_shape=(
            jax.ShapeDtypeStruct((rows, Q_WIDTH), BF16),
            jax.ShapeDtypeStruct((KV_HEADS, subs, LANES), F32),
        ),
        compiler_params=pltpu.CompilerParams(vmem_limit_bytes=VMEM_LIMIT),
        cost_estimate=pl.CostEstimate(
            flops=60_000_000_000, bytes_accessed=8_000_000, transcendentals=6_000_000
        ),
        name="attend",
    )(blocks, q, kv_all)


def attend_back_kernel(height, *refs):
    if height:
        low_ref, grad_ref, proj_ref = refs[9:12]
        attend_back_body(refs[:9], grad_ref, refs[12:23], (height, low_ref, proj_ref, refs[23:]))
    else:
        attend_back_body(refs[:9], refs[9], refs[10:], None)


def attend_back_body(inputs, grad_ref, scratch, product):
    q_ref, kv_ref, o_ref, do_ref, total_ref, cos_q, sin_q, cos_kv, sin_kv = inputs
    (dkv_acc, own_part, twin_out, twin_in, sum_out, sum_in, mine) = scratch[:7]
    (twin_send, twin_recv, sum_send, sum_recv) = scratch[7:]
    subs = q_ref.shape[0] // BLOCK
    chips = lax.axis_size("mp") // 2
    me = lax.axis_index("mp")
    row = lax.axis_index("rows")
    chip = me // 2
    core = me % 2
    twin = (row, me + 1 - 2 * core)
    width = GROUP * HEAD_DIM

    barrier = pltpu.get_barrier_semaphore()
    pl.semaphore_signal(barrier, inc=1, device_id=twin, device_id_type=MESH)
    for step in range(1, chips):
        pl.semaphore_signal(
            barrier,
            inc=1,
            device_id=(row, 2 * ((chip + step) % chips) + core),
            device_id_type=MESH,
        )
    if product:
        down, across = row // 2, row % 2
        for device in ((row + 1 - 2 * across, me), ((1 - down) * 2 + across, me)):
            pl.semaphore_signal(barrier, inc=1, device_id=device, device_id_type=MESH)
    pl.semaphore_wait(barrier, chips + 2 if product else chips)
    if product:
        reducer = Reducer(product[0], o_ref, product[1], None, product[2], product[3])

    def twin_copy(g):
        return pltpu.make_async_remote_copy(
            src_ref=twin_out.at[g % 2],
            dst_ref=twin_in.at[g],
            send_sem=twin_send.at[g % 2],
            recv_sem=twin_recv.at[g],
            device_id=twin,
            device_id_type=MESH,
        )

    def sum_copy(g, step):
        return pltpu.make_async_remote_copy(
            src_ref=sum_out.at[g, step - 1],
            dst_ref=sum_in.at[g, step - 1],
            send_sem=sum_send.at[g, step - 1],
            recv_sem=sum_recv.at[g, step - 1],
            device_id=(row, 2 * ((chip + step) % chips) + core),
            device_id_type=MESH,
        )

    def combine(g):
        twin_copy(g).wait_recv()
        for step in range(1, chips):
            goal = (chip + step) % chips
            sum_out[g, step - 1] = (
                own_part[g % 2, goal] + twin_in[g, goal].astype(F32)
            ).astype(BF16)
            sum_copy(g, step).start()
        mine[g] = own_part[g % 2, chip] + twin_in[g, chip].astype(F32)

    def head_step(g, _):
        if product:
            reducer.round(g)
        cols = pl.ds(pl.multiple_of(g * width, width), width)
        pair = pl.ds(pl.multiple_of(g * SLAB, SLAB), SLAB)
        dkv_acc[...] = jnp.zeros_like(dkv_acc)
        for sub in range(subs):
            rows = slice(sub * BLOCK, (sub + 1) * BLOCK)
            block = natural(me, sub, subs)
            queries = heads_to_lanes(q_ref[rows, cols].astype(F32))
            grads = heads_to_lanes(do_ref[rows, cols].astype(F32))
            outs = heads_to_lanes(o_ref[rows, cols].astype(F32))
            delta = jnp.sum(grads * outs, axis=0, keepdims=True)
            empty = jnp.zeros_like(queries)
            queries = jnp.concatenate([queries, empty], axis=0)
            grads = jnp.concatenate([empty, grads], axis=0)
            query_rows = queries.T.astype(BF16)
            grad_rows = grads.T.astype(BF16)
            queries = queries.astype(BF16)
            grads = grads.astype(BF16)
            log_total = total_ref[g, sub : sub + 1, :]

            def step(tile, dq, masked):
                keys = pl.ds(pl.multiple_of(tile * KTILE, KTILE), KTILE)
                kv = kv_ref[keys, pair]
                scores = jnp.dot(kv, queries, preferred_element_type=F32)
                probs = jnp.exp(scores - log_total)
                if masked:
                    probs = jnp.where(causal(tile, block), probs, 0.0)
                grad_probs = jnp.dot(kv, grads, preferred_element_type=F32)
                grad_scores = (probs * (grad_probs - delta)).astype(BF16)
                dkv_acc[keys, :] += jnp.dot(
                    grad_scores, query_rows, preferred_element_type=F32
                ) + jnp.dot(probs.astype(BF16), grad_rows, preferred_element_type=F32)
                return dq + over_rows(kv, grad_scores)

            full = block * BLOCK // KTILE
            dq = lax.fori_loop(
                0, full, lambda t, c: step(t, c, False), jnp.zeros((SLAB, LANES), F32)
            )
            dq = step(full, dq, True)
            dq = lanes_to_heads(dq[:HEAD_DIM, :]) * HEAD_DIM ** (-0.5)
            for t in range(width // SLAB):
                slab = dq[:, t * SLAB : (t + 1) * SLAB]
                turned = slab * cos_q[rows, :] - swap_halves(slab) * sin_q[rows, :]
                first = pl.multiple_of(g * width + t * SLAB, SLAB)
                grad_ref[rows, pl.ds(first, SLAB)] = turned.astype(BF16)

        @pl.when(g >= 2)
        def _():
            twin_copy(g - 2).wait_send()

        for goal in range(chips):
            for sub in range(subs):
                first = natural(2 * goal + core, sub, subs) * BLOCK
                own_part[g % 2, goal, sub] = dkv_acc[pl.ds(pl.multiple_of(first, BLOCK), BLOCK), :]
                first = natural(2 * goal + 1 - core, sub, subs) * BLOCK
                twin_out[g % 2, goal, sub] = dkv_acc[
                    pl.ds(pl.multiple_of(first, BLOCK), BLOCK), :
                ].astype(BF16)
        twin_copy(g).start()

        @pl.when(g >= 1)
        def _():
            combine(g - 1)

        return 0

    lax.fori_loop(0, KV_HEADS, head_step, 0)
    combine(KV_HEADS - 1)
    if product:
        lax.fori_loop(KV_HEADS, chips + 3, reducer.round, 0)

    for g in range(KV_HEADS):
        total = mine[g]
        for step in range(1, chips):
            sum_copy(g, step).wait_recv()
            total = total + sum_in[g, step - 1].astype(F32)
        slab = total.reshape(subs * BLOCK, SLAB)
        turned = slab * cos_kv[...] - swap_halves(slab) * sin_kv[...]
        first = Q_WIDTH + g * SLAB
        grad_ref[:, first : first + SLAB] = turned.astype(BF16)
    for g in range(KV_HEADS):
        for step in range(1, chips):
            sum_copy(g, step).wait_send()
    for g in range(KV_HEADS - 2, KV_HEADS):
        twin_copy(g).wait_send()
    if product:
        reducer.close()


def attend_back(q, kv_all, o, grad_o, totals, tables, low):
    rows = q.shape[0]
    subs = rows // BLOCK
    chips = lax.axis_size("mp") // 2
    vmem = pl.BlockSpec(memory_space=pltpu.VMEM)
    dma = pltpu.SemaphoreType.DMA
    part = (chips, subs, BLOCK, SLAB)
    args = (q, kv_all, o, grad_o, totals, *tables)
    out_shape = (jax.ShapeDtypeStruct((rows, Q_WIDTH + 2 * KV_WIDTH), BF16),)
    height, more = 0, []
    if lax.axis_size("rows") == 4:
        height, product, more = reducer_buffers(o, low)
        args += (low,)
        out_shape += (product,)
    return pl.pallas_call(
        functools.partial(attend_back_kernel, height),
        in_specs=[vmem] * len(args),
        out_specs=(vmem,) * len(out_shape),
        out_shape=out_shape,
        scratch_shapes=[
            pltpu.VMEM((LEN, SLAB), F32),
            pltpu.VMEM((2,) + part, F32),
            pltpu.VMEM((2,) + part, BF16),
            pltpu.VMEM((KV_HEADS,) + part, BF16),
            pltpu.VMEM((KV_HEADS, chips - 1) + part[1:], BF16),
            pltpu.VMEM((KV_HEADS, chips - 1) + part[1:], BF16),
            pltpu.VMEM((KV_HEADS,) + part[1:], F32),
            dma((2,)),
            dma((KV_HEADS,)),
            dma((KV_HEADS, chips - 1)),
            dma((KV_HEADS, chips - 1)),
        ]
        + more,
        compiler_params=pltpu.CompilerParams(
            collective_id=3, has_side_effects=True, vmem_limit_bytes=VMEM_LIMIT
        ),
        cost_estimate=pl.CostEstimate(
            flops=120_000_000_000, bytes_accessed=12_000_000, transcendentals=6_000_000
        ),
        name="attend_back",
    )(*args)


def pack_kv(columns):
    lead = columns.shape[:-1]
    kv = columns[..., Q_WIDTH:].reshape(*lead, 2, KV_HEADS, HEAD_DIM)
    kv = jnp.swapaxes(kv, -3, -2).reshape(*lead, 2 * KV_WIDTH)
    return jnp.concatenate([columns[..., :Q_WIDTH], kv], axis=-1)


def unpack_kv(columns):
    lead = columns.shape[:-1]
    kv = columns[..., Q_WIDTH:].reshape(*lead, KV_HEADS, 2, HEAD_DIM)
    kv = jnp.swapaxes(kv, -3, -2).reshape(*lead, 2 * KV_WIDTH)
    return jnp.concatenate([columns[..., :Q_WIDTH], kv], axis=-1)


def dot(left, right):
    return jnp.dot(left, right, preferred_element_type=F32)


def dot_nt(left, right):
    return lax.dot_general(left, right, (((1,), (1,)), ((), ())), preferred_element_type=F32)


def dot_tn(left, right):
    return lax.dot_general(left, right, (((0,), (0,)), ((), ())), preferred_element_type=F32)


def half_of(ref, chip, core, sub, rows):
    subs = ref.shape[0] // (rows * lax.axis_size("mp"))
    start = natural(2 * chip + core, sub, subs) * rows
    return ref.at[pl.ds(pl.multiple_of(start, rows), rows)]


def part_of(ref, chip, core, sub, rows):
    subs = ref.shape[0] // (rows * lax.axis_size("mp"))
    start = (subs * (2 * chip + core) + sub) * rows
    return ref.at[pl.ds(pl.multiple_of(start, rows), rows)]


def ffn_kernel(
    subs,
    quad,
    scale_ref,
    x_ref,
    cot_ref,
    gate_ref,
    up_ref,
    down_ref,
    part_ref,
    part_in,
    relay_in,
    part_sum,
    sum_ref,
    gate_out,
    up_out,
    down_out,
    *rest,
):
    rest, weights, weight_sem = rest[:-4], rest[-4:-1], rest[-1]
    loads = [
        pltpu.make_async_copy(source, target, weight_sem.at[i])
        for i, (source, target) in enumerate(zip((gate_ref, up_ref, down_ref), weights))
    ]
    for copy in loads:
        copy.start()
    gate_ref, up_ref, down_ref = weights
    slots = rest[:9] if quad else ()
    scratch = rest[9:] if quad else rest
    ffn_body(
        subs,
        quad,
        slots,
        loads,
        scale_ref,
        x_ref,
        cot_ref,
        gate_ref,
        up_ref,
        down_ref,
        part_ref,
        part_in,
        relay_in,
        part_sum,
        sum_ref,
        gate_out,
        up_out,
        down_out,
        *scratch,
    )


def ffn_body(
    subs,
    quad,
    slots,
    loads,
    scale_ref,
    x_ref,
    cot_ref,
    gate_ref,
    up_ref,
    down_ref,
    part_ref,
    part_in,
    relay_in,
    part_sum,
    sum_ref,
    gate_out,
    up_out,
    down_out,
    x_all,
    hid,
    dgate,
    dup,
    cot_buf,
    part_own,
    twin_buf,
    twin_in,
    send_buf,
    sums_in,
    cot_cols,
    wide_buf,
    tall_buf,
    x_send,
    x_recv,
    twin_x_send,
    twin_x_recv,
    twin_send,
    twin_recv,
    sum_send,
    sum_recv,
    p_send,
    p_recv,
    relay_recv,
    relay_sem,
    cot_sem,
    part_sem,
    cols_sem,
    out_sem,
    *row_scratch,
):
    chips = lax.axis_size("mp") // 2
    me = lax.axis_index("mp")
    row = lax.axis_index("rows")
    chip = me // 2
    core = me % 2
    rows = x_ref.shape[0] // subs
    units = chips * subs
    twin = (row, me + 1 - 2 * core)

    def on_chip(other):
        return (row, 2 * other + core)

    barrier = pltpu.get_barrier_semaphore()
    pl.semaphore_signal(barrier, inc=1, device_id=twin, device_id_type=MESH)
    for step in range(1, chips):
        pl.semaphore_signal(
            barrier, inc=1, device_id=on_chip((chip + step) % chips), device_id_type=MESH
        )
    down, across = row // 2, row % 2
    beside_row = row + 1 - 2 * across
    above_row = (1 - down) * 2 + across
    neighbours = ((beside_row, me), (above_row, me))
    if quad:
        for device in neighbours:
            pl.semaphore_signal(barrier, inc=1, device_id=device, device_id_type=MESH)
    pl.semaphore_wait(barrier, chips + 2 if quad else chips)

    def order(i):
        near = jnp.minimum(chip, chips - 1 - chip)
        long_side = jnp.where(chip < chips - 1 - chip, 1, -1)
        j = i - subs
        paired = j < 2 * subs * near
        rest = j - 2 * subs * near
        dist = jnp.where(paired, j // (2 * subs) + 1, near + 1 + rest // subs)
        sub = jnp.where(paired, (j % (2 * subs)) // 2, rest % subs)
        side = jnp.where(paired, 1 - 2 * (j % 2), long_side)
        own = i < subs
        return (jnp.where(own, chip, chip + side * dist), jnp.where(own, i, sub))

    def x_copy(other, sub, side, source=None):
        spot = half_of(x_all, other, core, sub, rows)
        return pltpu.make_async_remote_copy(
            src_ref=spot if source is None else source,
            dst_ref=spot,
            send_sem=x_send.at[(side + 1) // 2, other * subs + sub],
            recv_sem=x_recv.at[other * subs + sub],
            device_id=on_chip(chip + side),
            device_id_type=MESH,
        )

    def twin_x_copy(other, sub, source=None):
        spot = half_of(x_all, other, core, sub, rows)
        return pltpu.make_async_remote_copy(
            src_ref=spot if source is None else source,
            dst_ref=spot,
            send_sem=twin_x_send.at[other * subs + sub],
            recv_sem=twin_x_recv.at[other * subs + sub],
            device_id=twin,
            device_id_type=MESH,
        )

    def twin_sum_copy(slot):
        return pltpu.make_async_remote_copy(
            src_ref=twin_buf.at[slot],
            dst_ref=twin_in.at[slot],
            send_sem=twin_send.at[slot],
            recv_sem=twin_recv.at[slot],
            device_id=twin,
            device_id_type=MESH,
        )

    def sum_copy(other, sub):
        side = jnp.where(other > chip, 1, -1)
        slot = jnp.where((side == 1) & (other == chip + 1), chips, other)
        return pltpu.make_async_remote_copy(
            src_ref=send_buf.at[other * subs + sub],
            dst_ref=sums_in.at[slot, sub],
            send_sem=sum_send.at[other * subs + sub],
            recv_sem=sum_recv.at[slot, sub],
            device_id=on_chip(chip + side),
            device_id_type=MESH,
        )

    def sum_arrival(slot, sub):
        return pltpu.make_async_remote_copy(
            src_ref=send_buf.at[0],
            dst_ref=sums_in.at[slot, sub],
            send_sem=sum_send.at[0],
            recv_sem=sum_recv.at[slot, sub],
            device_id=twin,
            device_id_type=MESH,
        )

    def cot_copies(other, sub, slot):
        return [
            pltpu.make_async_copy(
                half_of(cot_ref, other, c, sub, rows),
                cot_buf.at[slot, pl.ds(c * rows, rows)],
                cot_sem.at[slot, c],
            )
            for c in range(2)
        ]

    def part_copy(i):
        other, sub = order(i)
        return pltpu.make_async_copy(
            part_own.at[i % 2], part_ref.at[other * subs + sub], part_sem.at[i % 2]
        )

    for sub in range(subs):
        source = x_ref.at[pl.ds(sub * rows, rows)]

        @pl.when(chip < chips - 1)
        def _():
            x_copy(chip, sub, 1, source).start()

        @pl.when(chip > 0)
        def _():
            x_copy(chip, sub, -1, source).start()

        twin_x_copy(chip, sub, source).start()
    for copy in cot_copies(chip, 0, 0):
        copy.start()
    for sub in range(subs):
        half_of(x_all, chip, core, sub, rows)[...] = x_ref[sub * rows : (sub + 1) * rows, :]

    def reduce_unit(i):
        other, sub = order(i)
        unit = other * subs + sub
        slot = i % 2
        twin_sum_copy(slot).wait_recv()
        part_own[slot] = (
            part_own[slot].astype(F32) + twin_in[slot, 1].astype(F32)
        ).astype(BF16)
        part_copy(i).start()
        arrived = twin_in[slot, 0].astype(F32)
        lines = pl.ds(pl.multiple_of(sub * rows, rows), rows)

        @pl.when(other == chip)
        def _():
            sum_ref[lines, :] = sum_ref[lines, :] + arrived

        @pl.when(other != chip)
        def _():
            send_buf[unit] = (send_buf[unit].astype(F32) + arrived).astype(BF16)

        @pl.when(((other > chip) & (chip == 0)) | ((other < chip) & (chip == chips - 1)))
        def _():
            sum_copy(other, sub).start()

    def pass_on(e):
        right, left = chips - 1 - chip, chip
        right_first = chip < chips // 2
        ahead = jnp.where(right_first, right, left)
        step = jnp.where(e < ahead, e + 1, e - ahead + 1)
        toward = jnp.where((e < ahead) == right_first, 1, -1)
        other = chip + toward * step

        @pl.when((chip > 0) & (chip < chips - 1))
        def _():
            for sub in range(subs):
                unit = other * subs + sub
                sum_arrival(other, sub).wait_recv()
                send_buf[unit] = (
                    send_buf[unit].astype(F32) + sums_in[other, sub].astype(F32)
                ).astype(BF16)
                sum_copy(other, sub).start()

    def unit_step(i, _):
        other, sub = order(i)
        slot = i % 2

        @pl.when(i + 1 < units)
        def _():
            for copy in cot_copies(*order(i + 1), 1 - slot):
                copy.start()

        @pl.when(other != chip)
        def _():
            x_copy(other, sub, 1).wait_recv()
            twin_x_copy(other, sub).start()

            @pl.when((other > chip) & (chip > 0))
            def _():
                x_copy(other, sub, -1).start()

            @pl.when((other < chip) & (chip < chips - 1))
            def _():
                x_copy(other, sub, 1).start()

        twin_x_copy(other, sub).wait_recv()
        for copy in cot_copies(other, sub, slot):
            copy.wait()
        halves = [half_of(x_all, other, c, sub, rows)[...] for c in range(2)]
        x = jnp.concatenate(halves, axis=0)
        gate = dot(x, gate_ref[...])
        up = dot(x, up_ref[...])
        grad = dot_nt(cot_buf[slot], down_ref[...]) * scale_ref[0]
        sig = 1.0 / (1.0 + jnp.exp(-gate))
        act = gate * sig
        h = (act * up).astype(BF16)
        dg = (grad * up * (sig * (1.0 + gate * (1.0 - sig)))).astype(BF16)
        du = (grad * act).astype(BF16)
        for c in range(2):
            piece = slice(c * rows, (c + 1) * rows)
            half_of(hid, other, c, sub, rows)[...] = h[piece]
            half_of(dgate, other, c, sub, rows)[...] = dg[piece]
            half_of(dup, other, c, sub, rows)[...] = du[piece]

        @pl.when(i >= 2)
        def _():
            part_copy(i - 2).wait()
            twin_sum_copy(slot).wait_send()

        part = dot(h, down_ref[...])

        def keep_part(own, away):
            part_own[slot] = own.astype(BF16)
            twin_buf[slot, 1] = away.astype(BF16)

        @pl.when(core == 0)
        def _():
            keep_part(part[:rows], part[rows:])

        @pl.when(core == 1)
        def _():
            keep_part(part[rows:], part[:rows])

        dx = dot_nt(dg, gate_ref[...]) + dot_nt(du, up_ref[...])

        def keep(own, away):
            twin_buf[slot, 0] = away.astype(BF16)

            @pl.when(other == chip)
            def _():
                sum_ref[pl.ds(pl.multiple_of(sub * rows, rows), rows), :] = own

            @pl.when(other != chip)
            def _():
                send_buf[other * subs + sub] = own.astype(BF16)

        @pl.when(core == 0)
        def _():
            keep(dx[:rows], dx[rows:])

        @pl.when(core == 1)
        def _():
            keep(dx[rows:], dx[:rows])

        twin_sum_copy(slot).start()

        @pl.when(i >= 1)
        def _():
            reduce_unit(i - 1)

        return 0

    for copy in loads:
        copy.wait()
    lax.fori_loop(0, units, unit_step, 0)
    reduce_unit(units - 1)
    for i in (units - 2, units - 1):
        part_copy(i).wait()
        twin_sum_copy(i % 2).wait_send()

    width = x_ref.shape[1]
    ff = gate_ref.shape[1]
    tall = tall_buf.shape[1]
    narrow = tall_buf.shape[2]
    down_cols = cot_cols.shape[2]
    col_steps = width // down_cols
    pieces = width // tall
    steps = pieces * (ff // narrow)
    wholes = (gate_out, up_out, down_out)

    if quad:
        firsts, seconds, finals = slots[0:3], slots[3:6], slots[6:9]
        tall_in, wide_in, moved, one_send, one_recv, two_send, two_recv, load_sem, fin_sem = (
            row_scratch[:2] + (row_scratch[2:5],) + row_scratch[5:]
        )

    def remote(source, dest, send, recv, device):
        return pltpu.make_async_remote_copy(
            src_ref=source,
            dst_ref=dest,
            send_sem=send,
            recv_sem=recv,
            device_id=device,
            device_id_type=MESH,
        )

    def block_at(a, block, d):
        high, wide = firsts[a].shape[2:]
        lines = pl.ds(pl.multiple_of(block * high, high), high)
        return wholes[a].at[lines, pl.ds(d * wide, wide)]

    def one_copy(a, d, k):
        block = k * 2 + 1 - across if d == 0 else (1 - down) * 2 + k
        return remote(
            block_at(a, block, d),
            firsts[a].at[d, k],
            one_send.at[a, d, k],
            one_recv.at[a, d, k],
            neighbours[d],
        )

    def two_copy(a, d):
        return remote(
            moved[a].at[d],
            seconds[a].at[d],
            two_send.at[a, d],
            two_recv.at[a, d],
            neighbours[1 - d],
        )

    def fin_copy(a, d):
        wide = firsts[a].shape[3]
        return pltpu.make_async_copy(
            (wide_in if a == 2 else tall_in).at[0],
            finals[a].at[:, pl.ds(d * wide, wide)],
            fin_sem.at[d],
        )

    def load(sources, buf):
        copies = [
            pltpu.make_async_copy(source, buf.at[i], load_sem.at[i])
            for i, source in enumerate(sources)
        ]
        for copy in copies:
            copy.start()
        for copy in copies:
            copy.wait()

    def stage_two(a):
        if quad:
            buf = wide_in if a == 2 else tall_in
            for d in range(2):
                for k in range(2):
                    one_copy(a, d, k).wait_recv()
                block = above_row if d == 0 else beside_row
                other = 1 - down if d == 0 else 1 - across
                load([block_at(a, block, d), firsts[a].at[d, other]], buf)
                moved[a][d] = (buf[0].astype(F32) + buf[1].astype(F32)).astype(BF16)
                two_copy(a, d).start()

    def stage_three(a):
        if quad:
            buf = wide_in if a == 2 else tall_in
            for d in range(2):
                two_copy(a, d).wait_recv()
                other = down if d == 0 else across
                load([block_at(a, row, d), firsts[a].at[d, other], seconds[a].at[d]], buf)
                buf[0] = (
                    buf[0].astype(F32) + buf[1].astype(F32) + buf[2].astype(F32)
                ).astype(BF16)
                fin_copy(a, d).start()
                fin_copy(a, d).wait()

    def end_far(source, other):
        return ((source == 0) & (other >= 2)) | ((source == chips - 1) & (other <= chips - 3))

    def relayed(source, other):
        return ((source == 1) & (other >= 2)) | ((source == chips - 2) & (other <= chips - 3))

    def p_copy(other, sub, source=None):
        return remote(
            part_ref.at[other * subs + sub] if source is None else source,
            part_in.at[chip, sub],
            p_send.at[other * subs + sub],
            p_recv.at[chip, sub],
            on_chip(other),
        )

    def relay_copy(other, sub):
        return remote(
            part_ref.at[other * subs + sub],
            relay_in.at[other, sub],
            p_send.at[other * subs + sub],
            relay_recv.at[other, sub],
            on_chip(jnp.where(chip == 0, 1, chips - 2)),
        )

    def send_parts(far):
        if True:
            for step in range(1, chips):
                other = (chip + step) % chips
                beyond = end_far(chip, other)
                for sub in range(subs):
                    if far:

                        @pl.when(beyond)
                        def _():
                            relay_copy(other, sub).start()

                    else:

                        @pl.when(jnp.logical_not(beyond | relayed(chip, other)))
                        def _():
                            p_copy(other, sub).start()

    def piece(index):
        return cot_buf.at[index // 2, pl.ds(index % 2 * rows, rows)]

    def fetch(source, index):
        copy = pltpu.make_async_copy(source, piece(index), relay_sem.at[index])
        copy.start()
        return copy

    def relay_parts():
        for step in range(1, chips):
            other = (chip + step) % chips

            @pl.when(relayed(chip, other))
            def _():
                for sub in range(subs):
                    mine = fetch(part_ref.at[other * subs + sub], 2 * sub)
                    remote(
                        part_ref.at[0],
                        relay_in.at[other, sub],
                        p_send.at[0],
                        relay_recv.at[other, sub],
                        twin,
                    ).wait_recv()
                    theirs = fetch(relay_in.at[other, sub], 2 * sub + 1)
                    mine.wait()
                    theirs.wait()
                    part_ref_sum = piece(2 * sub)[...].astype(F32) + piece(2 * sub + 1)[
                        ...
                    ].astype(F32)
                    piece(2 * sub)[...] = part_ref_sum.astype(BF16)
                    back = pltpu.make_async_copy(
                        piece(2 * sub), part_ref.at[other * subs + sub], relay_sem.at[2 * sub]
                    )
                    back.start()
                    back.wait()
                    p_copy(other, sub).start()

    def total_parts():
        for sub in range(subs):
            lines = slice(sub * rows, (sub + 1) * rows)
            for base in range(1, chips, 3):
                group = range(base, min(base + 3, chips))
                if base == 1:
                    mine = fetch(part_ref.at[chip * subs + sub], 0)
                for step in group:
                    other = (chip + step) % chips

                    @pl.when(jnp.logical_not(end_far(other, chip)))
                    def _():
                        remote(
                            part_ref.at[0],
                            part_in.at[other, sub],
                            p_send.at[0],
                            p_recv.at[other, sub],
                            twin,
                        ).wait_recv()
                        fetch(part_in.at[other, sub], step - base + 1)

                if base == 1:
                    mine.wait()
                    part_sum[lines, :] = piece(0)[...].astype(F32)
                for step in group:
                    other = (chip + step) % chips
                    index = step - base + 1

                    @pl.when(jnp.logical_not(end_far(other, chip)))
                    def _():
                        pltpu.make_async_copy(
                            part_in.at[other, sub], piece(index), relay_sem.at[index]
                        ).wait()
                        part_sum[lines, :] = part_sum[lines, :] + piece(index)[...].astype(F32)

    def spread_blocks(a, source):
        def where(j):
            d, k = j % 2, (j // 2) % 2
            first = jnp.where(d == 0, k * 2 + 1 - across, (1 - down) * 2 + k)
            late = jnp.where(j < 6, jnp.where(d == 0, above_row, beside_row), row)
            return jnp.where(j < 4, first, late), d, k

        def place(ref, block, d):
            lines = pl.ds(pl.multiple_of(block * tall, tall), tall)
            return ref.at[lines, pl.ds(pl.multiple_of(d * narrow, narrow), narrow)]

        def block_out(j):
            block, d, _ = where(j)
            return pltpu.make_async_copy(
                tall_buf.at[j % 2], place(wholes[a], block, d), out_sem.at[j % 2]
            )

        def block_send(j):
            block, d, k = where(j)
            target = jnp.where(d == 0, beside_row, above_row)
            return remote(
                place(wholes[a], block, d),
                firsts[a].at[d, k],
                one_send.at[a, d, k],
                one_recv.at[a, d, k],
                (target, me),
            )

        def block_step(j, _):
            block, d, _ = where(j)
            lines = pl.ds(pl.multiple_of(block * tall, tall), tall)
            cols = pl.ds(pl.multiple_of(d * narrow, narrow), narrow)
            tall_buf[j % 2] = dot_tn(x_all[:, lines], source[:, cols]).astype(BF16)

            @pl.when(j >= 1)
            def _():
                block_out(j - 1).wait()

            @pl.when((j >= 1) & (j <= 4))
            def _():
                block_send(j - 1).start()

            block_out(j).start()
            return 0

        lax.fori_loop(0, 8, block_step, 0)
        block_out(7).wait()

    send_parts(True)
    for a, source in enumerate((dgate, dup)):

        def tall_out(j):
            first = pl.multiple_of(j % pieces * tall, tall)
            col = pl.multiple_of(j // pieces * narrow, narrow)
            return pltpu.make_async_copy(
                tall_buf.at[j % 2],
                wholes[a].at[pl.ds(first, tall), pl.ds(col, narrow)],
                out_sem.at[j % 2],
            )

        def tall_step(j, _):
            @pl.when(j >= 2)
            def _():
                tall_out(j - 2).wait()

            first = pl.multiple_of(j % pieces * tall, tall)
            col = pl.multiple_of(j // pieces * narrow, narrow)
            tall_buf[j % 2] = dot_tn(
                x_all[:, pl.ds(first, tall)], source[:, pl.ds(col, narrow)]
            ).astype(BF16)
            tall_out(j).start()
            return 0

        if quad:
            spread_blocks(a, source)
        else:
            lax.fori_loop(0, steps, tall_step, 0)
            for j in range(steps - 2, steps):
                tall_out(j).wait()
        for e in range(a * (chips - 1) // 3, (a + 1) * (chips - 1) // 3):
            pass_on(e)
    send_parts(False)

    def cols_copy(j):
        return pltpu.make_async_copy(
            cot_ref.at[:, pl.ds(pl.multiple_of(j * down_cols, down_cols), down_cols)],
            cot_cols.at[j % 2],
            cols_sem.at[j % 2],
        )

    def wide_out(j):
        return pltpu.make_async_copy(
            wide_buf.at[j % 2],
            down_out.at[:, pl.ds(pl.multiple_of(j * down_cols, down_cols), down_cols)],
            out_sem.at[j % 2],
        )

    cols_copy(0).start()

    def down_step(j, _):
        @pl.when(j + 1 < col_steps)
        def _():
            cols_copy(j + 1).start()

        cols_copy(j).wait()

        @pl.when(j >= 2)
        def _():
            wide_out(j - 2).wait()

        if quad:

            @pl.when(j == col_steps // 2 + 1)
            def _():
                for k in range(2):
                    one_copy(2, 0, k).start()

        wide_buf[j % 2] = (dot_tn(hid[...], cot_cols[j % 2]) * scale_ref[0]).astype(BF16)
        wide_out(j).start()
        return 0

    lax.fori_loop(0, col_steps, down_step, 0)
    for j in range(max(0, col_steps - 2), col_steps):
        wide_out(j).wait()
    if quad:
        for k in range(2):
            one_copy(2, 1, k).start()
    for e in range(2 * (chips - 1) // 3, chips - 1):
        pass_on(e)
    stage_two(0)
    relay_parts()
    stage_two(1)
    stage_three(0)
    stage_two(2)
    stage_three(1)
    stage_three(2)
    total_parts()
    if quad:
        for a in range(3):
            for d in range(2):
                two_copy(a, d).wait_send()
                for k in range(2):
                    one_copy(a, d, k).wait_send()

    for sub in range(subs):
        lines = slice(sub * rows, (sub + 1) * rows)

        @pl.when(chip < chips - 1)
        def _():
            sum_arrival(chip, sub).wait_recv()
            sum_ref[lines, :] = sum_ref[lines, :] + sums_in[chip, sub].astype(F32)

        @pl.when(chip > 0)
        def _():
            sum_arrival(chips, sub).wait_recv()
            sum_ref[lines, :] = sum_ref[lines, :] + sums_in[chips, sub].astype(F32)

    def finish(i, _):
        other, sub = order(i)
        twin_x_copy(other, sub).wait_send()

        @pl.when(((other >= chip) & (chip > 0)))
        def _():
            x_copy(other, sub, -1).wait_send()

        @pl.when(((other <= chip) & (chip < chips - 1)))
        def _():
            x_copy(other, sub, 1).wait_send()

        @pl.when(other != chip)
        def _():
            sum_copy(other, sub).wait_send()
            p_copy(other, sub).wait_send()

        return 0

    lax.fori_loop(0, units, finish, 0)


def ffn(scale, x, cot_all, gate_weight, up_weight, down_weight):
    tokens, width = cot_all.shape
    rows_dev = x.shape[0]
    chips = lax.axis_size("mp") // 2
    ff = gate_weight.shape[1]
    subs = max(1, rows_dev // BLOCK)
    rows = rows_dev // subs
    units = chips * subs
    quad = lax.axis_size("rows") == 4
    narrow = ff // 2 if quad else ff // 3
    tall = width // 4
    down_cols = 256
    extra_out, row_scratch = (), []
    vmem = pl.BlockSpec(memory_space=pltpu.VMEM)
    hbm = pl.BlockSpec(memory_space=pl.ANY)
    dma = pltpu.SemaphoreType.DMA
    if quad:
        sizes = ((width // 4, ff // 2), (width // 4, ff // 2), (ff // 4, width // 2))
        extra_out = (
            tuple(jax.ShapeDtypeStruct((2, 2, *size), BF16) for size in sizes)
            + tuple(jax.ShapeDtypeStruct((2, *size), BF16) for size in sizes)
            + tuple(jax.ShapeDtypeStruct((size[0], 2 * size[1]), BF16) for size in sizes)
        )
        row_scratch = (
            [pltpu.VMEM((3, *sizes[0]), BF16), pltpu.VMEM((3, *sizes[2]), BF16)]
            + [pltpu.VMEM((2, *size), BF16) for size in sizes]
            + [dma((3, 2, 2)), dma((3, 2, 2)), dma((3, 2)), dma((3, 2)), dma((3,)), dma((2,))]
        )
    out = pl.pallas_call(
        functools.partial(ffn_kernel, subs, quad),
        out_shape=(
            jax.ShapeDtypeStruct((units, rows, width), BF16),
            jax.ShapeDtypeStruct((chips, subs, rows, width), BF16),
            jax.ShapeDtypeStruct((chips, subs, rows, width), BF16),
            jax.ShapeDtypeStruct((rows_dev, width), F32),
            jax.ShapeDtypeStruct((rows_dev, width), F32),
            jax.ShapeDtypeStruct((width, ff), BF16),
            jax.ShapeDtypeStruct((width, ff), BF16),
            jax.ShapeDtypeStruct((ff, width), BF16),
        )
        + extra_out,
        in_specs=[pl.BlockSpec(memory_space=pltpu.SMEM), vmem, hbm, hbm, hbm, hbm],
        out_specs=(hbm, hbm, hbm, vmem, vmem, hbm, hbm, hbm) + (hbm,) * len(extra_out),
        scratch_shapes=[
            pltpu.VMEM((tokens, width), BF16),
            pltpu.VMEM((tokens, ff), BF16),
            pltpu.VMEM((tokens, ff), BF16),
            pltpu.VMEM((tokens, ff), BF16),
            pltpu.VMEM((2, 2 * rows, width), BF16),
            pltpu.VMEM((2, rows, width), BF16),
            pltpu.VMEM((2, 2, rows, width), BF16),
            pltpu.VMEM((2, 2, rows, width), BF16),
            pltpu.VMEM((units, rows, width), BF16),
            pltpu.VMEM((chips + 1, subs, rows, width), BF16),
            pltpu.VMEM((2, tokens, down_cols), BF16),
            pltpu.VMEM((2, ff, down_cols), BF16),
            pltpu.VMEM((2, tall, narrow), BF16),
            dma((2, units)),
            dma((units,)),
            dma((units,)),
            dma((units,)),
            dma((2,)),
            dma((2,)),
            dma((units,)),
            dma((chips + 1, subs)),
            dma((units,)),
            dma((chips, subs)),
            dma((chips, subs)),
            dma((4,)),
            dma((2, 2)),
            dma((2,)),
            dma((2,)),
            dma((2,)),
        ]
        + row_scratch
        + [
            pltpu.VMEM((width, ff), BF16),
            pltpu.VMEM((width, ff), BF16),
            pltpu.VMEM((ff, width), BF16),
            dma((3,)),
        ],
        compiler_params=pltpu.CompilerParams(
            collective_id=1, has_side_effects=True, vmem_limit_bytes=VMEM_LIMIT
        ),
        cost_estimate=pl.CostEstimate(
            flops=60_000_000_000, bytes_accessed=60_000_000, transcendentals=2_000_000
        ),
        name="ffn",
    )(scale.reshape(1), x, cot_all, gate_weight, up_weight, down_weight)
    if quad:
        shards = out[14:17]
    else:
        shards = [lax.psum(part, "rows") for part in out[5:8]]
    return (*out[3:5], *shards)


class Reducer:
    def __init__(self, height, left, right, gains, out, bufs):
        self.height, self.right, self.gains, self.out = height, right, gains, out
        (self.turned, self.own, self.twin_out, self.twin_in, self.out1, self.in1) = bufs[:6]
        (self.out2, self.in2, self.out3, self.in3) = bufs[6:10]
        (self.s0, self.r0, self.s1, self.r1, self.s2, self.r2, self.s3) = bufs[10:]
        self.cols = self.own.shape[-1]
        self.chips = lax.axis_size("mp") // 2
        me = lax.axis_index("mp")
        self.row = lax.axis_index("rows")
        self.chip, self.core = me // 2, me % 2
        self.down, self.across = self.row // 2, self.row % 2
        self.twin = (self.row, me + 1 - 2 * self.core)
        self.beside = (self.row + 1 - 2 * self.across, me)
        self.above = ((1 - self.down) * 2 + self.across, me)
        self.turned[...] = left[...].T

    def remote(self, source, dest, send, recv, device):
        return pltpu.make_async_remote_copy(
            src_ref=source,
            dst_ref=dest,
            send_sem=send,
            recv_sem=recv,
            device_id=device,
            device_id_type=MESH,
        )

    def goal(self, i):
        return (self.chip + 1 + i) % self.chips

    def twin_copy(self, i):
        return self.remote(
            self.twin_out.at[i], self.twin_in.at[i], self.s0.at[i], self.r0.at[i], self.twin
        )

    def first_copy(self, i, d):
        return self.remote(
            self.out1.at[i, d],
            self.in1.at[i, d],
            self.s1.at[i, d],
            self.r1.at[i, d],
            (self.beside, self.above)[d],
        )

    def second_copy(self, i, d):
        return self.remote(
            self.out2.at[i, d],
            self.in2.at[i, d],
            self.s2.at[i, d],
            self.r2.at[i, d],
            (self.above, self.beside)[d],
        )

    def last_copy(self, i):
        return self.remote(
            self.out3.at[i],
            self.in3.at[i],
            self.s3.at[0, i],
            self.s3.at[1, i],
            (self.row, 2 * self.goal(i) + self.core),
        )

    def make(self, i):
        height = self.height
        for r in range(4):
            first = (r * self.chips + self.goal(i)) * 2 * height
            lines = pl.ds(pl.multiple_of(first, 16), 2 * height)
            block = dot(self.turned[lines, :], self.right[...])
            spare = self.cols - block.shape[1]
            if spare:
                piece = self.gains[:, pl.ds(pl.multiple_of(first, 128), 2 * height)]
                piece = jnp.concatenate(
                    [piece, jnp.zeros((spare - piece.shape[0], 2 * height), F32)], axis=0
                ).T
                block = jnp.concatenate([block, piece], axis=1)

            @pl.when(self.core == 0)
            def _():
                self.own[i, r] = block[:height]
                self.twin_out[i, r] = block[height:].astype(BF16)

            @pl.when(self.core == 1)
            def _():
                self.own[i, r] = block[height:]
                self.twin_out[i, r] = block[:height].astype(BF16)

        self.twin_copy(i).start()

    def first_stage(self, i):
        half = self.cols // 2
        own = self.own
        self.twin_copy(i).wait_recv()
        for r in range(4):
            own[i, r] = own[i, r] + self.twin_in[i, r].astype(F32)
        for k in range(2):
            self.out1[i, 0, k] = own[i, k * 2 + 1 - self.across, :, :half].astype(BF16)
            self.out1[i, 1, k] = own[i, (1 - self.down) * 2 + k, :, half:].astype(BF16)
        for d in range(2):
            self.first_copy(i, d).start()

    def second_stage(self, i):
        half = self.cols // 2
        for d in range(2):
            self.first_copy(i, d).wait_recv()
        above = (1 - self.down) * 2 + self.across
        beside = self.down * 2 + 1 - self.across
        self.out2[i, 0] = (
            self.own[i, above, :, :half] + self.in1[i, 0, 1 - self.down].astype(F32)
        ).astype(BF16)
        self.out2[i, 1] = (
            self.own[i, beside, :, half:] + self.in1[i, 1, 1 - self.across].astype(F32)
        ).astype(BF16)
        for d in range(2):
            self.second_copy(i, d).start()

    def third_stage(self, i):
        half = self.cols // 2
        for d in range(2):
            self.second_copy(i, d).wait_recv()
        left = (
            self.own[i, self.row, :, :half]
            + self.in1[i, 0, self.down].astype(F32)
            + self.in2[i, 0].astype(F32)
        )
        right = (
            self.own[i, self.row, :, half:]
            + self.in1[i, 1, self.across].astype(F32)
            + self.in2[i, 1].astype(F32)
        )

        @pl.when(i < self.chips - 1)
        def _():
            self.out3[i, :, :half] = left.astype(BF16)
            self.out3[i, :, half:] = right.astype(BF16)
            self.last_copy(i).start()

        @pl.when(i == self.chips - 1)
        def _():
            self.out[:, :half] = left
            self.out[:, half:] = right

    def round(self, n, _=None):
        stages = (self.make, self.first_stage, self.second_stage, self.third_stage)
        for stage, work in enumerate(stages):

            @pl.when((n >= stage) & (n < self.chips + stage))
            def _():
                work(n - stage)

        return 0

    def close(self):
        for i in range(self.chips - 1):
            self.last_copy(i).wait_recv()
            self.out[...] = self.out[...] + self.in3[i].astype(F32)

        def finish(i, _):
            self.twin_copy(i).wait_send()
            for d in range(2):
                self.first_copy(i, d).wait_send()
                self.second_copy(i, d).wait_send()

            @pl.when(i < self.chips - 1)
            def _():
                self.last_copy(i).wait_send()

            return 0

        lax.fori_loop(0, self.chips, finish, 0)


def reducer_buffers(left, right):
    chips = lax.axis_size("mp") // 2
    shards = lax.axis_size("rows") * lax.axis_size("mp")
    height = left.shape[1] // shards
    cols = -(-right.shape[1] // 256) * 256
    half = cols // 2
    dma = pltpu.SemaphoreType.DMA
    return (
        height,
        jax.ShapeDtypeStruct((height, cols), F32),
        [
            pltpu.VMEM((left.shape[1], left.shape[0]), BF16),
            pltpu.VMEM((chips, 4, height, cols), F32),
            pltpu.VMEM((chips, 4, height, cols), BF16),
            pltpu.VMEM((chips, 4, height, cols), BF16),
            pltpu.VMEM((chips, 2, 2, height, half), BF16),
            pltpu.VMEM((chips, 2, 2, height, half), BF16),
            pltpu.VMEM((chips, 2, height, half), BF16),
            pltpu.VMEM((chips, 2, height, half), BF16),
            pltpu.VMEM((chips - 1, height, cols), BF16),
            pltpu.VMEM((chips - 1, height, cols), BF16),
            dma((chips,)),
            dma((chips,)),
            dma((chips, 2)),
            dma((chips, 2)),
            dma((chips, 2)),
            dma((chips, 2)),
            dma((2, chips)),
        ],
    )


def reduce_kernel(height, left, right, gains, half_ref, low_ref, out, swapped, wide_ref, *bufs):
    bufs, (land, low_buf, wide_buf, swap_sems, low_sems, wide_sems) = bufs[:-6], bufs[-6:]
    mp = lax.axis_size("mp")
    chips = mp // 2
    me = lax.axis_index("mp")
    row = lax.axis_index("rows")
    chip, core = me // 2, me % 2
    down, across = row // 2, row % 2
    mirror = (row, mp - 1 - me)
    barrier = pltpu.get_barrier_semaphore()
    devices = [
        mirror,
        (row, me + 1 - 2 * core),
        (row + 1 - 2 * across, me),
        ((1 - down) * 2 + across, me),
    ] + [(row, 2 * ((chip + step) % chips) + core) for step in range(1, chips)]
    for device in devices:
        pl.semaphore_signal(barrier, inc=1, device_id=device, device_id_type=MESH)
    pl.semaphore_wait(barrier, chips + 3)
    swap = pltpu.make_async_remote_copy(
        src_ref=half_ref,
        dst_ref=land,
        send_sem=swap_sems.at[0],
        recv_sem=swap_sems.at[1],
        device_id=mirror,
        device_id_type=MESH,
    )
    swap.start()
    reducer = Reducer(height, left, right, gains, out, bufs)
    tall = low_buf.shape[1]
    pieces = low_ref.shape[0] // tall

    def low_copy(j):
        lines = pl.ds(pl.multiple_of(j * tall, tall), tall)
        return pltpu.make_async_copy(low_ref.at[lines], low_buf.at[j % 2], low_sems.at[j % 2])

    def wide_copy(j):
        lines = pl.ds(pl.multiple_of(j * tall, tall), tall)
        return pltpu.make_async_copy(wide_buf.at[j % 2], wide_ref.at[lines], wide_sems.at[j % 2])

    def widen(j, _=None):
        @pl.when(j + 1 < pieces)
        def _():
            low_copy(j + 1).start()

        low_copy(j).wait()

        @pl.when(j >= 2)
        def _():
            wide_copy(j - 2).wait()

        wide_buf[j % 2] = low_buf[j % 2].astype(F32)
        wide_copy(j).start()
        return 0

    low_copy(0).start()

    def both(n, _):
        reducer.round(n)
        widen(n)
        return 0

    rounds = chips + 3
    lax.fori_loop(0, min(rounds, pieces), both, 0)
    if pieces > rounds:
        lax.fori_loop(rounds, pieces, widen, 0)
    else:
        lax.fori_loop(pieces, rounds, reducer.round, 0)
    reducer.close()
    for j in (pieces - 2, pieces - 1):
        wide_copy(j).wait()
    swap.wait()
    swapped[...] = land[...].astype(F32)


def reduce_product(left, right, gains, half, low):
    height, out_shape, scratch = reducer_buffers(left, right)
    vmem = pl.BlockSpec(memory_space=pltpu.VMEM)
    hbm = pl.BlockSpec(memory_space=pl.ANY)
    dma = pltpu.SemaphoreType.DMA
    tall = low.shape[0] // 8
    return pl.pallas_call(
        functools.partial(reduce_kernel, height),
        out_shape=(
            out_shape,
            jax.ShapeDtypeStruct(half.shape, F32),
            jax.ShapeDtypeStruct(low.shape, F32),
        ),
        in_specs=[vmem] * 4 + [hbm],
        out_specs=(vmem, vmem, hbm),
        scratch_shapes=scratch
        + [
            pltpu.VMEM(half.shape, BF16),
            pltpu.VMEM((2, tall, low.shape[1]), BF16),
            pltpu.VMEM((2, tall, low.shape[1]), F32),
            dma((2,)),
            dma((2,)),
            dma((2,)),
        ],
        compiler_params=pltpu.CompilerParams(
            collective_id=2, has_side_effects=True, vmem_limit_bytes=VMEM_LIMIT
        ),
        cost_estimate=pl.CostEstimate(
            flops=50_000_000_000, bytes_accessed=10_000_000, transcendentals=0
        ),
        name="reduce_product",
    )(left, right, gains, half, low)


def natural(device, sub, subs):
    if subs == 2:
        return sub * (2 * lax.axis_size("mp") - 1 - 2 * device) + (1 - sub) * 2 * device
    return subs * device + sub


def front_kernel(
    shard_ref,
    x_ref,
    cos_q,
    sin_q,
    cos_kv,
    sin_kv,
    w_out,
    extra_ref,
    xf_ref,
    normed_ref,
    inv_ref,
    q_ref,
    kv_out,
    w_all,
    x_in,
    kv_all,
    swap_send,
    swap_recv,
    z_send,
    z_recv,
    xy_send,
    xy_recv,
    far_send,
    far_recv,
    twin_send,
    twin_recv,
    kz_send,
    kz_recv,
    kt_send,
    kt_recv,
    out_sem,
):
    mp = lax.axis_size("mp")
    chips = mp // 2
    me = lax.axis_index("mp")
    row = lax.axis_index("rows")
    chip = me // 2
    core = me % 2
    down, across = row // 2, row % 2
    subs = x_ref.shape[0] // BLOCK
    height = shard_ref.shape[0]
    half = w_all.shape[1] // 2
    beside_row = row + 1 - 2 * across
    above_row = (1 - down) * 2 + across
    far_row = (1 - down) * 2 + 1 - across
    twin = (row, me + 1 - 2 * core)
    beside = (beside_row, me)
    above = (above_row, me)
    mirror = (row, mp - 1 - me)

    barrier = pltpu.get_barrier_semaphore()
    for device in (twin, beside, above, mirror):
        pl.semaphore_signal(barrier, inc=1, device_id=device, device_id_type=MESH)

    @pl.when(chip < chips - 1)
    def _():
        pl.semaphore_signal(barrier, inc=1, device_id=(row, me + 2), device_id_type=MESH)

    @pl.when(chip > 0)
    def _():
        pl.semaphore_signal(barrier, inc=1, device_id=(row, me - 2), device_id_type=MESH)

    ends = jnp.where(chip < chips - 1, 1, 0) + jnp.where(chip > 0, 1, 0)
    pl.semaphore_wait(barrier, 4 + ends)

    def remote(source, dest, send, recv, device):
        return pltpu.make_async_remote_copy(
            src_ref=source,
            dst_ref=dest,
            send_sem=send,
            recv_sem=recv,
            device_id=device,
            device_id_type=MESH,
        )

    def spot(r, k, side=None):
        lines = pl.ds(pl.multiple_of((r * mp + 2 * k + core) * height, height), height)
        if side is None:
            return w_all.at[lines]
        return w_all.at[lines, pl.ds(side * half, half)]

    def z_copy(k, side):
        return remote(
            spot(row, k),
            spot(row, k),
            z_send.at[(side + 1) // 2, k],
            z_recv.at[k],
            (row, me + 2 * side),
        )

    def near_copy(k, d):
        return remote(
            spot(row, k), spot(row, k), xy_send.at[d, k], xy_recv.at[d, k], (beside, above)[d]
        )

    def near_row(d):
        return (beside_row, above_row)[d]

    def far_copy(k, d):
        place = spot(near_row(d), k, d)
        return remote(place, place, far_send.at[d, k], far_recv.at[d, k], (above, beside)[d])

    def twin_copy(k, kind):
        if kind < 3:
            place = spot((row, beside_row, above_row)[kind], k)
        else:
            place = spot(far_row, k, kind - 3)
        return remote(place, place, twin_send.at[kind, k], twin_recv.at[kind, k], twin)

    def order(i):
        near = jnp.minimum(chip, chips - 1 - chip)
        long_side = jnp.where(chip < chips - 1 - chip, 1, -1)
        paired = i <= 2 * near
        dist = jnp.where(paired, (i + 1) // 2, i - near)
        side = jnp.where(paired, 2 * (i % 2) - 1, long_side)
        return chip + side * dist

    if subs == 2:
        swap = remote(x_ref.at[pl.ds(BLOCK, BLOCK)], x_in, swap_send, swap_recv, mirror)
        swap.start()
    own_lines = pl.ds(pl.multiple_of((row * mp + me) * height, height), height)
    w_all[own_lines, :] = shard_ref[...]

    def gather_step(n, _):
        @pl.when(n < chips)
        def _():
            k = order(n)

            @pl.when(n > 0)
            def _():
                z_copy(k, 1).wait_recv()

            for d in range(2):
                near_copy(k, d).start()

            @pl.when((k >= chip) & (chip > 0))
            def _():
                z_copy(k, -1).start()

            @pl.when((k <= chip) & (chip < chips - 1))
            def _():
                z_copy(k, 1).start()

            twin_copy(k, 0).start()

        @pl.when((n >= 1) & (n < chips + 1))
        def _():
            k = order(n - 1)
            for d in range(2):
                near_copy(k, d).wait_recv()
                far_copy(k, d).start()
                twin_copy(k, 1 + d).start()

        @pl.when(n >= 2)
        def _():
            k = order(n - 2)
            for d in range(2):
                far_copy(k, d).wait_recv()
                twin_copy(k, 3 + d).start()

        return 0

    lax.fori_loop(0, chips + 2, gather_step, 0)

    xf_ref[:BLOCK, :] = x_ref[:BLOCK, :]
    if subs == 2:
        swap.wait_recv()
        xf_ref[BLOCK:, :] = x_in[...]

    def drain_step(k, _):
        for kind in range(5):
            twin_copy(k, kind).wait_recv()
        return 0

    lax.fori_loop(0, chips, drain_step, 0)
    save = pltpu.make_async_copy(w_all, w_out, out_sem)
    save.start()
    cols = Q_WIDTH + 2 * KV_WIDTH
    extra = w_all[:, cols:].astype(F32).T[:8, :]
    extra_ref[...] = extra
    x = xf_ref[...].astype(F32)
    inverse = lax.rsqrt(jnp.mean(x * x, axis=-1, keepdims=True) + EPS)
    inv_ref[...] = inverse
    normed_ref[...] = (x * inverse * extra[0:1, :]).astype(BF16)

    def place_of(device, sub):
        first = natural(device, sub, subs) * BLOCK
        return kv_all.at[pl.ds(pl.multiple_of(first, BLOCK), BLOCK)]

    part = dot(normed_ref[...], w_all[:, Q_WIDTH:cols])
    for g in range(KV_HEADS):
        slab = part[:, g * SLAB : (g + 1) * SLAB]
        turned = (slab * cos_kv[...] + swap_halves(slab) * sin_kv[...]).astype(BF16)
        for sub in range(subs):
            place_of(me, sub)[:, g * SLAB : (g + 1) * SLAB] = turned[
                sub * BLOCK : (sub + 1) * BLOCK, :
            ]

    def kz_copy(k, sub, side):
        place = place_of(2 * k + core, sub)
        return remote(
            place,
            place,
            kz_send.at[(side + 1) // 2, k * subs + sub],
            kz_recv.at[k * subs + sub],
            (row, me + 2 * side),
        )

    def kt_copy(k, sub):
        place = place_of(2 * k + core, sub)
        return remote(
            place, place, kt_send.at[k * subs + sub], kt_recv.at[k * subs + sub], twin
        )

    def spread(n, _):
        k = order(n)
        for sub in range(subs):

            @pl.when(n > 0)
            def _():
                kz_copy(k, sub, 1).wait_recv()

            @pl.when((k >= chip) & (chip > 0))
            def _():
                kz_copy(k, sub, -1).start()

            @pl.when((k <= chip) & (chip < chips - 1))
            def _():
                kz_copy(k, sub, 1).start()

            kt_copy(k, sub).start()

        return 0

    spread(0, 0)
    for s in range(Q_WIDTH // 256):
        part = dot(normed_ref[...], w_all[:, s * 256 : (s + 1) * 256])
        for t in range(2):
            slab = part[:, t * SLAB : (t + 1) * SLAB]
            col = s * 256 + t * SLAB
            turned = slab * cos_q[...] + swap_halves(slab) * sin_q[...]
            q_ref[:, col : col + SLAB] = (
                turned.astype(BF16).astype(F32) * HEAD_DIM ** (-0.5)
            ).astype(BF16)
    lax.fori_loop(1, chips, spread, 0)

    def finish(k, _):
        for sub in range(subs):
            kt_copy(k, sub).wait_recv()
            kt_copy(k, sub).wait_send()
        for kind in range(5):
            twin_copy(k, kind).wait_send()
        for d in range(2):
            near_copy(k, d).wait_send()
            far_copy(k, d).wait_send()

        @pl.when((k >= chip) & (chip > 0))
        def _():
            z_copy(k, -1).wait_send()
            for sub in range(subs):
                kz_copy(k, sub, -1).wait_send()

        @pl.when((k <= chip) & (chip < chips - 1))
        def _():
            z_copy(k, 1).wait_send()
            for sub in range(subs):
                kz_copy(k, sub, 1).wait_send()

        return 0

    lax.fori_loop(0, chips, finish, 0)
    if subs == 2:
        swap.wait_send()
    kv_out[...] = kv_all[...]
    save.wait()


def front(shard, x, tables):
    rows, width = x.shape
    subs = rows // BLOCK
    chips = lax.axis_size("mp") // 2
    cols = shard.shape[1]
    total = shard.shape[0] * lax.axis_size("rows") * lax.axis_size("mp")
    vmem = pl.BlockSpec(memory_space=pltpu.VMEM)
    hbm = pl.BlockSpec(memory_space=pl.ANY)
    dma = pltpu.SemaphoreType.DMA
    return pl.pallas_call(
        front_kernel,
        out_shape=(
            jax.ShapeDtypeStruct((total, cols), BF16),
            jax.ShapeDtypeStruct((8, total), F32),
            jax.ShapeDtypeStruct((rows, width), BF16),
            jax.ShapeDtypeStruct((rows, width), BF16),
            jax.ShapeDtypeStruct((rows, 1), F32),
            jax.ShapeDtypeStruct((rows, Q_WIDTH), BF16),
            jax.ShapeDtypeStruct((LEN, 2 * KV_WIDTH), BF16),
        ),
        in_specs=[vmem] * 6,
        out_specs=(hbm,) + (vmem,) * 6,
        scratch_shapes=[
            pltpu.VMEM((total, cols), BF16),
            pltpu.VMEM((BLOCK, width), BF16),
            pltpu.VMEM((LEN, 2 * KV_WIDTH), BF16),
            dma,
            dma,
            dma((2, chips)),
            dma((chips,)),
            dma((2, chips)),
            dma((2, chips)),
            dma((2, chips)),
            dma((2, chips)),
            dma((5, chips)),
            dma((5, chips)),
            dma((2, chips * subs)),
            dma((chips * subs,)),
            dma((chips * subs,)),
            dma((chips * subs,)),
            dma,
        ],
        compiler_params=pltpu.CompilerParams(
            collective_id=4, has_side_effects=True, vmem_limit_bytes=VMEM_LIMIT
        ),
        cost_estimate=pl.CostEstimate(
            flops=30_000_000_000, bytes_accessed=12_000_000, transcendentals=0
        ),
        name="front",
    )(shard, x, *tables)


def on_device(
    inputs,
    cotangent,
    corpus_ids,
    corpus_weight,
    attn_gain,
    qkv_weight,
    out_weight,
    ffn_gain,
    gate_weight,
    up_weight,
    down_weight,
):
    both = ("rows", "mp")
    rows_dev, width = inputs.shape
    mp = lax.axis_size("mp")
    me = lax.axis_index("mp")
    row_groups = lax.axis_size("rows")
    corpora = corpus_weight.shape[0]
    subs = rows_dev // BLOCK
    folded = subs == 2
    mirror = [(i, mp - 1 - i) for i in range(mp)]

    def fold(rows):
        if not folded:
            return rows
        return jnp.concatenate(
            [rows[:BLOCK], lax.ppermute(rows[BLOCK:], "mp", mirror)], axis=0
        )

    def to_order(gathered):
        if not folded:
            return gathered
        parts = gathered.reshape(mp, 2, BLOCK, gathered.shape[-1])
        return jnp.stack([parts[:, 0], parts[::-1, 1]], axis=1).reshape(gathered.shape)

    if folded:
        blocks = jnp.stack([2 * me, 2 * mp - 1 - 2 * me]).astype(jnp.int32)
    else:
        blocks = (subs * me + jnp.arange(subs)).astype(jnp.int32)
    positions = (blocks[:, None] * BLOCK + jnp.arange(BLOCK)[None, :]).reshape(-1)

    shard_rows = qkv_weight.shape[0]
    ident = jnp.broadcast_to(corpus_ids.astype(BF16)[:1, None], (shard_rows, 1))
    spare = (-(Q_WIDTH + 2 * KV_WIDTH + 3)) % 128
    shard = jnp.concatenate(
        [
            pack_kv(qkv_weight),
            attn_gain[:, None],
            ffn_gain[:, None],
            ident,
            jnp.zeros((shard_rows, spare), BF16),
        ],
        axis=1,
    )
    qkv_cols = Q_WIDTH + 2 * KV_WIDTH
    cot_all = lax.all_gather(cotangent, "mp", axis=0, tiled=True)
    out_full = lax.all_gather(out_weight, both, axis=0, tiled=True)
    tables = rope_tables(positions)
    if row_groups == 4:
        qkv_ext, extras, x, normed_one, inverse_one, q, kv_all = front(shard, inputs, tables)
        qkv_full = qkv_ext[:, :qkv_cols]
    else:
        qkv_ext = lax.all_gather(shard, both, axis=0, tiled=True)
        qkv_full = qkv_ext[:, :qkv_cols]
        extras = qkv_ext[:, qkv_cols:].astype(F32).T
        x = fold(inputs)
        normed_one, inverse_one, q, kv = qkv_project(x, extras[0:1], qkv_full, tables)
        kv_all = to_order(lax.all_gather(kv, "mp", axis=0, tiled=True))
    gain_one, gain_two = extras[0:1], extras[1:2]
    all_ids = extras[2].reshape(row_groups, -1)[:, 0]
    my_id = corpus_ids[0].astype(F32)
    count = jnp.sum((all_ids == my_id).astype(F32))
    weight_seq = jnp.sum(
        jnp.where(jnp.arange(corpora) == corpus_ids[0], corpus_weight, 0.0)
    )
    seq_scale = weight_seq * row_groups / (corpora * count)
    o, totals = attend(blocks, q, kv_all)

    residual = x.astype(F32)
    middle = residual + dot(o, out_full)
    inverse_two = lax.rsqrt(jnp.mean(middle * middle, axis=-1, keepdims=True) + EPS)
    normed_two = (middle * inverse_two * gain_two).astype(BF16)
    ffn_sum, grad_normed_two, gate_grad, up_grad, down_grad = ffn(
        seq_scale, normed_two, cot_all, gate_weight, up_weight, down_weight
    )
    outputs = fold((middle + ffn_sum).astype(BF16))

    cot = jnp.concatenate(
        [
            lax.dynamic_slice(cot_all, (blocks[sub] * BLOCK, 0), (BLOCK, width))
            for sub in range(subs)
        ],
        axis=0,
    )
    grad_out = cot.astype(F32) * seq_scale
    scaled_two = grad_normed_two * gain_two
    ffn_gain_part = jnp.sum(grad_normed_two * middle * inverse_two, axis=0)
    grad_middle = (
        grad_out
        + inverse_two * scaled_two
        - middle * inverse_two**3 * jnp.mean(scaled_two * middle, axis=-1, keepdims=True)
    )
    grad_middle_low = grad_middle.astype(BF16)
    if row_groups == 4:
        gate_grad, up_grad, down_grad = (
            lax.all_gather(g, "rows", axis=0, tiled=True)
            for g in (gate_grad, up_grad, down_grad)
        )
    grad_o = dot_nt(grad_middle_low, out_full).astype(BF16)
    grad_qkv, *proj = attend_back(q, kv_all, o, grad_o, totals, tables, grad_middle_low)
    grad_normed_one = dot_nt(grad_qkv, qkv_full)
    scaled_one = grad_normed_one * gain_one
    attn_gain_part = jnp.sum(grad_normed_one * residual * inverse_one, axis=0)
    input_grad = (
        grad_middle
        + inverse_one * scaled_one
        - residual * inverse_one**3 * jnp.mean(scaled_one * residual, axis=-1, keepdims=True)
    )
    if folded and row_groups != 4:
        input_grad = jnp.concatenate(
            [
                input_grad[:BLOCK],
                lax.ppermute(input_grad[BLOCK:].astype(BF16), "mp", mirror).astype(F32),
            ],
            axis=0,
        )
    gain_parts = jnp.concatenate(
        [attn_gain_part[None], ffn_gain_part[None], jnp.zeros((6, width), F32)], axis=0
    )
    if row_groups == 4:
        proj_grad = proj[0]
        part, swapped, gate_grad = reduce_product(
            normed_one, grad_qkv, gain_parts, input_grad[-BLOCK:].astype(BF16), gate_grad
        )
        if folded:
            input_grad = jnp.concatenate([input_grad[:BLOCK], swapped], axis=0)
    else:
        part = jnp.concatenate(
            [dot_tn(normed_one, grad_qkv), gain_parts.T, jnp.zeros((width, 120), F32)], axis=1
        )
        part, proj_grad = (
            lax.psum_scatter(p.astype(BF16), both, scatter_dimension=0, tiled=True).astype(F32)
            for p in (part, dot_tn(o, grad_middle_low))
        )
    qkv_grad = unpack_kv(part[:, :qkv_cols])
    attn_gain_grad = part[:, qkv_cols]
    ffn_gain_grad = part[:, qkv_cols + 1]
    if row_groups != 4:
        gate_grad = gate_grad.astype(F32)
    up_grad, part = lax.optimization_barrier((up_grad, part))
    up_grad = up_grad.astype(F32)
    down_grad, part = lax.optimization_barrier((down_grad, part))
    down_grad = down_grad.astype(F32)
    attn_gain_grad = part[:, qkv_cols]
    ffn_gain_grad = part[:, qkv_cols + 1]
    return (
        outputs,
        input_grad,
        qkv_grad,
        proj_grad,
        gate_grad,
        up_grad,
        down_grad,
        attn_gain_grad,
        ffn_gain_grad,
    )


def solution(mesh):
    split = P(("rows", "mp"), None)
    line = P(("rows", "mp"))
    in_specs = (
        split,
        split,
        P("rows"),
        P(),
        line,
        split,
        split,
        line,
        P(None, "mp"),
        P(None, "mp"),
        P("mp", None),
    )
    out_specs = (
        split,
        split,
        split,
        split,
        P(None, "mp"),
        P(None, "mp"),
        P("mp", None),
        line,
        line,
    )
    return jax.shard_map(
        on_device, mesh=mesh, in_specs=in_specs, out_specs=out_specs, check_vma=False
    )
```
